256 devices in a mesh: row: 16 (over z, core), col: 16 (over x, y).
Axes of the slice: x: 4, y: 4, z: 8, core: 2. Of those that a mesh axis runs over, the one named last changes fastest.
Arguments:
- panel: float32 [16384, 128], P(('row', 'col')), as said below
- mobility: float32 [16384, 16384], P('row', 'col'), as said below
Outputs:
- updated: float32 [16384, 16384], P('row', 'col')
- panel_factor: float32 [128, 128], replicated
Inputs may be any that keep to these rules, and one draw needn't show every extreme that they name: Each row and each column of the panel has its own scale. `mobility`: Symmetric.
All inputs are finite; a program needn't handle non-finite values.
Results may differ from the reference program's by a relative error of at most 0.000076.
Values sent between devices are 32-bit elements; how exact they have to be, the bound alone decides.
No kernel may reach another device: no remote copies, remote signals or barrier semaphores. Data moves between devices by JAX's collectives and lax.ppermute only.
A program may use at most 64 MiB of HBM per device.

```python
import math
import jax
import jax.numpy as jnp
from jax import lax

PANEL = 128
ORDER = 16384


def draw_panel(key, part):
    all_keys = jax.random.split(key, 3)
    values = jnp.clip(jax.random.normal(all_keys[0], (ORDER, PANEL), jnp.float32), -6.0, 6.0)
    row_scale = jnp.exp(jax.random.uniform(all_keys[1], (ORDER, 1), jnp.float32) * math.log(10.0))
    col_scale = jnp.exp(jax.random.uniform(all_keys[2], (1, PANEL), jnp.float32) * math.log(10.0))
    position = jnp.arange(ORDER, dtype=jnp.float32)[:, None] / float(max(ORDER - 1, 1))
    growth = jnp.sqrt(1.0 + 2.0 * position)
    return values * row_scale * col_scale * growth * (1.5 / math.sqrt(43.0 * ORDER))


def draw_mobility(key, part):
    all_keys = jax.random.split(key, 2)
    values = jnp.clip(jax.random.normal(all_keys[0], (ORDER, ORDER), jnp.float32), -5.0, 5.0)
    symmetric = (values + values.T) * math.sqrt(0.5)
    diagonal_values = jax.random.uniform(all_keys[1], (ORDER,), jnp.float32, 1.0, 3.0)
    on_diagonal = jnp.arange(ORDER, dtype=jnp.int32)[:, None] == jnp.arange(ORDER, dtype=jnp.int32)[None, :]
    return symmetric + jnp.where(on_diagonal, diagonal_values[None, :], 0.0)


def setup_inputs(seed: int = 0) -> dict:
    seeds = jax.random.split(jax.random.key(seed), 3)
    return {
        "panel": draw_panel(jax.random.fold_in(seeds[2], 71), 0),
        "mobility": draw_mobility(jax.random.fold_in(seeds[2], 71), 0),
    }


def product(first_op, second_op):
    return jnp.dot(first_op.astype(jnp.float32), second_op.astype(jnp.float32), precision=lax.Precision.HIGHEST, preferred_element_type=jnp.float32)

def reference(panel, mobility):
    gram = product(panel.T, panel)
    lower_factor = jnp.linalg.cholesky(gram)
    panel_factor = lower_factor.T
    ortho = jax.scipy.linalg.solve_triangular(lower_factor, panel.T, lower=True).T
    unit_rows = (jnp.arange(ORDER, dtype=jnp.int32)[:, None] == jnp.arange(PANEL, dtype=jnp.int32)[None, :]).astype(jnp.float32)
    basis = ortho + unit_rows
    core_matrix = basis[:PANEL].T
    kernel = jnp.linalg.inv(core_matrix)
    spread = product(product(mobility, basis), kernel)
    inner = product(kernel.T, product(basis.T, spread))
    correction = spread - 0.5 * product(basis, inner)
    left_side = jnp.concatenate([basis, correction], axis=1)
    right_side = jnp.concatenate([correction, basis], axis=1)
    updated = mobility - product(left_side, right_side.T)
    return (updated, panel_factor)
```

```python
import jax
import jax.numpy as jnp
from jax import lax
from jax.sharding import PartitionSpec as P

BOTH = ("row", "col")


def product(first_op, second_op):
    return jnp.dot(
        first_op, second_op, precision=lax.Precision.HIGHEST, preferred_element_type=jnp.float32
    )


def product_tn(first_op, second_op):
    return lax.dot_general(
        first_op,
        second_op,
        (((0,), (0,)), ((), ())),
        precision=lax.Precision.HIGHEST,
        preferred_element_type=jnp.float32,
    )


def product_nt(first_op, second_op):
    return lax.dot_general(
        first_op,
        second_op,
        (((1,), (1,)), ((), ())),
        precision=lax.Precision.HIGHEST,
        preferred_element_type=jnp.float32,
    )


def invert_core(core_matrix):
    identity = jnp.eye(core_matrix.shape[0], dtype=jnp.float32)

    def newton_step(index, approx):
        return product(approx, 2.0 * identity - product(core_matrix, approx))

    return lax.fori_loop(0, 12, newton_step, identity)


def on_device(panel, mobility):
    piece, width = panel.shape
    n_row, n_col = lax.axis_size("row"), lax.axis_size("col")
    block_rows, block_cols = mobility.shape
    row, col = lax.axis_index("row"), lax.axis_index("col")
    half = row % 2
    n_z = n_row // 2
    share = width // n_col
    z_groups = [[2 * z + h for z in range(n_z)] for h in range(2)]
    pairs = [[2 * z, 2 * z + 1] for z in range(n_z)]
    transposing = [(i * n_col + j, j * n_col + i) for i in range(n_row) for j in range(n_col)]
    swap = [(i, i ^ 1) for i in range(n_row)]

    def gather_col(rows):
        return lax.all_to_all(jnp.broadcast_to(rows[None], (n_col,) + rows.shape), "col", 0, 0)

    def gather_z(rows):
        copies = jnp.broadcast_to(rows[None], (n_z,) + rows.shape)
        return lax.all_to_all(copies, "row", 0, 0, axis_index_groups=z_groups)

    def gather_pair(rows):
        return lax.all_gather(rows, "row", axis=0, axis_index_groups=pairs)

    def in_order(parts):
        return parts.reshape(2, n_z, piece, width).transpose(1, 0, 2, 3).reshape(block_rows, width)

    turned_panel = lax.ppermute(panel, BOTH, transposing)
    panel_rows = gather_col(panel).reshape(block_rows, width)
    gram_part = product_tn(panel_rows, panel_rows).reshape(2, width // 2, width)
    keep = lax.dynamic_index_in_dim(gram_part, half, 0, False)
    give = lax.dynamic_index_in_dim(gram_part, 1 - half, 0, False)
    gram_part = keep + lax.ppermute(give, "row", swap)
    top_part = lax.dynamic_slice_in_dim(panel_rows, col * share, share, 0)
    z_parts = gather_z(jnp.concatenate([turned_panel, gram_part, top_part], 0))
    gram_part = jnp.sum(z_parts[:, piece : piece + width // 2], 0)
    both = gather_pair(
        jnp.concatenate(
            [z_parts[:, :piece].reshape(n_z * piece, width), gram_part, z_parts[0, -share:]], 0
        )
    )
    panel_cols = in_order(both[:, : n_z * piece])
    gram = both[:, n_z * piece : n_z * piece + width // 2].reshape(width, width)
    top_part = both[0, -share:]

    identity = jnp.eye(width, dtype=jnp.float32)
    lower_factor = jnp.linalg.cholesky(gram)
    panel_factor = lower_factor.T
    inverse_factor = jax.scipy.linalg.solve_triangular(lower_factor, identity, lower=True)

    def unit_rows(index):
        place = index * block_rows + jnp.arange(block_rows, dtype=jnp.int32)
        return (place[:, None] == jnp.arange(width, dtype=jnp.int32)[None, :]).astype(jnp.float32)

    basis_rows = product_nt(panel_rows, inverse_factor) + unit_rows(row)
    basis_cols = product_nt(panel_cols, inverse_factor) + unit_rows(col)
    partial = product(mobility, basis_cols)
    small = product_tn(basis_rows, partial)
    sent = jnp.concatenate(
        [
            partial.reshape(n_col, piece, width),
            small.reshape(n_col, share, width),
            jnp.broadcast_to(top_part[None], (n_col, share, width)),
        ],
        1,
    )
    got = lax.all_to_all(sent, "col", 0, 0)
    image = jnp.sum(got[:, : piece + share], 0)
    turned_image = lax.ppermute(image[:piece], BOTH, transposing)
    top_rows = got[:, piece + share :].reshape(width, width)
    kernel = invert_core(identity + product_nt(inverse_factor, top_rows))
    z_parts = gather_z(jnp.concatenate([turned_image, image[piece:]], 0))
    both = gather_pair(
        jnp.concatenate(
            [z_parts[:, :piece].reshape(n_z * piece, width), jnp.sum(z_parts[:, piece:], 0)], 0
        )
    )
    image_cols = in_order(both[:, : n_z * piece])
    small = both[0, n_z * piece :] + both[1, n_z * piece :]
    col_parts = gather_col(jnp.concatenate([image[:piece], small], 0))
    image_rows = col_parts[:, :piece].reshape(block_rows, width)
    small = col_parts[:, piece:].reshape(width, width)

    half_inner = 0.5 * product_tn(kernel, product(small, kernel))
    correction_rows = product(image_rows, kernel) - product(basis_rows, half_inner)
    correction_cols = product(image_cols, kernel) - product(basis_cols, half_inner)
    left_side = jnp.concatenate([basis_rows, correction_rows], axis=1)
    right_side = jnp.concatenate([correction_cols, basis_cols], axis=1)
    updated = mobility - product_nt(left_side, right_side)
    return (updated, panel_factor)


def solution(mesh):
    in_specs = (P(("row", "col"), None), P("row", "col"))
    out_specs = (P("row", "col"), P())
    return jax.shard_map(
        on_device, mesh=mesh, in_specs=in_specs, out_specs=out_specs, check_vma=False
    )
```

```python
import jax
import jax.numpy as jnp
from jax import lax
from jax.experimental import pallas as pl
from jax.experimental.pallas import tpu as pltpu
from jax.sharding import PartitionSpec as P

BOTH = ("row", "col")
STEP = 8
NN = (((1,), (0,)), ((), ()))
TN = (((0,), (0,)), ((), ()))
NT = (((1,), (1,)), ((), ()))


def product(first_op, second_op, dims=NN):
    return lax.dot_general(
        first_op,
        second_op,
        dims,
        precision=lax.Precision.HIGHEST,
        preferred_element_type=jnp.float32,
    )


def split(value):
    high = value.astype(jnp.bfloat16)
    return high, (value - high.astype(jnp.float32)).astype(jnp.bfloat16)


def left_terms(value):
    high, low = split(value)
    return jnp.concatenate([high, low, high], 1)


def right_terms(value):
    high, low = split(value)
    return jnp.concatenate([high, high, low], 1)


def exact_dot(first_op, second_op, dims):
    return lax.dot_general(first_op, second_op, dims, preferred_element_type=jnp.float32)


def unit_rows(index, shape):
    rows = lax.broadcasted_iota(jnp.int32, shape, 0) + index * shape[0]
    return jnp.where(rows == lax.broadcasted_iota(jnp.int32, shape, 1), 1.0, 0.0)


def eye(width):
    return unit_rows(0, (width, width))


def pieces_of(pairs_ref, n_z, piece):
    return jnp.concatenate(
        [pairs_ref[h, z * piece : (z + 1) * piece, :] for z in range(n_z) for h in range(2)], 0
    )


def factor_kernel(gram_ref, upper_ref, inverse_ref, work, other):
    width = gram_ref.shape[0]
    full = (STEP, width)
    lane = lax.broadcasted_iota(jnp.int32, full, 1)
    work[...] = gram_ref[...]
    other[...] = eye(width)
    for first in range(0, width, STEP):
        a_rows = [jnp.broadcast_to(work[first + k : first + k + 1, :], full) for k in range(STEP)]
        x_rows = [jnp.broadcast_to(other[first + k : first + k + 1, :], full) for k in range(STEP)]
        entry, mult, inv = {}, {}, {}
        for i in range(STEP):
            for k in range(i + 1):
                column = a_rows[i][:, first + k : first + k + 1]
                entry[i, k] = jnp.broadcast_to(column, full)
        for k in range(STEP):
            inv[k] = 1.0 / entry[k, k]
            for i in range(k + 1, STEP):
                mult[i, k] = entry[i, k] * inv[k]
            for i in range(k + 1, STEP):
                for l in range(k + 1, i + 1):
                    entry[i, l] = entry[i, l] - mult[i, k] * entry[l, k]
        for i in range(STEP):
            for k in range(i):
                a_rows[i] = a_rows[i] - mult[i, k] * a_rows[k]
                x_rows[i] = x_rows[i] - mult[i, k] * x_rows[k]
        for k in range(STEP):
            root = lax.rsqrt(entry[k, k])
            root = root * (1.5 - 0.5 * entry[k, k] * root * root)
            row = slice(first + k, first + k + 1)
            upper_ref[row, :] = jnp.where(lane >= first + k, a_rows[k] * root, 0.0)[:1]
            inverse_ref[row, :] = (x_rows[k] * root)[:1]
        if first + STEP == width:
            break
        a_back = [a_rows[k] * inv[k] for k in range(STEP)]
        x_back = [x_rows[k] * inv[k] for k in range(STEP)]
        for k in range(STEP - 2, -1, -1):
            for l in range(k + 1, STEP):
                a_back[k] = a_back[k] - mult[l, k] * a_back[l]
                x_back[k] = x_back[k] - mult[l, k] * x_back[l]
        for g in range(first + STEP, width, STEP):
            block = work[g : g + STEP, :]
            a_new, x_new = block, other[g : g + STEP, :]
            for k in range(STEP):
                column = jnp.broadcast_to(block[:, first + k : first + k + 1], full)
                a_new = a_new - column * a_back[k]
                x_new = x_new - column * x_back[k]
            work[g : g + STEP, :] = a_new
            other[g : g + STEP, :] = x_new


def factor(gram):
    width = gram.shape[0]
    shape = jax.ShapeDtypeStruct((width, width), jnp.float32)
    return pl.pallas_call(
        factor_kernel,
        out_shape=(shape, shape),
        scratch_shapes=[pltpu.VMEM((width, width), jnp.float32)] * 2,
        cost_estimate=pl.CostEstimate(
            flops=400_000_000, bytes_accessed=20_000_000, transcendentals=0
        ),
        name="factor",
    )(gram)


def partial_kernel(n_z, piece, share, place_ref, pairs_ref, mob_ref, out_ref, rhs):
    width = pairs_ref.shape[2]
    rows = mob_ref.shape[0]

    @pl.when(pl.program_id(0) == 0)
    def _():
        high, low = split(pieces_of(pairs_ref, n_z, piece))
        rhs[:, :width] = high
        rhs[:, width:] = low

    high, low = split(mob_ref[...])
    wide = exact_dot(high, rhs[...], NN)
    found = wide[:, :width] + wide[:, width:] + exact_dot(low, rhs[:, :width], NN)
    count = rows // piece
    out_ref[:, :piece, :] = found.reshape(count, piece, width)
    first = jnp.where(place_ref[1] == 0, mob_ref[:, :width], 0.0)
    out_ref[:, piece : 2 * piece, :] = first.reshape(count, piece, width)
    out_ref[:, 2 * piece :, :] = jnp.broadcast_to(
        pairs_ref[0, pairs_ref.shape[1] - share :, :][None], (count, share, width)
    )


def partial_sums(place, pairs, mobility, n_z, piece, share):
    n_rows, n_cols = mobility.shape
    width = pairs.shape[2]
    per = 2 * piece + share
    tile = 256
    return pl.pallas_call(
        lambda *refs: partial_kernel(n_z, piece, share, *refs),
        grid_spec=pltpu.PrefetchScalarGridSpec(
            num_scalar_prefetch=1,
            grid=(n_rows // tile,),
            in_specs=[
                pl.BlockSpec(pairs.shape, lambda i, p: (0, 0, 0)),
                pl.BlockSpec((tile, n_cols), lambda i, p: (i, 0)),
            ],
            out_specs=pl.BlockSpec((tile // piece, per, width), lambda i, p: (i, 0, 0)),
            scratch_shapes=[pltpu.VMEM((n_cols, 2 * width), jnp.bfloat16)],
        ),
        out_shape=jax.ShapeDtypeStruct((n_rows // piece, per, width), jnp.float32),
        cost_estimate=pl.CostEstimate(
            flops=6 * n_rows * n_cols * width, bytes_accessed=6_000_000, transcendentals=0
        ),
        name="partial_sums",
    )(place, pairs, mobility)


def image_kernel(piece, got_ref, inverse_ref, image_ref, copies_ref, top_ref):
    total = got_ref[0, : 2 * piece, :]
    for k in range(1, got_ref.shape[0]):
        total = total + got_ref[k, : 2 * piece, :]
    image = product(total[:piece], inverse_ref[...], NT) + total[piece:]
    image_ref[...] = image
    copies_ref[...] = jnp.broadcast_to(image[None], copies_ref.shape)
    top_ref[...] = got_ref[:, 2 * piece :, :].reshape(top_ref.shape)


def image_piece(got, inverse, piece):
    count, _, width = got.shape
    share = width // count
    return pl.pallas_call(
        lambda *refs: image_kernel(piece, *refs),
        out_shape=(
            jax.ShapeDtypeStruct((piece, width), jnp.float32),
            jax.ShapeDtypeStruct((count, piece, width), jnp.float32),
            jax.ShapeDtypeStruct((width, width), jnp.float32),
        ),
        cost_estimate=pl.CostEstimate(
            flops=10_000_000, bytes_accessed=2_000_000, transcendentals=0
        ),
        name="image_piece",
    )(got, inverse)


def basis_kernel(n_z, piece, place, rows_ref, pairs_ref, inverse_ref, top_ref, *outs):
    basis_rows, basis_cols, twisted, turned, kernel_ref, state_ref = outs
    width = inverse_ref.shape[0]
    inverse = inverse_ref[...]
    identity = eye(width)
    ratio = -product(inverse, top_ref[...], NT)

    state_ref[:width, :] = ratio
    state_ref[width:, :] = identity

    def go_on(state):
        return jnp.logical_and(state[0] < 40, state[1] > 1e-10)

    def double(state):
        power = state_ref[:width, :]
        both = product(state_ref[...], power)
        state_ref[:width, :] = both[:width]
        state_ref[width:, :] = state_ref[width:, :] + both[width:]
        return state[0] + 1, jnp.max(jnp.abs(both[:width]))

    lax.while_loop(go_on, double, (0, jnp.max(jnp.abs(ratio))))
    total = state_ref[width:, :]
    kernel = total + product(total, identity - product(identity - ratio, total))
    kernel_ref[...] = kernel
    inverse_terms = right_terms(inverse)
    rows = exact_dot(left_terms(rows_ref[...]), inverse_terms, NT)
    rows = rows + unit_rows(place[0], rows_ref.shape)
    basis_rows[...] = rows
    cols = exact_dot(left_terms(pieces_of(pairs_ref, n_z, piece)), inverse_terms, NT)
    basis_cols[...] = cols + unit_rows(place[1], cols.shape)
    terms = left_terms(rows)
    twisted[...] = exact_dot(terms, right_terms(kernel.T), NT)
    turned[...] = exact_dot(terms, right_terms(kernel), NT)


def bases(place, panel_rows, pairs, inverse, top_rows, n_z, piece):
    width = inverse.shape[0]
    long = jax.ShapeDtypeStruct(panel_rows.shape, jnp.float32)
    vmem = pl.BlockSpec(memory_space=pltpu.VMEM)
    return pl.pallas_call(
        lambda *refs: basis_kernel(n_z, piece, *refs),
        in_specs=[pl.BlockSpec(memory_space=pltpu.SMEM)] + [vmem] * 4,
        out_specs=[vmem] * 5,
        out_shape=(long, long, long, long, jax.ShapeDtypeStruct((width, width), jnp.float32)),
        scratch_shapes=[pltpu.VMEM((2 * width, width), jnp.float32)],
        cost_estimate=pl.CostEstimate(
            flops=300_000_000, bytes_accessed=10_000_000, transcendentals=0
        ),
        name="bases",
    )(place, panel_rows, pairs, inverse, top_rows)


def first_update_kernel(image_ref, kernel_ref, cols_ref, mob_ref, out_ref, rhs):
    @pl.when(pl.program_id(0) == 0)
    def _():
        rhs[...] = right_terms(cols_ref[...])

    spread = product(image_ref[...], kernel_ref[...])
    out_ref[...] = mob_ref[...] - exact_dot(left_terms(spread), rhs[...], NT)


def first_update(image_rows, kernel, basis_cols, mobility):
    n_rows, n_cols = mobility.shape
    width = kernel.shape[0]
    tile = 256
    return pl.pallas_call(
        first_update_kernel,
        grid=(n_rows // tile,),
        in_specs=[
            pl.BlockSpec((tile, width), lambda i: (i, 0)),
            pl.BlockSpec((width, width), lambda i: (0, 0)),
            pl.BlockSpec((n_cols, width), lambda i: (0, 0)),
            pl.BlockSpec((tile, n_cols), lambda i: (i, 0)),
        ],
        out_specs=pl.BlockSpec((tile, n_cols), lambda i: (i, 0)),
        out_shape=jax.ShapeDtypeStruct(mobility.shape, jnp.float32),
        scratch_shapes=[pltpu.VMEM((n_cols, 3 * width), jnp.bfloat16)],
        cost_estimate=pl.CostEstimate(
            flops=6 * n_rows * n_cols * width, bytes_accessed=9_000_000, transcendentals=0
        ),
        name="first_update",
    )(image_rows, kernel, basis_cols, mobility)


def last_update_kernel(n_z, piece, pairs_ref, cols_ref, turned_ref, half_ref, out_ref, rhs):
    width = cols_ref.shape[1]

    @pl.when(pl.program_id(0) == 0)
    def _():
        start = n_z * piece
        small = pairs_ref[:, start : start + width // 2, :].reshape(width, width)
        image_cols = pieces_of(pairs_ref, n_z, piece)
        rhs[...] = right_terms(image_cols - product(cols_ref[...], small))

    out_ref[...] = half_ref[...] - exact_dot(left_terms(turned_ref[...]), rhs[...], NT)


def last_update(pairs, basis_cols, turned, halfway, n_z, piece):
    n_rows, n_cols = halfway.shape
    width = basis_cols.shape[1]
    tile = 256
    return pl.pallas_call(
        lambda *refs: last_update_kernel(n_z, piece, *refs),
        grid=(n_rows // tile,),
        in_specs=[
            pl.BlockSpec(pairs.shape, lambda i: (0, 0, 0)),
            pl.BlockSpec((n_cols, width), lambda i: (0, 0)),
            pl.BlockSpec((tile, width), lambda i: (i, 0)),
            pl.BlockSpec((tile, n_cols), lambda i: (i, 0)),
        ],
        out_specs=pl.BlockSpec((tile, n_cols), lambda i: (i, 0)),
        out_shape=jax.ShapeDtypeStruct(halfway.shape, jnp.float32),
        scratch_shapes=[pltpu.VMEM((n_cols, 3 * width), jnp.bfloat16)],
        cost_estimate=pl.CostEstimate(
            flops=6 * n_rows * n_cols * width, bytes_accessed=9_000_000, transcendentals=0
        ),
        name="last_update",
    )(pairs, basis_cols, turned, halfway)


def on_device(panel, mobility):
    piece, width = panel.shape
    n_row, n_col = lax.axis_size("row"), lax.axis_size("col")
    block_rows, block_cols = mobility.shape
    row, col = lax.axis_index("row"), lax.axis_index("col")
    place = jnp.stack([row, col]).astype(jnp.int32)
    half = row % 2
    n_z = n_row // 2
    share = width // n_col
    z_groups = [[2 * z + h for z in range(n_z)] for h in range(2)]
    pairs = [[2 * z, 2 * z + 1] for z in range(n_z)]
    transposing = [(i * n_col + j, j * n_col + i) for i in range(n_row) for j in range(n_col)]
    swap = [(i, i ^ 1) for i in range(n_row)]

    def copies(rows, count):
        return jnp.broadcast_to(rows[None], (count,) + rows.shape)

    def gather_row(lone, summed, extra):
        summed = summed.reshape(2, width // 2, width)
        keep = lax.dynamic_index_in_dim(summed, half, 0, False)
        give = lax.dynamic_index_in_dim(summed, 1 - half, 0, False)
        summed = keep + lax.ppermute(give, "row", swap)
        sent = jnp.concatenate([lone, summed] + extra, 0)
        parts = lax.all_to_all(copies(sent, n_z), "row", 0, 0, axis_index_groups=z_groups)
        lone = parts[:, :piece].reshape(n_z * piece, width)
        summed = jnp.sum(parts[:, piece : piece + width // 2], 0)
        extra = [parts[0, piece + width // 2 :]] if extra else []
        sent = jnp.concatenate([lone, summed] + extra, 0)
        return lax.all_gather(sent, "row", axis=0, axis_index_groups=pairs)

    turned_panel = lax.ppermute(panel, BOTH, transposing)
    panel_rows = lax.all_to_all(copies(panel, n_col), "col", 0, 0).reshape(block_rows, width)
    gram_part = product(panel_rows, panel_rows, TN)
    top_part = lax.dynamic_slice_in_dim(panel_rows, col * share, share, 0)
    panel_pairs = gather_row(turned_panel, gram_part, [top_part])
    start = n_z * piece
    gram = panel_pairs[:, start : start + width // 2].reshape(width, width)

    sent = partial_sums(place, panel_pairs, mobility, n_z, piece, share)
    got = lax.all_to_all(sent, "col", 0, 0)
    panel_factor, inverse = factor(gram)
    image, image_copies, top_rows = image_piece(got, inverse, piece)
    turned_image = lax.ppermute(image, BOTH, transposing)
    image_rows = lax.all_to_all(image_copies, "col", 0, 0).reshape(block_rows, width)
    basis_rows, basis_cols, twisted, turned, kernel = bases(
        place, panel_rows, panel_pairs, inverse, top_rows, n_z, piece
    )
    inner_part = product(twisted, image_rows, TN)
    image_pairs = gather_row(turned_image, inner_part, [])
    halfway = first_update(image_rows, kernel, basis_cols, mobility)
    updated = last_update(image_pairs, basis_cols, turned, halfway, n_z, piece)
    return (updated, panel_factor)


def solution(mesh):
    in_specs = (P(("row", "col"), None), P("row", "col"))
    out_specs = (P("row", "col"), P())
    return jax.shard_map(
        on_device, mesh=mesh, in_specs=in_specs, out_specs=out_specs, check_vma=False
    )
```

```python
import jax
import jax.numpy as jnp
from jax import lax
from jax.experimental import pallas as pl
from jax.experimental.pallas import tpu as pltpu
from jax.sharding import PartitionSpec as P

BOTH = ("row", "col")
STEP = 8
MIB = 1 << 20
NN = (((1,), (0,)), ((), ()))
TN = (((0,), (0,)), ((), ()))
NT = (((1,), (1,)), ((), ()))


def product(first_op, second_op, dims=NN):
    return lax.dot_general(
        first_op,
        second_op,
        dims,
        precision=lax.Precision.HIGHEST,
        preferred_element_type=jnp.float32,
    )


def split(value):
    high = value.astype(jnp.bfloat16)
    return high, (value - high.astype(jnp.float32)).astype(jnp.bfloat16)


def left_terms(value):
    high, low = split(value)
    return jnp.concatenate([high, low, high], 1)


def right_terms(value):
    high, low = split(value)
    return jnp.concatenate([high, high, low], 1)


def exact_dot(first_op, second_op, dims):
    return lax.dot_general(first_op, second_op, dims, preferred_element_type=jnp.float32)


def unit_rows(index, shape):
    rows = lax.broadcasted_iota(jnp.int32, shape, 0) + index * shape[0]
    return jnp.where(rows == lax.broadcasted_iota(jnp.int32, shape, 1), 1.0, 0.0)


def eye(width):
    return unit_rows(0, (width, width))


def pieces_of(pairs_ref, n_z, piece):
    return jnp.concatenate(
        [pairs_ref[h, z * piece : (z + 1) * piece, :] for z in range(n_z) for h in range(2)], 0
    )


def keep_and_give(place_ref, value, keep_ref, give_ref):
    side = value.shape[0] // 2
    even = lax.rem(place_ref[0], 2) == 0
    keep_ref[...] = jnp.where(even, value[:side], value[side:])
    give_ref[...] = jnp.where(even, value[side:], value[:side])


def gram_kernel(piece, place_ref, got_ref, rows_ref, keep_ref, give_ref, top_ref, first_ref):
    share = top_ref.shape[0]
    rows = got_ref[:, :piece, :].reshape(rows_ref.shape)
    rows_ref[...] = rows
    keep_and_give(place_ref, product(rows, rows, TN), keep_ref, give_ref)
    start = pl.multiple_of(place_ref[1] * share, share)
    top_ref[...] = rows_ref[pl.ds(start, share), :]
    first_ref[...] = got_ref[0, piece:, :]


def gram_parts(place, got, piece):
    count, _, width = got.shape
    vmem = pl.BlockSpec(memory_space=pltpu.VMEM)
    shapes = [(count * piece, width), (width // 2, width), (width // 2, width)]
    shapes += [(width // count, width), (piece, width)]
    return pl.pallas_call(
        lambda *refs: gram_kernel(piece, *refs),
        in_specs=[pl.BlockSpec(memory_space=pltpu.SMEM), vmem],
        out_specs=[vmem] * 5,
        out_shape=[jax.ShapeDtypeStruct(shape, jnp.float32) for shape in shapes],
        cost_estimate=pl.CostEstimate(
            flops=200_000_000, bytes_accessed=3_000_000, transcendentals=0
        ),
        compiler_params=pltpu.CompilerParams(vmem_limit_bytes=8 * MIB),
        name="gram_parts",
    )(place, got)


def inner_kernel(place_ref, twisted_ref, rows_ref, keep_ref, give_ref):
    keep_and_give(place_ref, product(twisted_ref[...], rows_ref[...]), keep_ref, give_ref)


def inner_parts(place, twisted, rows):
    width = rows.shape[1]
    vmem = pl.BlockSpec(memory_space=pltpu.VMEM)
    return pl.pallas_call(
        inner_kernel,
        in_specs=[pl.BlockSpec(memory_space=pltpu.SMEM), vmem, vmem],
        out_specs=[vmem] * 2,
        out_shape=[jax.ShapeDtypeStruct((width // 2, width), jnp.float32)] * 2,
        cost_estimate=pl.CostEstimate(
            flops=200_000_000, bytes_accessed=1_000_000, transcendentals=0
        ),
        compiler_params=pltpu.CompilerParams(vmem_limit_bytes=6 * MIB),
        name="inner_parts",
    )(place, twisted, rows)


def factor_kernel(gram_ref, upper_ref, inverse_ref, work, other):
    width = upper_ref.shape[0]
    full = (STEP, width)
    lane = lax.broadcasted_iota(jnp.int32, full, 1)
    work[...] = gram_ref[...].reshape(width, width)
    other[...] = eye(width)
    for first in range(0, width, STEP):
        a_rows = [jnp.broadcast_to(work[first + k : first + k + 1, :], full) for k in range(STEP)]
        x_rows = [jnp.broadcast_to(other[first + k : first + k + 1, :], full) for k in range(STEP)]
        entry, mult, inv = {}, {}, {}
        for i in range(STEP):
            for k in range(i + 1):
                column = a_rows[i][:, first + k : first + k + 1]
                entry[i, k] = jnp.broadcast_to(column, full)
        for k in range(STEP):
            inv[k] = 1.0 / entry[k, k]
            for i in range(k + 1, STEP):
                mult[i, k] = entry[i, k] * inv[k]
            for i in range(k + 1, STEP):
                for l in range(k + 1, i + 1):
                    entry[i, l] = entry[i, l] - mult[i, k] * entry[l, k]
        for i in range(STEP):
            for k in range(i):
                a_rows[i] = a_rows[i] - mult[i, k] * a_rows[k]
                x_rows[i] = x_rows[i] - mult[i, k] * x_rows[k]
        for k in range(STEP):
            root = lax.rsqrt(entry[k, k])
            root = root * (1.5 - 0.5 * entry[k, k] * root * root)
            row = slice(first + k, first + k + 1)
            upper_ref[row, :] = jnp.where(lane >= first + k, a_rows[k] * root, 0.0)[:1]
            inverse_ref[row, :] = (x_rows[k] * root)[:1]
        if first + STEP == width:
            break
        a_back = [a_rows[k] * inv[k] for k in range(STEP)]
        x_back = [x_rows[k] * inv[k] for k in range(STEP)]
        for k in range(STEP - 2, -1, -1):
            for l in range(k + 1, STEP):
                a_back[k] = a_back[k] - mult[l, k] * a_back[l]
                x_back[k] = x_back[k] - mult[l, k] * x_back[l]
        for g in range(first + STEP, width, STEP):
            block = work[g : g + STEP, :]
            a_new, x_new = block, other[g : g + STEP, :]
            for k in range(STEP):
                column = jnp.broadcast_to(block[:, first + k : first + k + 1], full)
                a_new = a_new - column * a_back[k]
                x_new = x_new - column * x_back[k]
            work[g : g + STEP, :] = a_new
            other[g : g + STEP, :] = x_new


def factor(pairs, start):
    width = pairs.shape[2]
    side = width // 2
    shape = jax.ShapeDtypeStruct((width, width), jnp.float32)
    return pl.pallas_call(
        factor_kernel,
        grid=(1,),
        in_specs=[pl.BlockSpec((2, side, width), lambda i: (0, start // side, 0))],
        out_specs=[pl.BlockSpec((width, width), lambda i: (0, 0))] * 2,
        out_shape=(shape, shape),
        scratch_shapes=[pltpu.VMEM((width, width), jnp.float32)] * 2,
        cost_estimate=pl.CostEstimate(
            flops=400_000_000, bytes_accessed=20_000_000, transcendentals=0
        ),
        compiler_params=pltpu.CompilerParams(vmem_limit_bytes=4 * MIB),
        name="factor",
    )(pairs)


def partial_kernel(n_z, piece, share, pairs_ref, mob_ref, out_ref, rhs, held, sems):
    width = pairs_ref.shape[2]
    n_rows = held.shape[0]
    parts = sems.shape[0]
    tile = n_rows // parts
    loads = []
    for k in range(parts):
        rows = pl.ds(k * tile, tile)
        loads.append(pltpu.make_async_copy(mob_ref.at[rows], held.at[rows], sems.at[k]))
        loads[k].start()
    high, low = split(pieces_of(pairs_ref, n_z, piece))
    rhs[:, :width] = high
    rhs[:, width:] = low
    last = pairs_ref.shape[1] - share
    out_ref[:, piece:, :] = jnp.broadcast_to(
        pairs_ref[0, last:, :][None], (out_ref.shape[0], share, width)
    )
    count = tile // piece
    for k in range(parts):
        loads[k].wait()
        high, low = split(held[k * tile : (k + 1) * tile, :])
        wide = exact_dot(high, rhs[...], NN)
        found = wide[:, :width] + wide[:, width:] + exact_dot(low, rhs[:, :width], NN)
        out_ref[k * count : (k + 1) * count, :piece, :] = found.reshape(count, piece, width)


def partial_sums(pairs, mobility, n_z, piece, share):
    n_rows, n_cols = mobility.shape
    width = pairs.shape[2]
    vmem = pl.BlockSpec(memory_space=pltpu.VMEM)
    return pl.pallas_call(
        lambda *refs: partial_kernel(n_z, piece, share, *refs),
        in_specs=[vmem, pl.BlockSpec(memory_space=pl.ANY)],
        out_specs=vmem,
        out_shape=jax.ShapeDtypeStruct((n_rows // piece, piece + share, width), jnp.float32),
        scratch_shapes=[
            pltpu.VMEM((n_cols, 2 * width), jnp.bfloat16),
            pltpu.VMEM(mobility.shape, jnp.float32),
            pltpu.SemaphoreType.DMA((4,)),
        ],
        cost_estimate=pl.CostEstimate(
            flops=6 * n_rows * n_cols * width, bytes_accessed=6_000_000, transcendentals=0
        ),
        compiler_params=pltpu.CompilerParams(vmem_limit_bytes=58 * MIB),
        name="partial_sums",
    )(pairs, mobility)


def image_kernel(piece, got_ref, first_ref, inverse_ref, image_ref, copies_ref, top_ref):
    total = got_ref[0, :piece, :]
    for k in range(1, got_ref.shape[0]):
        total = total + got_ref[k, :piece, :]
    image = product(total, inverse_ref[...], NT) + first_ref[...]
    image_ref[...] = image
    copies_ref[...] = jnp.broadcast_to(image[None], copies_ref.shape)
    top_ref[...] = got_ref[:, piece:, :].reshape(top_ref.shape)


def image_piece(got, first, inverse, piece):
    count, _, width = got.shape
    square = jax.ShapeDtypeStruct((width, width), jnp.float32)
    return pl.pallas_call(
        lambda *refs: image_kernel(piece, *refs),
        grid=(1,),
        in_specs=[
            pl.BlockSpec(got.shape, lambda i: (0, 0, 0)),
            pl.BlockSpec((piece, width), lambda i: (0, 0)),
            pl.BlockSpec((width, width), lambda i: (0, 0)),
        ],
        out_specs=[
            pl.BlockSpec((piece, width), lambda i: (0, 0)),
            pl.BlockSpec((count, piece, width), lambda i: (0, 0, 0)),
            pl.BlockSpec((width, width), lambda i: (0, 0)),
        ],
        out_shape=(
            jax.ShapeDtypeStruct((piece, width), jnp.float32),
            jax.ShapeDtypeStruct((count, piece, width), jnp.float32),
            square,
        ),
        cost_estimate=pl.CostEstimate(
            flops=10_000_000, bytes_accessed=2_000_000, transcendentals=0
        ),
        compiler_params=pltpu.CompilerParams(vmem_limit_bytes=6 * MIB),
        name="image_piece",
    )(got, first, inverse)


def basis_kernel(n_z, piece, place, rows_ref, pairs_ref, inverse_ref, top_ref, *outs):
    cols_left, cols_right, twisted, turned, kernel_ref, state_ref = outs
    width = inverse_ref.shape[0]
    inverse = inverse_ref[...]
    identity = eye(width)
    ratio = -product(inverse, top_ref[...], NT)

    state_ref[:width, :] = ratio
    state_ref[width:, :] = identity

    def go_on(state):
        return jnp.logical_and(state[0] < 40, state[1] > 1e-10)

    def double(state):
        power = state_ref[:width, :]
        both = product(state_ref[...], power)
        state_ref[:width, :] = both[:width]
        state_ref[width:, :] = state_ref[width:, :] + both[width:]
        return state[0] + 1, jnp.max(jnp.abs(both[:width]))

    lax.while_loop(go_on, double, (0, jnp.max(jnp.abs(ratio))))
    total = state_ref[width:, :]
    kernel = total + product(total, identity - product(identity - ratio, total))
    kernel_ref[...] = kernel
    inverse_terms = right_terms(inverse)
    rows = exact_dot(left_terms(rows_ref[...]), inverse_terms, NT)
    rows = rows + unit_rows(place[0], rows_ref.shape)
    cols = exact_dot(left_terms(pieces_of(pairs_ref, n_z, piece)), inverse_terms, NT)
    cols = cols + unit_rows(place[1], cols.shape)
    cols_left[...] = left_terms(cols)
    cols_right[...] = right_terms(cols)
    terms = left_terms(rows)
    twisted[...] = exact_dot(right_terms(kernel.T), terms, NT)
    turned[...] = left_terms(exact_dot(terms, right_terms(kernel), NT))


def bases(place, panel_rows, pairs, inverse, top_rows, n_z, piece):
    width = inverse.shape[0]
    terms = jax.ShapeDtypeStruct((panel_rows.shape[0], 3 * width), jnp.bfloat16)
    vmem = pl.BlockSpec(memory_space=pltpu.VMEM)
    return pl.pallas_call(
        lambda *refs: basis_kernel(n_z, piece, *refs),
        in_specs=[pl.BlockSpec(memory_space=pltpu.SMEM)] + [vmem] * 4,
        out_specs=[vmem] * 5,
        out_shape=(
            terms,
            terms,
            jax.ShapeDtypeStruct(panel_rows.shape[::-1], jnp.float32),
            terms,
            jax.ShapeDtypeStruct((width, width), jnp.float32),
        ),
        scratch_shapes=[pltpu.VMEM((2 * width, width), jnp.float32)],
        cost_estimate=pl.CostEstimate(
            flops=300_000_000, bytes_accessed=10_000_000, transcendentals=0
        ),
        compiler_params=pltpu.CompilerParams(vmem_limit_bytes=16 * MIB),
        name="bases",
    )(place, panel_rows, pairs, inverse, top_rows)


def stream(source_ref, out_ref, held, sems_in, sems_out, prepare, change):
    parts = sems_in.shape[0]
    tile = held.shape[0] // parts
    loads, stores = [], []
    for k in range(parts):
        rows = pl.ds(k * tile, tile)
        loads.append(pltpu.make_async_copy(source_ref.at[rows], held.at[rows], sems_in.at[k]))
        stores.append(pltpu.make_async_copy(held.at[rows], out_ref.at[rows], sems_out.at[k]))
        loads[k].start()
    prepare()
    for k in range(parts):
        loads[k].wait()
        rows = slice(k * tile, (k + 1) * tile)
        held[rows, :] = change(held[rows, :], rows)
        stores[k].start()
    for k in range(parts):
        stores[k].wait()


def first_update_kernel(image_ref, kernel_ref, cols_ref, mob_ref, out_ref, lhs, held, *sems):
    def prepare():
        lhs[...] = left_terms(product(image_ref[...], kernel_ref[...]))

    def change(value, rows):
        return value - exact_dot(lhs[rows, :], cols_ref[...], NT)

    stream(mob_ref, out_ref, held, *sems, prepare, change)


def update_call(kernel, inputs, matrix, terms, name):
    n_rows, n_cols = matrix.shape
    vmem = pl.BlockSpec(memory_space=pltpu.VMEM)
    hbm = pl.BlockSpec(memory_space=pl.ANY)
    return pl.pallas_call(
        kernel,
        in_specs=[vmem] * len(inputs) + [hbm],
        out_specs=hbm,
        out_shape=jax.ShapeDtypeStruct(matrix.shape, jnp.float32),
        scratch_shapes=[
            pltpu.VMEM((n_rows, terms), jnp.bfloat16),
            pltpu.VMEM(matrix.shape, jnp.float32),
            pltpu.SemaphoreType.DMA((4,)),
            pltpu.SemaphoreType.DMA((4,)),
        ],
        cost_estimate=pl.CostEstimate(
            flops=2 * n_rows * n_cols * terms, bytes_accessed=9_000_000, transcendentals=0
        ),
        compiler_params=pltpu.CompilerParams(vmem_limit_bytes=58 * MIB),
        name=name,
    )(*inputs, matrix)


def last_update_kernel(n_z, piece, pairs_ref, cols_ref, turned_ref, half_ref, out_ref, rhs, held, *sems):
    width = pairs_ref.shape[2]

    def prepare():
        start = n_z * piece
        small = pairs_ref[:, start : start + width // 2, :].reshape(width, width)
        change_cols = exact_dot(cols_ref[...], right_terms(small.T), NT)
        rhs[...] = right_terms(pieces_of(pairs_ref, n_z, piece) - change_cols)

    def change(value, rows):
        return value - exact_dot(turned_ref[rows, :], rhs[...], NT)

    stream(half_ref, out_ref, held, *sems, prepare, change)


def on_device(panel, mobility):
    piece, width = panel.shape
    n_row, n_col = lax.axis_size("row"), lax.axis_size("col")
    block_rows, block_cols = mobility.shape
    row, col = lax.axis_index("row"), lax.axis_index("col")
    place = jnp.stack([row, col]).astype(jnp.int32)
    n_z = n_row // 2
    share = width // n_col
    z_groups = [[2 * z + h for z in range(n_z)] for h in range(2)]
    pairs = [[2 * z, 2 * z + 1] for z in range(n_z)]
    transposing = [(i * n_col + j, j * n_col + i) for i in range(n_row) for j in range(n_col)]
    swap = [(i, i ^ 1) for i in range(n_row)]

    def copies(rows, count):
        return jnp.broadcast_to(rows[None], (count,) + rows.shape)

    def gather_row(lone, keep, give, extra):
        summed = keep + lax.ppermute(give, "row", swap)
        sent = copies(jnp.concatenate([lone, summed] + extra, 0), n_z)
        parts = lax.all_to_all(sent, "row", 0, 0, axis_index_groups=z_groups)
        lone = parts[:, :piece].reshape(n_z * piece, width)
        summed = jnp.sum(parts[:, piece : piece + width // 2], 0)
        extra = [parts[0, piece + width // 2 :]] if extra else []
        sent = jnp.concatenate([lone, summed] + extra, 0)
        return lax.all_gather(sent, "row", axis=0, axis_index_groups=pairs)

    turned_panel = lax.ppermute(panel, BOTH, transposing)
    first_cols = mobility[:, :width].reshape(n_col, piece, width)
    got = lax.all_to_all(
        jnp.concatenate([copies(panel, n_col), first_cols], 1), "col", 0, 0
    )
    got, turned_panel = lax.optimization_barrier((got, turned_panel))
    panel_rows, keep, give, top_part, first = gram_parts(place, got, piece)
    panel_pairs = gather_row(turned_panel, keep, give, [top_part])

    sent = partial_sums(panel_pairs, mobility, n_z, piece, share)
    got = lax.all_to_all(sent, "col", 0, 0)
    panel_factor, inverse = factor(panel_pairs, n_z * piece)
    image, image_copies, top_rows = image_piece(got, first, inverse, piece)
    turned_image = lax.ppermute(image, BOTH, transposing)
    image_rows = lax.all_to_all(image_copies, "col", 0, 0).reshape(block_rows, width)
    cols_left, cols_right, twisted, turned, kernel = bases(
        place, panel_rows, panel_pairs, inverse, top_rows, n_z, piece
    )
    image_rows, turned_image = lax.optimization_barrier((image_rows, turned_image))
    keep, give = inner_parts(place, twisted, image_rows)
    image_pairs = gather_row(turned_image, keep, give, [])
    terms = 3 * width
    halfway = update_call(
        first_update_kernel, (image_rows, kernel, cols_right), mobility, terms, "first_update"
    )
    updated = update_call(
        lambda *refs: last_update_kernel(n_z, piece, *refs),
        (image_pairs, cols_left, turned),
        halfway,
        terms,
        "last_update",
    )
    return (updated, panel_factor)


def solution(mesh):
    in_specs = (P(("row", "col"), None), P("row", "col"))
    out_specs = (P("row", "col"), P())
    return jax.shard_map(
        on_device, mesh=mesh, in_specs=in_specs, out_specs=out_specs, check_vma=False
    )
```

```python
import jax
import jax.numpy as jnp
from jax import lax
from jax.experimental import pallas as pl
from jax.experimental.pallas import tpu as pltpu
from jax.sharding import PartitionSpec as P

BOTH = ("row", "col")
STEP = 8
MIB = 1 << 20
NN = (((1,), (0,)), ((), ()))
TN = (((0,), (0,)), ((), ()))
NT = (((1,), (1,)), ((), ()))


def product(first_op, second_op, dims=NN):
    return lax.dot_general(
        first_op,
        second_op,
        dims,
        precision=lax.Precision.HIGHEST,
        preferred_element_type=jnp.float32,
    )


def split(value):
    high = value.astype(jnp.bfloat16)
    return high, (value - high.astype(jnp.float32)).astype(jnp.bfloat16)


def left_terms(value):
    high, low = split(value)
    return jnp.concatenate([high, low, high], 1)


def right_terms(value):
    high, low = split(value)
    return jnp.concatenate([high, high, low], 1)


def exact_dot(first_op, second_op, dims):
    return lax.dot_general(first_op, second_op, dims, preferred_element_type=jnp.float32)


def unit_rows(index, shape):
    rows = lax.broadcasted_iota(jnp.int32, shape, 0) + index * shape[0]
    return jnp.where(rows == lax.broadcasted_iota(jnp.int32, shape, 1), 1.0, 0.0)


def eye(width):
    return unit_rows(0, (width, width))


def pieces_of(pairs_ref, n_z, piece):
    return jnp.concatenate(
        [pairs_ref[h, z * piece : (z + 1) * piece, :] for z in range(n_z) for h in range(2)], 0
    )


def pack(place_ref, value, keep_ref, give_ref):
    side = value.shape[0] // 2
    half = side // 2
    top = value[:side]
    low = pltpu.roll(value[side:], side, 1)
    row = lax.broadcasted_iota(jnp.int32, top.shape, 0)
    lane = lax.broadcasted_iota(jnp.int32, top.shape, 1)
    rows = jnp.where(jnp.logical_and(row < lane, lane < side), low, top)
    last = jnp.sum(jnp.where(row == lane, low, 0.0), axis=0, keepdims=True)
    even = lax.rem(place_ref[0], 2) == 0
    keep_ref[:half, :] = jnp.where(even, rows[:half], rows[half:])
    give_ref[:half, :] = jnp.where(even, rows[half:], rows[:half])
    keep_ref[half:, :] = jnp.broadcast_to(last, (STEP, last.shape[1]))
    give_ref[half:, :] = jnp.broadcast_to(last, (STEP, last.shape[1]))


def unpack(packed):
    half = packed.shape[1] - STEP
    side = 2 * half
    rows = packed[:, :half, :].reshape(side, packed.shape[2])
    turned = rows.T
    row = lax.broadcasted_iota(jnp.int32, (side, side), 0)
    lane = lax.broadcasted_iota(jnp.int32, (side, side), 1)
    left, across = rows[:, :side], turned[:side]
    last = packed[0, half : half + 1, :side]
    a = jnp.where(row >= lane, left, across)
    d = jnp.where(row == lane, last, jnp.where(row < lane, left, across))
    return jnp.concatenate(
        [
            jnp.concatenate([a, rows[:, side:]], 1),
            jnp.concatenate([turned[side:], d], 1),
        ],
        0,
    )


def gram_kernel(place_ref, rows_ref, keep_ref, give_ref, top_ref):
    share = top_ref.shape[0]
    rows = rows_ref[...]
    pack(place_ref, product(rows, rows, TN), keep_ref, give_ref)
    start = pl.multiple_of(place_ref[1] * share, share)
    top_ref[...] = rows_ref[pl.ds(start, share), :]


def inner_kernel(place_ref, turned_ref, rows_ref, keep_ref, give_ref):
    terms = product(turned_ref[...], rows_ref[...])
    pack(place_ref, 0.5 * (terms + terms.T), keep_ref, give_ref)


def packed_parts(kernel, place, operands, extra, name):
    width = operands[-1].shape[1]
    vmem = pl.BlockSpec(memory_space=pltpu.VMEM)
    shapes = [(width // 4 + STEP, width)] * 2 + extra
    return pl.pallas_call(
        kernel,
        in_specs=[pl.BlockSpec(memory_space=pltpu.SMEM)] + [vmem] * len(operands),
        out_specs=[vmem] * len(shapes),
        out_shape=[jax.ShapeDtypeStruct(shape, jnp.float32) for shape in shapes],
        cost_estimate=pl.CostEstimate(
            flops=200_000_000, bytes_accessed=3_000_000, transcendentals=0
        ),
        compiler_params=pltpu.CompilerParams(vmem_limit_bytes=8 * MIB),
        name=name,
    )(place, *operands)


def factor_kernel(gram_ref, upper_ref, inverse_ref, work, other):
    width = upper_ref.shape[0]
    full = (STEP, width)
    lane = lax.broadcasted_iota(jnp.int32, full, 1)
    work[...] = unpack(gram_ref[...])
    other[...] = eye(width)
    for first in range(0, width, STEP):
        a_rows = [jnp.broadcast_to(work[first + k : first + k + 1, :], full) for k in range(STEP)]
        x_rows = [jnp.broadcast_to(other[first + k : first + k + 1, :], full) for k in range(STEP)]
        entry, mult, inv = {}, {}, {}
        for i in range(STEP):
            for k in range(i + 1):
                column = a_rows[i][:, first + k : first + k + 1]
                entry[i, k] = jnp.broadcast_to(column, full)
        for k in range(STEP):
            inv[k] = 1.0 / entry[k, k]
            for i in range(k + 1, STEP):
                mult[i, k] = entry[i, k] * inv[k]
            for i in range(k + 1, STEP):
                for l in range(k + 1, i + 1):
                    entry[i, l] = entry[i, l] - mult[i, k] * entry[l, k]
        for i in range(STEP):
            for k in range(i):
                a_rows[i] = a_rows[i] - mult[i, k] * a_rows[k]
                x_rows[i] = x_rows[i] - mult[i, k] * x_rows[k]
        for k in range(STEP):
            root = lax.rsqrt(entry[k, k])
            root = root * (1.5 - 0.5 * entry[k, k] * root * root)
            row = slice(first + k, first + k + 1)
            upper_ref[row, :] = jnp.where(lane >= first + k, a_rows[k] * root, 0.0)[:1]
            inverse_ref[row, :] = (x_rows[k] * root)[:1]
        if first + STEP == width:
            break
        a_back = [a_rows[k] * inv[k] for k in range(STEP)]
        x_back = [x_rows[k] * inv[k] for k in range(STEP)]
        for k in range(STEP - 2, -1, -1):
            for l in range(k + 1, STEP):
                a_back[k] = a_back[k] - mult[l, k] * a_back[l]
                x_back[k] = x_back[k] - mult[l, k] * x_back[l]
        for g in range(first + STEP, width, STEP):
            block = work[g : g + STEP, :]
            a_new, x_new = block, other[g : g + STEP, :]
            for k in range(STEP):
                column = jnp.broadcast_to(block[:, first + k : first + k + 1], full)
                a_new = a_new - column * a_back[k]
                x_new = x_new - column * x_back[k]
            work[g : g + STEP, :] = a_new
            other[g : g + STEP, :] = x_new


def factor(packed):
    width = packed.shape[2]
    shape = jax.ShapeDtypeStruct((width, width), jnp.float32)
    vmem = pl.BlockSpec(memory_space=pltpu.VMEM)
    return pl.pallas_call(
        factor_kernel,
        in_specs=[vmem],
        out_specs=[vmem] * 2,
        out_shape=(shape, shape),
        scratch_shapes=[pltpu.VMEM((width, width), jnp.float32)] * 2,
        cost_estimate=pl.CostEstimate(
            flops=400_000_000, bytes_accessed=200_000, transcendentals=0
        ),
        compiler_params=pltpu.CompilerParams(vmem_limit_bytes=4 * MIB),
        name="factor",
    )(packed)


def partial_kernel(n_z, piece, share, place, pairs_ref, inverse_ref, mob_ref, *refs):
    out_ref, rhs, held, sems = refs
    width = pairs_ref.shape[2]
    n_rows = held.shape[0]
    parts = sems.shape[0]
    tile = n_rows // parts
    loads = []
    for k in range(parts):
        rows = pl.ds(k * tile, tile)
        loads.append(pltpu.make_async_copy(mob_ref.at[rows], held.at[rows], sems.at[k]))
        loads[k].start()
    cols = exact_dot(
        left_terms(pieces_of(pairs_ref, n_z, piece)), right_terms(inverse_ref[...]), NT
    )
    high, low = split(cols + unit_rows(place[1], cols.shape))
    rhs[:, :width] = high
    rhs[:, width:] = low
    last = pairs_ref.shape[1] - share
    out_ref[:, piece:, :] = jnp.broadcast_to(
        pairs_ref[0, last:, :][None], (out_ref.shape[0], share, width)
    )
    count = tile // piece
    for k in range(parts):
        loads[k].wait()
        high, low = split(held[k * tile : (k + 1) * tile, :])
        wide = exact_dot(high, rhs[...], NN)
        found = wide[:, :width] + wide[:, width:] + exact_dot(low, rhs[:, :width], NN)
        out_ref[k * count : (k + 1) * count, :piece, :] = found.reshape(count, piece, width)


def partial_sums(place, pairs, inverse, mobility, n_z, piece, share):
    n_rows, n_cols = mobility.shape
    width = pairs.shape[2]
    vmem = pl.BlockSpec(memory_space=pltpu.VMEM)
    return pl.pallas_call(
        lambda *refs: partial_kernel(n_z, piece, share, *refs),
        in_specs=[pl.BlockSpec(memory_space=pltpu.SMEM), vmem, vmem, pl.BlockSpec(memory_space=pl.ANY)],
        out_specs=vmem,
        out_shape=jax.ShapeDtypeStruct((n_rows // piece, piece + share, width), jnp.float32),
        scratch_shapes=[
            pltpu.VMEM((n_cols, 2 * width), jnp.bfloat16),
            pltpu.VMEM(mobility.shape, jnp.float32),
            pltpu.SemaphoreType.DMA((4,)),
        ],
        cost_estimate=pl.CostEstimate(
            flops=6 * n_rows * n_cols * width, bytes_accessed=6_000_000, transcendentals=0
        ),
        compiler_params=pltpu.CompilerParams(vmem_limit_bytes=58 * MIB),
        name="partial_sums",
    )(place, pairs, inverse, mobility)


def image_kernel(piece, got_ref, image_ref, copies_ref, top_ref):
    image = got_ref[0, :piece, :]
    for k in range(1, got_ref.shape[0]):
        image = image + got_ref[k, :piece, :]
    image_ref[...] = image
    copies_ref[...] = jnp.broadcast_to(image[None], copies_ref.shape)
    top_ref[...] = got_ref[:, piece:, :].reshape(top_ref.shape)


def image_piece(got, piece):
    count, _, width = got.shape
    vmem = pl.BlockSpec(memory_space=pltpu.VMEM)
    return pl.pallas_call(
        lambda *refs: image_kernel(piece, *refs),
        in_specs=[vmem],
        out_specs=[vmem] * 3,
        out_shape=(
            jax.ShapeDtypeStruct((piece, width), jnp.float32),
            jax.ShapeDtypeStruct((count, piece, width), jnp.float32),
            jax.ShapeDtypeStruct((width, width), jnp.float32),
        ),
        cost_estimate=pl.CostEstimate(
            flops=10_000_000, bytes_accessed=2_000_000, transcendentals=0
        ),
        compiler_params=pltpu.CompilerParams(vmem_limit_bytes=6 * MIB),
        name="image_piece",
    )(got)


def basis_kernel(n_z, piece, place, rows_ref, pairs_ref, inverse_ref, *outs):
    cols_ref, cols_right, basis_rows, turned_rows = outs
    inverse_terms = right_terms(inverse_ref[...])
    rows = exact_dot(left_terms(rows_ref[...]), inverse_terms, NT)
    rows = rows + unit_rows(place[0], rows_ref.shape)
    basis_rows[...] = rows
    turned_rows[...] = rows.T
    cols = exact_dot(left_terms(pieces_of(pairs_ref, n_z, piece)), inverse_terms, NT)
    cols = cols + unit_rows(place[1], cols.shape)
    cols_ref[...] = cols
    cols_right[...] = right_terms(cols)


def kernel_kernel(inverse_ref, top_ref, rows_ref, cols_ref, *outs):
    cols_left, rows_left, kernel_ref, state_ref = outs
    width = inverse_ref.shape[0]
    identity = eye(width)
    ratio = -product(inverse_ref[...], top_ref[...], NT)
    state_ref[:width, :] = ratio
    state_ref[width:, :] = identity

    def go_on(state):
        return jnp.logical_and(state[0] < 40, state[1] > 1e-10)

    def double(state):
        power = state_ref[:width, :]
        both = product(state_ref[...], power)
        state_ref[:width, :] = both[:width]
        state_ref[width:, :] = state_ref[width:, :] + both[width:]
        return state[0] + 1, jnp.max(jnp.abs(both[:width]))

    lax.while_loop(go_on, double, (0, jnp.max(jnp.abs(ratio))))
    total = state_ref[width:, :]
    kernel = total + product(total, identity - product(identity - ratio, total))
    kernel_ref[...] = kernel
    kernel_terms = right_terms(kernel)
    cols_left[...] = left_terms(exact_dot(left_terms(cols_ref[...]), kernel_terms, NT))
    rows_left[...] = left_terms(exact_dot(left_terms(rows_ref[...]), kernel_terms, NT))


def side_call(kernel, operands, shapes, scratch, name):
    vmem = pl.BlockSpec(memory_space=pltpu.VMEM)
    smem = pl.BlockSpec(memory_space=pltpu.SMEM)
    return pl.pallas_call(
        kernel,
        in_specs=[smem if operand.ndim == 1 else vmem for operand in operands],
        out_specs=[vmem] * len(shapes),
        out_shape=shapes,
        scratch_shapes=scratch,
        cost_estimate=pl.CostEstimate(
            flops=300_000_000, bytes_accessed=10_000_000, transcendentals=0
        ),
        compiler_params=pltpu.CompilerParams(vmem_limit_bytes=58 * MIB),
        name=name,
    )(*operands)


def stream(source_ref, out_ref, held, sems_in, sems_out, prepare, change):
    parts = sems_in.shape[0]
    tile = held.shape[0] // parts
    loads, stores = [], []
    for k in range(parts):
        rows = pl.ds(k * tile, tile)
        loads.append(pltpu.make_async_copy(source_ref.at[rows], held.at[rows], sems_in.at[k]))
        stores.append(pltpu.make_async_copy(held.at[rows], out_ref.at[rows], sems_out.at[k]))
        loads[k].start()
    prepare()
    for k in range(parts):
        loads[k].wait()
        rows = slice(k * tile, (k + 1) * tile)
        held[rows, :] = change(held[rows, :], rows)
        stores[k].start()
    for k in range(parts):
        stores[k].wait()


def first_update_kernel(image_ref, kernel_ref, cols_ref, mob_ref, out_ref, lhs, held, *sems):
    def prepare():
        lhs[...] = left_terms(product(image_ref[...], kernel_ref[...]))

    def change(value, rows):
        return value - exact_dot(lhs[rows, :], cols_ref[...], NT)

    stream(mob_ref, out_ref, held, *sems, prepare, change)


def update_call(kernel, inputs, matrix, terms, name):
    n_rows, n_cols = matrix.shape
    vmem = pl.BlockSpec(memory_space=pltpu.VMEM)
    hbm = pl.BlockSpec(memory_space=pl.ANY)
    return pl.pallas_call(
        kernel,
        in_specs=[vmem] * len(inputs) + [hbm],
        out_specs=hbm,
        out_shape=jax.ShapeDtypeStruct(matrix.shape, jnp.float32),
        scratch_shapes=[
            pltpu.VMEM((n_rows, terms), jnp.bfloat16),
            pltpu.VMEM(matrix.shape, jnp.float32),
            pltpu.SemaphoreType.DMA((4,)),
            pltpu.SemaphoreType.DMA((4,)),
        ],
        cost_estimate=pl.CostEstimate(
            flops=2 * n_rows * n_cols * terms, bytes_accessed=9_000_000, transcendentals=0
        ),
        compiler_params=pltpu.CompilerParams(vmem_limit_bytes=58 * MIB),
        name=name,
    )(*inputs, matrix)


def last_update_kernel(n_z, piece, pairs_ref, cols_ref, turned_ref, half_ref, out_ref, rhs, held, *sems):
    def prepare():
        small = unpack(pairs_ref[:, n_z * piece :, :])
        change_cols = exact_dot(cols_ref[...], right_terms(small), NT)
        rhs[...] = right_terms(pieces_of(pairs_ref, n_z, piece) - change_cols)

    def change(value, rows):
        return value - exact_dot(turned_ref[rows, :], rhs[...], NT)

    stream(half_ref, out_ref, held, *sems, prepare, change)


def on_device(panel, mobility):
    piece, width = panel.shape
    n_row, n_col = lax.axis_size("row"), lax.axis_size("col")
    block_rows, block_cols = mobility.shape
    row, col = lax.axis_index("row"), lax.axis_index("col")
    place = jnp.stack([row, col]).astype(jnp.int32)
    n_z = n_row // 2
    share = width // n_col
    z_groups = [[2 * z + h for z in range(n_z)] for h in range(2)]
    pairs = [[2 * z, 2 * z + 1] for z in range(n_z)]
    transposing = [(i * n_col + j, j * n_col + i) for i in range(n_row) for j in range(n_col)]
    swap = [(i, i ^ 1) for i in range(n_row)]

    def copies(rows, count):
        return jnp.broadcast_to(rows[None], (count,) + rows.shape)

    def gather_row(lone, keep, give, extra):
        summed = keep + lax.ppermute(give, "row", swap)
        sent = copies(jnp.concatenate([lone, summed] + extra, 0), n_z)
        parts = lax.all_to_all(sent, "row", 0, 0, axis_index_groups=z_groups)
        lone = parts[:, :piece].reshape(n_z * piece, width)
        packed = summed.shape[0]
        summed = jnp.sum(parts[:, piece : piece + packed], 0)
        extra = [parts[0, piece + packed :]] if extra else []
        sent = jnp.concatenate([lone, summed] + extra, 0)
        return lax.all_gather(sent, "row", axis=0, axis_index_groups=pairs)

    turned_panel = lax.ppermute(panel, BOTH, transposing)
    panel_rows = lax.all_to_all(copies(panel, n_col), "col", 0, 0).reshape(block_rows, width)
    panel_rows, turned_panel = lax.optimization_barrier((panel_rows, turned_panel))
    keep, give, top_part = packed_parts(
        gram_kernel, place, (panel_rows,), [(share, width)], "gram_parts"
    )
    panel_pairs = gather_row(turned_panel, keep, give, [top_part])

    start = n_z * piece
    panel_factor, inverse = factor(panel_pairs[:, start : start + keep.shape[0]])
    sent = partial_sums(place, panel_pairs, inverse, mobility, n_z, piece, share)
    got = lax.all_to_all(sent, "col", 0, 0)
    long = jax.ShapeDtypeStruct((block_rows, width), jnp.float32)
    wide = jax.ShapeDtypeStruct((block_rows, 3 * width), jnp.bfloat16)
    tall = jax.ShapeDtypeStruct((width, block_rows), jnp.float32)
    square = jax.ShapeDtypeStruct((width, width), jnp.float32)
    basis_cols, cols_right, basis_rows, turned_rows = side_call(
        lambda *refs: basis_kernel(n_z, piece, *refs),
        (place, panel_rows, panel_pairs, inverse),
        [long, wide, long, tall],
        [],
        "bases",
    )
    got, turned_rows = lax.optimization_barrier((got, turned_rows))
    image, image_copies, top_rows = image_piece(got, piece)
    turned_image = lax.ppermute(image, BOTH, transposing)
    image_rows = lax.all_to_all(image_copies, "col", 0, 0).reshape(block_rows, width)
    cols_left, turned, kernel = side_call(
        kernel_kernel,
        (inverse, top_rows, basis_rows, basis_cols),
        [wide, wide, square],
        [pltpu.VMEM((2 * width, width), jnp.float32)],
        "kernel",
    )
    image_rows, turned_image = lax.optimization_barrier((image_rows, turned_image))
    keep, give = packed_parts(inner_kernel, place, (turned_rows, image_rows), [], "inner_parts")
    image_pairs = gather_row(turned_image, keep, give, [])
    terms = 3 * width
    halfway = update_call(
        first_update_kernel, (image_rows, kernel, cols_right), mobility, terms, "first_update"
    )
    updated = update_call(
        lambda *refs: last_update_kernel(n_z, piece, *refs),
        (image_pairs, cols_left, turned),
        halfway,
        terms,
        "last_update",
    )
    return (updated, panel_factor)


def solution(mesh):
    in_specs = (P(("row", "col"), None), P("row", "col"))
    out_specs = (P("row", "col"), P())
    return jax.shard_map(
        on_device, mesh=mesh, in_specs=in_specs, out_specs=out_specs, check_vma=False
    )
```

```python
import jax
import jax.numpy as jnp
from jax import lax
from jax.experimental import pallas as pl
from jax.experimental.pallas import tpu as pltpu
from jax.sharding import PartitionSpec as P

BOTH = ("row", "col")
STEP = 8
MIB = 1 << 20
NN = (((1,), (0,)), ((), ()))
TN = (((0,), (0,)), ((), ()))
NT = (((1,), (1,)), ((), ()))


def product(first_op, second_op, dims=NN):
    return lax.dot_general(
        first_op,
        second_op,
        dims,
        precision=lax.Precision.HIGHEST,
        preferred_element_type=jnp.float32,
    )


def split(value):
    high = value.astype(jnp.bfloat16)
    return high, (value - high.astype(jnp.float32)).astype(jnp.bfloat16)


def left_terms(value):
    high, low = split(value)
    return jnp.concatenate([high, low, high], 1)


def right_terms(value):
    high, low = split(value)
    return jnp.concatenate([high, high, low], 1)


def exact_dot(first_op, second_op, dims):
    return lax.dot_general(first_op, second_op, dims, preferred_element_type=jnp.float32)


def unit_rows(index, shape):
    rows = lax.broadcasted_iota(jnp.int32, shape, 0) + index * shape[0]
    return jnp.where(rows == lax.broadcasted_iota(jnp.int32, shape, 1), 1.0, 0.0)


def eye(width):
    return unit_rows(0, (width, width))


def pieces_of(pairs_ref, n_z, piece):
    return jnp.concatenate(
        [pairs_ref[h, z * piece : (z + 1) * piece, :] for z in range(n_z) for h in range(2)], 0
    )


def pack(value, keep_ref, give_ref):
    side = value.shape[0] // 2
    half = side // 2
    top = value[:side]
    low = pltpu.roll(value[side:], side, 1)
    row = lax.broadcasted_iota(jnp.int32, top.shape, 0)
    lane = lax.broadcasted_iota(jnp.int32, top.shape, 1)
    rows = jnp.where(jnp.logical_and(row < lane, lane < side), low, top)
    last = jnp.sum(jnp.where(row == lane, low, 0.0), axis=0, keepdims=True)
    even = lax.rem(lax.axis_index("row"), 2) == 0
    keep_ref[:half, :] = jnp.where(even, rows[:half], rows[half:])
    give_ref[:half, :] = jnp.where(even, rows[half:], rows[:half])
    keep_ref[half:, :] = jnp.broadcast_to(last, (STEP, last.shape[1]))
    give_ref[half:, :] = jnp.broadcast_to(last, (STEP, last.shape[1]))


def unpack(packed):
    half = packed.shape[1] - STEP
    side = 2 * half
    rows = packed[:, :half, :].reshape(side, packed.shape[2])
    turned = rows.T
    row = lax.broadcasted_iota(jnp.int32, (side, side), 0)
    lane = lax.broadcasted_iota(jnp.int32, (side, side), 1)
    left, across = rows[:, :side], turned[:side]
    last = packed[0, half : half + 1, :side]
    a = jnp.where(row >= lane, left, across)
    d = jnp.where(row == lane, last, jnp.where(row < lane, left, across))
    return jnp.concatenate(
        [
            jnp.concatenate([a, rows[:, side:]], 1),
            jnp.concatenate([turned[side:], d], 1),
        ],
        0,
    )


def gram_kernel(rows_ref, keep_ref, give_ref, top_ref):
    share = top_ref.shape[0]
    rows = rows_ref[...]
    pack(product(rows, rows, TN), keep_ref, give_ref)
    start = pl.multiple_of(lax.axis_index("col") * share, share)
    top_ref[...] = rows_ref[pl.ds(start, share), :]


def inner_kernel(turned_ref, rows_ref, keep_ref, give_ref):
    terms = product(turned_ref[...], rows_ref[...])
    pack(0.5 * (terms + terms.T), keep_ref, give_ref)


def packed_parts(kernel, operands, extra, name):
    width = operands[-1].shape[1]
    vmem = pl.BlockSpec(memory_space=pltpu.VMEM)
    shapes = [(width // 4 + STEP, width)] * 2 + extra
    return pl.pallas_call(
        kernel,
        in_specs=[vmem] * len(operands),
        out_specs=[vmem] * len(shapes),
        out_shape=[jax.ShapeDtypeStruct(shape, jnp.float32) for shape in shapes],
        cost_estimate=pl.CostEstimate(
            flops=200_000_000, bytes_accessed=3_000_000, transcendentals=0
        ),
        compiler_params=pltpu.CompilerParams(vmem_limit_bytes=8 * MIB),
        name=name,
    )(*operands)


def factor_kernel(gram_ref, upper_ref, inverse_ref, work, other):
    width = upper_ref.shape[0]
    full = (STEP, width)
    lane = lax.broadcasted_iota(jnp.int32, full, 1)
    work[...] = unpack(gram_ref[...])
    other[...] = eye(width)
    for first in range(0, width, STEP):
        a_rows = [jnp.broadcast_to(work[first + k : first + k + 1, :], full) for k in range(STEP)]
        x_rows = [jnp.broadcast_to(other[first + k : first + k + 1, :], full) for k in range(STEP)]
        entry, mult, inv = {}, {}, {}
        for i in range(STEP):
            for k in range(i + 1):
                column = a_rows[i][:, first + k : first + k + 1]
                entry[i, k] = jnp.broadcast_to(column, full)
        for k in range(STEP):
            inv[k] = 1.0 / entry[k, k]
            for i in range(k + 1, STEP):
                mult[i, k] = entry[i, k] * inv[k]
            for i in range(k + 1, STEP):
                for l in range(k + 1, i + 1):
                    entry[i, l] = entry[i, l] - mult[i, k] * entry[l, k]
        for i in range(STEP):
            for k in range(i):
                a_rows[i] = a_rows[i] - mult[i, k] * a_rows[k]
                x_rows[i] = x_rows[i] - mult[i, k] * x_rows[k]
        for k in range(STEP):
            root = lax.rsqrt(entry[k, k])
            root = root * (1.5 - 0.5 * entry[k, k] * root * root)
            row = slice(first + k, first + k + 1)
            upper_ref[row, :] = jnp.where(lane >= first + k, a_rows[k] * root, 0.0)[:1]
            inverse_ref[row, :] = (x_rows[k] * root)[:1]
        if first + STEP == width:
            break
        a_back = [a_rows[k] * inv[k] for k in range(STEP)]
        x_back = [x_rows[k] * inv[k] for k in range(STEP)]
        for k in range(STEP - 2, -1, -1):
            for l in range(k + 1, STEP):
                a_back[k] = a_back[k] - mult[l, k] * a_back[l]
                x_back[k] = x_back[k] - mult[l, k] * x_back[l]
        for g in range(first + STEP, width, STEP):
            block = work[g : g + STEP, :]
            a_new, x_new = block, other[g : g + STEP, :]
            for k in range(STEP):
                column = jnp.broadcast_to(block[:, first + k : first + k + 1], full)
                a_new = a_new - column * a_back[k]
                x_new = x_new - column * x_back[k]
            work[g : g + STEP, :] = a_new
            other[g : g + STEP, :] = x_new


def factor(packed):
    width = packed.shape[2]
    shape = jax.ShapeDtypeStruct((width, width), jnp.float32)
    vmem = pl.BlockSpec(memory_space=pltpu.VMEM)
    return pl.pallas_call(
        factor_kernel,
        in_specs=[vmem],
        out_specs=[vmem] * 2,
        out_shape=(shape, shape),
        scratch_shapes=[pltpu.VMEM((width, width), jnp.float32)] * 2,
        cost_estimate=pl.CostEstimate(
            flops=400_000_000, bytes_accessed=200_000, transcendentals=0
        ),
        compiler_params=pltpu.CompilerParams(vmem_limit_bytes=4 * MIB),
        name="factor",
    )(packed)


def partial_kernel(n_z, piece, share, pairs_ref, inverse_ref, mob_ref, out_ref, rhs):
    width = pairs_ref.shape[2]
    n_rows = mob_ref.shape[0]
    tile = 256
    cols = exact_dot(
        left_terms(pieces_of(pairs_ref, n_z, piece)), right_terms(inverse_ref[...]), NT
    )
    high, low = split(cols + unit_rows(lax.axis_index("col"), cols.shape))
    rhs[:, :width] = high
    rhs[:, width:] = low
    last = pairs_ref.shape[1] - share
    out_ref[:, piece:, :] = jnp.broadcast_to(
        pairs_ref[0, last:, :][None], (out_ref.shape[0], share, width)
    )
    count = tile // piece
    for k in range(n_rows // tile):
        high, low = split(mob_ref[k * tile : (k + 1) * tile, :])
        wide = exact_dot(high, rhs[...], NN)
        found = wide[:, :width] + wide[:, width:] + exact_dot(low, rhs[:, :width], NN)
        out_ref[k * count : (k + 1) * count, :piece, :] = found.reshape(count, piece, width)


def partial_sums(pairs, inverse, mobility, n_z, piece, share):
    n_rows, n_cols = mobility.shape
    width = pairs.shape[2]
    vmem = pl.BlockSpec(memory_space=pltpu.VMEM)
    return pl.pallas_call(
        lambda *refs: partial_kernel(n_z, piece, share, *refs),
        in_specs=[vmem] * 3,
        out_specs=vmem,
        out_shape=jax.ShapeDtypeStruct((n_rows // piece, piece + share, width), jnp.float32),
        scratch_shapes=[pltpu.VMEM((n_cols, 2 * width), jnp.bfloat16)],
        cost_estimate=pl.CostEstimate(
            flops=6 * n_rows * n_cols * width, bytes_accessed=6_000_000, transcendentals=0
        ),
        compiler_params=pltpu.CompilerParams(vmem_limit_bytes=14 * MIB),
        name="partial_sums",
    )(pairs, inverse, mobility)


def image_kernel(piece, got_ref, image_ref, copies_ref, top_ref):
    image = got_ref[0, :piece, :]
    for k in range(1, got_ref.shape[0]):
        image = image + got_ref[k, :piece, :]
    image_ref[...] = image
    copies_ref[...] = jnp.broadcast_to(image[None], copies_ref.shape)
    top_ref[...] = got_ref[:, piece:, :].reshape(top_ref.shape)


def image_piece(got, piece):
    count, _, width = got.shape
    vmem = pl.BlockSpec(memory_space=pltpu.VMEM)
    return pl.pallas_call(
        lambda *refs: image_kernel(piece, *refs),
        in_specs=[vmem],
        out_specs=[vmem] * 3,
        out_shape=(
            jax.ShapeDtypeStruct((piece, width), jnp.float32),
            jax.ShapeDtypeStruct((count, piece, width), jnp.float32),
            jax.ShapeDtypeStruct((width, width), jnp.float32),
        ),
        cost_estimate=pl.CostEstimate(
            flops=10_000_000, bytes_accessed=2_000_000, transcendentals=0
        ),
        compiler_params=pltpu.CompilerParams(vmem_limit_bytes=6 * MIB),
        name="image_piece",
    )(got)


def rows_kernel(rows_ref, inverse_ref, turned_ref):
    rows = exact_dot(left_terms(rows_ref[...]), right_terms(inverse_ref[...]), NT)
    turned_ref[...] = (rows + unit_rows(lax.axis_index("row"), rows.shape)).T


def kernel_kernel(n_z, piece, inverse_ref, top_ref, turned_ref, pairs_ref, *outs):
    cols_left, cols_right, rows_left, kernel_ref, state_ref = outs
    width = inverse_ref.shape[0]
    identity = eye(width)
    ratio = -product(inverse_ref[...], top_ref[...], NT)
    state_ref[:width, :] = ratio
    state_ref[width:, :] = identity

    def go_on(state):
        return jnp.logical_and(state[0] < 40, state[1] > 1e-10)

    def double(state):
        power = state_ref[:width, :]
        both = product(state_ref[...], power)
        state_ref[:width, :] = both[:width]
        state_ref[width:, :] = state_ref[width:, :] + both[width:]
        return state[0] + 1, jnp.max(jnp.abs(both[:width]))

    lax.while_loop(go_on, double, (0, jnp.max(jnp.abs(ratio))))
    total = state_ref[width:, :]
    kernel = total + product(total, identity - product(identity - ratio, total))
    kernel_ref[...] = kernel
    kernel_terms = right_terms(kernel)
    cols = exact_dot(
        left_terms(pieces_of(pairs_ref, n_z, piece)), right_terms(inverse_ref[...]), NT
    )
    cols = cols + unit_rows(lax.axis_index("col"), cols.shape)
    cols_right[...] = right_terms(cols)
    cols_left[...] = left_terms(exact_dot(left_terms(cols), kernel_terms, NT))
    rows_left[...] = left_terms(exact_dot(left_terms(turned_ref[...].T), kernel_terms, NT))


def side_call(kernel, operands, shapes, scratch, name):
    vmem = pl.BlockSpec(memory_space=pltpu.VMEM)
    return pl.pallas_call(
        kernel,
        in_specs=[vmem] * len(operands),
        out_specs=[vmem] * len(shapes),
        out_shape=shapes,
        scratch_shapes=scratch,
        cost_estimate=pl.CostEstimate(
            flops=300_000_000, bytes_accessed=10_000_000, transcendentals=0
        ),
        compiler_params=pltpu.CompilerParams(vmem_limit_bytes=14 * MIB),
        name=name,
    )(*operands)


def stream(source_ref, out_ref, held, sems_in, sems_out, prepare, change):
    parts = sems_in.shape[0]
    tile = held.shape[0] // parts
    loads, stores = [], []
    for k in range(parts):
        rows = pl.ds(k * tile, tile)
        loads.append(pltpu.make_async_copy(source_ref.at[rows], held.at[rows], sems_in.at[k]))
        stores.append(pltpu.make_async_copy(held.at[rows], out_ref.at[rows], sems_out.at[k]))
        loads[k].start()
    prepare()
    for k in range(parts):
        loads[k].wait()
        rows = slice(k * tile, (k + 1) * tile)
        held[rows, :] = change(held[rows, :], rows)
        stores[k].start()
    for k in range(parts):
        stores[k].wait()


def first_update_kernel(image_ref, kernel_ref, cols_ref, mob_ref, out_ref, lhs, held, *sems):
    def prepare():
        lhs[...] = left_terms(product(image_ref[...], kernel_ref[...]))

    def change(value, rows):
        return value - exact_dot(lhs[rows, :], cols_ref[...], NT)

    stream(mob_ref, out_ref, held, *sems, prepare, change)


def update_call(kernel, inputs, matrix, terms, name):
    n_rows, n_cols = matrix.shape
    vmem = pl.BlockSpec(memory_space=pltpu.VMEM)
    hbm = pl.BlockSpec(memory_space=pltpu.HBM)
    matrix = pltpu.with_memory_space_constraint(matrix, pltpu.HBM)
    return pl.pallas_call(
        kernel,
        in_specs=[vmem] * len(inputs) + [hbm],
        out_specs=hbm,
        out_shape=pltpu.HBM(matrix.shape, jnp.float32),
        scratch_shapes=[
            pltpu.VMEM((n_rows, terms), jnp.bfloat16),
            pltpu.VMEM(matrix.shape, jnp.float32),
            pltpu.SemaphoreType.DMA((4,)),
            pltpu.SemaphoreType.DMA((4,)),
        ],
        cost_estimate=pl.CostEstimate(
            flops=2 * n_rows * n_cols * terms, bytes_accessed=9_000_000, transcendentals=0
        ),
        compiler_params=pltpu.CompilerParams(vmem_limit_bytes=14 * MIB),
        name=name,
    )(*inputs, matrix)


def last_update_kernel(n_z, piece, pairs_ref, cols_ref, turned_ref, half_ref, out_ref, rhs, held, *sems):
    def prepare():
        small = unpack(pairs_ref[:, n_z * piece :, :])
        change_cols = exact_dot(cols_ref[...], right_terms(small), NT)
        rhs[...] = right_terms(pieces_of(pairs_ref, n_z, piece) - change_cols)

    def change(value, rows):
        return value - exact_dot(turned_ref[rows, :], rhs[...], NT)

    stream(half_ref, out_ref, held, *sems, prepare, change)


def on_device(panel, mobility):
    piece, width = panel.shape
    n_row, n_col = lax.axis_size("row"), lax.axis_size("col")
    block_rows, block_cols = mobility.shape
    n_z = n_row // 2
    share = width // n_col
    z_groups = [[2 * z + h for z in range(n_z)] for h in range(2)]
    pairs = [[2 * z, 2 * z + 1] for z in range(n_z)]
    transposing = [(i * n_col + j, j * n_col + i) for i in range(n_row) for j in range(n_col)]
    swap = [(i, i ^ 1) for i in range(n_row)]

    def copies(rows, count):
        return jnp.broadcast_to(rows[None], (count,) + rows.shape)

    def gather_row(lone, keep, give, extra):
        summed = keep + lax.ppermute(give, "row", swap)
        sent = copies(jnp.concatenate([lone, summed] + extra, 0), n_z)
        parts = lax.all_to_all(sent, "row", 0, 0, axis_index_groups=z_groups)
        lone = parts[:, :piece].reshape(n_z * piece, width)
        packed = summed.shape[0]
        summed = jnp.sum(parts[:, piece : piece + packed], 0)
        extra = [parts[0, piece + packed :]] if extra else []
        sent = jnp.concatenate([lone, summed] + extra, 0)
        return lax.all_gather(sent, "row", axis=0, axis_index_groups=pairs)

    turned_panel = lax.ppermute(panel, BOTH, transposing)
    panel_rows = lax.all_to_all(copies(panel, n_col), "col", 0, 0).reshape(block_rows, width)
    panel_rows, turned_panel = lax.optimization_barrier((panel_rows, turned_panel))
    keep, give, top_part = packed_parts(
        gram_kernel, (panel_rows,), [(share, width)], "gram_parts"
    )
    panel_pairs = gather_row(turned_panel, keep, give, [top_part])

    start = n_z * piece
    panel_factor, inverse = factor(panel_pairs[:, start : start + keep.shape[0]])
    sent = partial_sums(panel_pairs, inverse, mobility, n_z, piece, share)
    got = lax.all_to_all(sent, "col", 0, 0)
    wide = jax.ShapeDtypeStruct((block_rows, 3 * width), jnp.bfloat16)
    tall = jax.ShapeDtypeStruct((width, block_rows), jnp.float32)
    square = jax.ShapeDtypeStruct((width, width), jnp.float32)
    (turned_rows,) = side_call(rows_kernel, (panel_rows, inverse), [tall], [], "basis_rows")
    got, turned_rows = lax.optimization_barrier((got, turned_rows))
    image, image_copies, top_rows = image_piece(got, piece)
    turned_image = lax.ppermute(image, BOTH, transposing)
    image_rows = lax.all_to_all(image_copies, "col", 0, 0).reshape(block_rows, width)
    cols_left, cols_right, rows_left, kernel = side_call(
        lambda *refs: kernel_kernel(n_z, piece, *refs),
        (inverse, top_rows, turned_rows, panel_pairs),
        [wide, wide, wide, square],
        [pltpu.VMEM((2 * width, width), jnp.float32)],
        "kernel",
    )
    image_rows, turned_image = lax.optimization_barrier((image_rows, turned_image))
    keep, give = packed_parts(inner_kernel, (turned_rows, image_rows), [], "inner_parts")
    image_pairs = gather_row(turned_image, keep, give, [])
    terms = 3 * width
    halfway = update_call(
        first_update_kernel, (image_rows, kernel, cols_right), mobility, terms, "first_update"
    )
    updated = update_call(
        lambda *refs: last_update_kernel(n_z, piece, *refs),
        (image_pairs, cols_left, rows_left),
        halfway,
        terms,
        "last_update",
    )
    return (updated, panel_factor)


def solution(mesh):
    in_specs = (P(("row", "col"), None), P("row", "col"))
    out_specs = (P("row", "col"), P())
    return jax.shard_map(
        on_device, mesh=mesh, in_specs=in_specs, out_specs=out_specs, check_vma=False
    )
```

```python
import jax
import jax.numpy as jnp
from jax import lax
from jax.experimental import pallas as pl
from jax.experimental.pallas import tpu as pltpu
from jax.sharding import PartitionSpec as P

BOTH = ("row", "col")
STEP = 8
MIB = 1 << 20
NN = (((1,), (0,)), ((), ()))
TN = (((0,), (0,)), ((), ()))
NT = (((1,), (1,)), ((), ()))


def product(first_op, second_op, dims=NN):
    return lax.dot_general(
        first_op,
        second_op,
        dims,
        precision=lax.Precision.HIGHEST,
        preferred_element_type=jnp.float32,
    )


def split(value):
    high = value.astype(jnp.bfloat16)
    return high, (value - high.astype(jnp.float32)).astype(jnp.bfloat16)


def both_terms(value):
    return jnp.concatenate(split(value), 1)


def left_terms(value):
    high, low = split(value)
    return jnp.concatenate([high, low, high], 1)


def right_terms(value):
    high, low = split(value)
    return jnp.concatenate([high, high, low], 1)


def to_left(pair):
    return jnp.concatenate([pair, pair[:, : pair.shape[1] // 2]], 1)


def to_right(pair):
    return jnp.concatenate([pair[:, : pair.shape[1] // 2], pair], 1)


def exact_dot(first_op, second_op, dims):
    return lax.dot_general(first_op, second_op, dims, preferred_element_type=jnp.float32)


def unit_rows(index, shape):
    rows = lax.broadcasted_iota(jnp.int32, shape, 0) + index * shape[0]
    return jnp.where(rows == lax.broadcasted_iota(jnp.int32, shape, 1), 1.0, 0.0)


def eye(width):
    return unit_rows(0, (width, width))


def pieces_of(parts_ref, piece):
    count, _, width = parts_ref.shape
    return parts_ref[:, :piece, :].reshape(count * piece, width)


def pack(value, keep_ref, give_ref):
    side = value.shape[0] // 2
    half = side // 2
    top = value[:side]
    low = pltpu.roll(value[side:], side, 1)
    row = lax.broadcasted_iota(jnp.int32, top.shape, 0)
    lane = lax.broadcasted_iota(jnp.int32, top.shape, 1)
    rows = jnp.where(jnp.logical_and(row < lane, lane < side), low, top)
    last = jnp.sum(jnp.where(row == lane, low, 0.0), axis=0, keepdims=True)
    even = lax.rem(lax.axis_index("row"), 2) == 0
    keep_ref[:half, :] = jnp.where(even, rows[:half], rows[half:])
    give_ref[:half, :] = jnp.where(even, rows[half:], rows[:half])
    keep_ref[half:, :] = jnp.broadcast_to(last, (STEP, last.shape[1]))
    give_ref[half:, :] = jnp.broadcast_to(last, (STEP, last.shape[1]))


def unpack(parts_ref, piece):
    width = parts_ref.shape[2]
    half = width // 4
    stop = piece + half + STEP
    sums = [parts_ref[h, piece:stop, :] for h in range(2)]
    for i in range(2, parts_ref.shape[0]):
        sums[i % 2] = sums[i % 2] + parts_ref[i, piece:stop, :]
    side = 2 * half
    rows = jnp.concatenate([sums[0][:half], sums[1][:half]], 0)
    turned = rows.T
    row = lax.broadcasted_iota(jnp.int32, (side, side), 0)
    lane = lax.broadcasted_iota(jnp.int32, (side, side), 1)
    left, across = rows[:, :side], turned[:side]
    last = sums[0][half : half + 1, :side]
    a = jnp.where(row >= lane, left, across)
    d = jnp.where(row == lane, last, jnp.where(row < lane, left, across))
    return jnp.concatenate(
        [
            jnp.concatenate([a, rows[:, side:]], 1),
            jnp.concatenate([turned[side:], d], 1),
        ],
        0,
    )


def gram_kernel(rows_ref, keep_ref, give_ref, top_ref):
    share = top_ref.shape[0]
    rows = rows_ref[...]
    pack(product(rows, rows, TN), keep_ref, give_ref)
    start = pl.multiple_of(lax.axis_index("col") * share, share)
    top_ref[...] = rows_ref[pl.ds(start, share), :]


def inner_kernel(turned_ref, rows_ref, keep_ref, give_ref):
    terms = product(turned_ref[...], rows_ref[...])
    pack(0.5 * (terms + terms.T), keep_ref, give_ref)


def packed_parts(kernel, operands, extra, name):
    width = operands[-1].shape[1]
    vmem = pl.BlockSpec(memory_space=pltpu.VMEM)
    shapes = [(width // 4 + STEP, width)] * 2 + extra
    return pl.pallas_call(
        kernel,
        in_specs=[vmem] * len(operands),
        out_specs=[vmem] * len(shapes),
        out_shape=[jax.ShapeDtypeStruct(shape, jnp.float32) for shape in shapes],
        cost_estimate=pl.CostEstimate(
            flops=200_000_000, bytes_accessed=3_000_000, transcendentals=0
        ),
        compiler_params=pltpu.CompilerParams(vmem_limit_bytes=8 * MIB),
        name=name,
    )(*operands)


def factor_kernel(piece, parts_ref, upper_ref, inverse_ref, work, other):
    width = upper_ref.shape[0]
    full = (STEP, width)
    lane = lax.broadcasted_iota(jnp.int32, full, 1)
    work[...] = unpack(parts_ref, piece)
    other[...] = eye(width)
    for first in range(0, width, STEP):
        a_rows = [jnp.broadcast_to(work[first + k : first + k + 1, :], full) for k in range(STEP)]
        x_rows = [jnp.broadcast_to(other[first + k : first + k + 1, :], full) for k in range(STEP)]
        entry, mult, inv = {}, {}, {}
        for i in range(STEP):
            for k in range(i + 1):
                column = a_rows[i][:, first + k : first + k + 1]
                entry[i, k] = jnp.broadcast_to(column, full)
        for k in range(STEP):
            inv[k] = 1.0 / entry[k, k]
            for i in range(k + 1, STEP):
                mult[i, k] = entry[i, k] * inv[k]
            for i in range(k + 1, STEP):
                for l in range(k + 1, i + 1):
                    entry[i, l] = entry[i, l] - mult[i, k] * entry[l, k]
        for i in range(STEP):
            for k in range(i):
                a_rows[i] = a_rows[i] - mult[i, k] * a_rows[k]
                x_rows[i] = x_rows[i] - mult[i, k] * x_rows[k]
        for k in range(STEP):
            root = lax.rsqrt(entry[k, k])
            root = root * (1.5 - 0.5 * entry[k, k] * root * root)
            row = slice(first + k, first + k + 1)
            upper_ref[row, :] = jnp.where(lane >= first + k, a_rows[k] * root, 0.0)[:1]
            inverse_ref[row, :] = (x_rows[k] * root)[:1]
        if first + STEP == width:
            break
        a_back = [a_rows[k] * inv[k] for k in range(STEP)]
        x_back = [x_rows[k] * inv[k] for k in range(STEP)]
        for k in range(STEP - 2, -1, -1):
            for l in range(k + 1, STEP):
                a_back[k] = a_back[k] - mult[l, k] * a_back[l]
                x_back[k] = x_back[k] - mult[l, k] * x_back[l]
        for g in range(first + STEP, width, STEP):
            block = work[g : g + STEP, :]
            a_new, x_new = block, other[g : g + STEP, :]
            for k in range(STEP):
                column = jnp.broadcast_to(block[:, first + k : first + k + 1], full)
                a_new = a_new - column * a_back[k]
                x_new = x_new - column * x_back[k]
            work[g : g + STEP, :] = a_new
            other[g : g + STEP, :] = x_new


def factor(parts, piece):
    width = parts.shape[2]
    shape = jax.ShapeDtypeStruct((width, width), jnp.float32)
    vmem = pl.BlockSpec(memory_space=pltpu.VMEM)
    return pl.pallas_call(
        lambda *refs: factor_kernel(piece, *refs),
        in_specs=[vmem],
        out_specs=[vmem] * 2,
        out_shape=(shape, shape),
        scratch_shapes=[pltpu.VMEM((width, width), jnp.float32)] * 2,
        cost_estimate=pl.CostEstimate(
            flops=400_000_000, bytes_accessed=200_000, transcendentals=0
        ),
        compiler_params=pltpu.CompilerParams(vmem_limit_bytes=4 * MIB),
        name="factor",
    )(parts)


def partial_kernel(piece, share, parts_ref, inverse_ref, mob_ref, out_ref, rhs):
    width = parts_ref.shape[2]
    n_rows = mob_ref.shape[0]
    tile = 256
    cols = exact_dot(
        left_terms(pieces_of(parts_ref, piece)), right_terms(inverse_ref[...]), NT
    )
    high, low = split(cols + unit_rows(lax.axis_index("col"), cols.shape))
    rhs[:, :width] = high
    rhs[:, width:] = low
    last = parts_ref.shape[1] - share
    out_ref[:, piece:, :] = jnp.broadcast_to(
        parts_ref[0, last:, :][None], (out_ref.shape[0], share, width)
    )
    count = tile // piece
    for k in range(n_rows // tile):
        high, low = split(mob_ref[k * tile : (k + 1) * tile, :])
        wide = exact_dot(high, rhs[...], NN)
        found = wide[:, :width] + wide[:, width:] + exact_dot(low, rhs[:, :width], NN)
        out_ref[k * count : (k + 1) * count, :piece, :] = found.reshape(count, piece, width)


def partial_sums(parts, inverse, mobility, piece, share):
    n_rows, n_cols = mobility.shape
    width = parts.shape[2]
    vmem = pl.BlockSpec(memory_space=pltpu.VMEM)
    return pl.pallas_call(
        lambda *refs: partial_kernel(piece, share, *refs),
        in_specs=[vmem] * 3,
        out_specs=vmem,
        out_shape=jax.ShapeDtypeStruct((n_rows // piece, piece + share, width), jnp.float32),
        scratch_shapes=[pltpu.VMEM((n_cols, 2 * width), jnp.bfloat16)],
        cost_estimate=pl.CostEstimate(
            flops=6 * n_rows * n_cols * width, bytes_accessed=6_000_000, transcendentals=0
        ),
        compiler_params=pltpu.CompilerParams(vmem_limit_bytes=14 * MIB),
        name="partial_sums",
    )(parts, inverse, mobility)


def image_kernel(piece, got_ref, image_ref, copies_ref, top_ref):
    image = got_ref[0, :piece, :]
    for k in range(1, got_ref.shape[0]):
        image = image + got_ref[k, :piece, :]
    image_ref[...] = image
    copies_ref[...] = jnp.broadcast_to(image[None], copies_ref.shape)
    top_ref[...] = got_ref[:, piece:, :].reshape(top_ref.shape)


def image_piece(got, piece):
    count, _, width = got.shape
    vmem = pl.BlockSpec(memory_space=pltpu.VMEM)
    return pl.pallas_call(
        lambda *refs: image_kernel(piece, *refs),
        in_specs=[vmem],
        out_specs=[vmem] * 3,
        out_shape=(
            jax.ShapeDtypeStruct((piece, width), jnp.float32),
            jax.ShapeDtypeStruct((count, piece, width), jnp.float32),
            jax.ShapeDtypeStruct((width, width), jnp.float32),
        ),
        cost_estimate=pl.CostEstimate(
            flops=10_000_000, bytes_accessed=2_000_000, transcendentals=0
        ),
        compiler_params=pltpu.CompilerParams(vmem_limit_bytes=6 * MIB),
        name="image_piece",
    )(got)


def rows_kernel(rows_ref, inverse_ref, turned_ref):
    rows = exact_dot(left_terms(rows_ref[...]), right_terms(inverse_ref[...]), NT)
    turned_ref[...] = (rows + unit_rows(lax.axis_index("row"), rows.shape)).T


def kernel_kernel(piece, inverse_ref, top_ref, turned_ref, parts_ref, *outs):
    cols_out, rows_left, kernel_ref, state_ref = outs
    width = inverse_ref.shape[0]
    identity = eye(width)
    ratio = -product(inverse_ref[...], top_ref[...], NT)
    state_ref[:width, :] = ratio
    state_ref[width:, :] = identity

    def go_on(state):
        return jnp.logical_and(state[0] < 40, state[1] > 1e-10)

    def double(state):
        power = state_ref[:width, :]
        both = product(state_ref[...], power)
        state_ref[:width, :] = both[:width]
        state_ref[width:, :] = state_ref[width:, :] + both[width:]
        return state[0] + 1, jnp.max(jnp.abs(both[:width]))

    lax.while_loop(go_on, double, (0, jnp.max(jnp.abs(ratio))))
    total = state_ref[width:, :]
    kernel = total + product(total, identity - product(identity - ratio, total))
    kernel_ref[...] = kernel
    kernel_terms = right_terms(kernel)
    cols = exact_dot(
        left_terms(pieces_of(parts_ref, piece)), right_terms(inverse_ref[...]), NT
    )
    cols = cols + unit_rows(lax.axis_index("col"), cols.shape)
    cols_out[...] = both_terms(cols)
    rows_left[...] = both_terms(exact_dot(left_terms(turned_ref[...].T), kernel_terms, NT))


def side_call(kernel, operands, shapes, scratch, name):
    vmem = pl.BlockSpec(memory_space=pltpu.VMEM)
    return pl.pallas_call(
        kernel,
        in_specs=[vmem] * len(operands),
        out_specs=[vmem] * len(shapes),
        out_shape=shapes,
        scratch_shapes=scratch,
        cost_estimate=pl.CostEstimate(
            flops=300_000_000, bytes_accessed=10_000_000, transcendentals=0
        ),
        compiler_params=pltpu.CompilerParams(vmem_limit_bytes=14 * MIB),
        name=name,
    )(*operands)


def update_kernel(piece, *refs):
    parts_ref, image_ref, kernel_ref, cols_ref, rows_left, mob_ref = refs[:6]
    out_ref, lhs, rhs, held, sems_in, sems_out = refs[6:]
    count = sems_in.shape[0]
    tile = held.shape[0] // count
    loads, stores = [], []
    for k in range(count):
        rows = pl.ds(k * tile, tile)
        loads.append(pltpu.make_async_copy(mob_ref.at[rows], held.at[rows], sems_in.at[k]))
        stores.append(pltpu.make_async_copy(held.at[rows], out_ref.at[rows], sems_out.at[k]))
        loads[k].start()
    middle = lhs.shape[1] // 2
    lhs[:, :middle] = left_terms(product(image_ref[...], kernel_ref[...]))
    lhs[:, middle:] = to_left(rows_left[...])
    small = right_terms(product(unpack(parts_ref, piece), kernel_ref[...]))
    change = exact_dot(to_left(cols_ref[...]), small, NT)
    rhs[:, :middle] = to_right(cols_ref[...])
    rhs[:, middle:] = right_terms(pieces_of(parts_ref, piece) - change)
    for k in range(count):
        loads[k].wait()
        rows = slice(k * tile, (k + 1) * tile)
        held[rows, :] = held[rows, :] - exact_dot(lhs[rows, :], rhs[...], NT)
        stores[k].start()
    for k in range(count):
        stores[k].wait()


def update(operands, mobility, piece):
    n_rows, n_cols = mobility.shape
    terms = 3 * operands[-1].shape[1]
    vmem = pl.BlockSpec(memory_space=pltpu.VMEM)
    hbm = pl.BlockSpec(memory_space=pltpu.HBM)
    mobility = pltpu.with_memory_space_constraint(mobility, pltpu.HBM)
    return pl.pallas_call(
        lambda *refs: update_kernel(piece, *refs),
        in_specs=[vmem] * len(operands) + [hbm],
        out_specs=hbm,
        out_shape=pltpu.HBM(mobility.shape, jnp.float32),
        scratch_shapes=[
            pltpu.VMEM((n_rows, terms), jnp.bfloat16),
            pltpu.VMEM((n_cols, terms), jnp.bfloat16),
            pltpu.VMEM(mobility.shape, jnp.float32),
            pltpu.SemaphoreType.DMA((4,)),
            pltpu.SemaphoreType.DMA((4,)),
        ],
        cost_estimate=pl.CostEstimate(
            flops=2 * n_rows * n_cols * terms, bytes_accessed=9_000_000, transcendentals=0
        ),
        compiler_params=pltpu.CompilerParams(vmem_limit_bytes=20 * MIB),
        name="update",
    )(*operands, mobility)


def on_device(panel, mobility):
    piece, width = panel.shape
    n_row, n_col = lax.axis_size("row"), lax.axis_size("col")
    block_rows, block_cols = mobility.shape
    share = width // n_col
    transposing = [(i * n_col + j, j * n_col + i) for i in range(n_row) for j in range(n_col)]
    swap = [(i, i ^ 1) for i in range(n_row)]

    def copies(rows, count):
        return jnp.broadcast_to(rows[None], (count,) + rows.shape)

    def gather_row(lone, keep, give, extra):
        summed = keep + lax.ppermute(give, "row", swap)
        sent = jnp.concatenate([lone, summed] + extra, 0)
        return lax.all_gather(sent, "row", axis=0)

    turned_panel = lax.ppermute(panel, BOTH, transposing)
    panel_rows = lax.all_to_all(copies(panel, n_col), "col", 0, 0).reshape(block_rows, width)
    panel_rows, turned_panel = lax.optimization_barrier((panel_rows, turned_panel))
    keep, give, top_part = packed_parts(
        gram_kernel, (panel_rows,), [(share, width)], "gram_parts"
    )
    panel_parts = gather_row(turned_panel, keep, give, [top_part])

    panel_factor, inverse = factor(panel_parts, piece)
    sent = partial_sums(panel_parts, inverse, mobility, piece, share)
    got = lax.all_to_all(sent, "col", 0, 0)
    wide = jax.ShapeDtypeStruct((block_rows, 2 * width), jnp.bfloat16)
    tall = jax.ShapeDtypeStruct((width, block_rows), jnp.float32)
    square = jax.ShapeDtypeStruct((width, width), jnp.float32)
    (turned_rows,) = side_call(rows_kernel, (panel_rows, inverse), [tall], [], "basis_rows")
    got, turned_rows = lax.optimization_barrier((got, turned_rows))
    image, image_copies, top_rows = image_piece(got, piece)
    turned_image = lax.ppermute(image, BOTH, transposing)
    image_rows = lax.all_to_all(image_copies, "col", 0, 0).reshape(block_rows, width)
    basis_cols, rows_left, kernel = side_call(
        lambda *refs: kernel_kernel(piece, *refs),
        (inverse, top_rows, turned_rows, panel_parts),
        [wide, wide, square],
        [pltpu.VMEM((2 * width, width), jnp.float32)],
        "kernel",
    )
    image_rows, turned_image, rows_left = lax.optimization_barrier(
        (image_rows, turned_image, rows_left)
    )
    keep, give = packed_parts(inner_kernel, (turned_rows, image_rows), [], "inner_parts")
    image_parts = gather_row(turned_image, keep, give, [])
    operands = (image_parts, image_rows, kernel, basis_cols, rows_left)
    updated = update(operands, mobility, piece)
    return (updated, panel_factor)


def solution(mesh):
    in_specs = (P(("row", "col"), None), P("row", "col"))
    out_specs = (P("row", "col"), P())
    return jax.shard_map(
        on_device, mesh=mesh, in_specs=in_specs, out_specs=out_specs, check_vma=False
    )
```

```python
import jax
import jax.numpy as jnp
from jax import lax
from jax.experimental import pallas as pl
from jax.experimental.pallas import tpu as pltpu
from jax.sharding import PartitionSpec as P

BOTH = ("row", "col")
STEP = 8
MIB = 1 << 20
NN = (((1,), (0,)), ((), ()))
TN = (((0,), (0,)), ((), ()))
NT = (((1,), (1,)), ((), ()))


def product(first_op, second_op, dims=NN):
    return lax.dot_general(
        first_op,
        second_op,
        dims,
        precision=lax.Precision.HIGHEST,
        preferred_element_type=jnp.float32,
    )


def split(value):
    high = value.astype(jnp.bfloat16)
    return high, (value - high.astype(jnp.float32)).astype(jnp.bfloat16)


def both_terms(value):
    return jnp.concatenate(split(value), 1)


def left_terms(value):
    high, low = split(value)
    return jnp.concatenate([high, low, high], 1)


def right_terms(value):
    high, low = split(value)
    return jnp.concatenate([high, high, low], 1)


def to_left(pair):
    return jnp.concatenate([pair, pair[:, : pair.shape[1] // 2]], 1)


def to_right(pair):
    return jnp.concatenate([pair[:, : pair.shape[1] // 2], pair], 1)


def exact_dot(first_op, second_op, dims):
    return lax.dot_general(first_op, second_op, dims, preferred_element_type=jnp.float32)


def unit_rows(index, shape):
    rows = lax.broadcasted_iota(jnp.int32, shape, 0) + index * shape[0]
    return jnp.where(rows == lax.broadcasted_iota(jnp.int32, shape, 1), 1.0, 0.0)


def eye(width):
    return unit_rows(0, (width, width))


def pieces_of(parts_ref, piece):
    count, _, width = parts_ref.shape
    return parts_ref[:, :piece, :].reshape(count * piece, width)


def pack(value, keep_ref, give_ref):
    side = value.shape[0] // 2
    half = side // 2
    top = value[:side]
    low = pltpu.roll(value[side:], side, 1)
    row = lax.broadcasted_iota(jnp.int32, top.shape, 0)
    lane = lax.broadcasted_iota(jnp.int32, top.shape, 1)
    rows = jnp.where(jnp.logical_and(row < lane, lane < side), low, top)
    last = jnp.sum(jnp.where(row == lane, low, 0.0), axis=0, keepdims=True)
    even = lax.rem(lax.axis_index("row"), 2) == 0
    keep_ref[:half, :] = jnp.where(even, rows[:half], rows[half:])
    give_ref[:half, :] = jnp.where(even, rows[half:], rows[:half])
    keep_ref[half:, :] = jnp.broadcast_to(last, (STEP, last.shape[1]))
    give_ref[half:, :] = jnp.broadcast_to(last, (STEP, last.shape[1]))


def unpack(parts_ref, piece):
    width = parts_ref.shape[2]
    half = width // 4
    stop = piece + half + STEP
    sums = [parts_ref[h, piece:stop, :] for h in range(2)]
    for i in range(2, parts_ref.shape[0]):
        sums[i % 2] = sums[i % 2] + parts_ref[i, piece:stop, :]
    side = 2 * half
    rows = jnp.concatenate([sums[0][:half], sums[1][:half]], 0)
    turned = rows.T
    row = lax.broadcasted_iota(jnp.int32, (side, side), 0)
    lane = lax.broadcasted_iota(jnp.int32, (side, side), 1)
    left, across = rows[:, :side], turned[:side]
    last = sums[0][half : half + 1, :side]
    a = jnp.where(row >= lane, left, across)
    d = jnp.where(row == lane, last, jnp.where(row < lane, left, across))
    return jnp.concatenate(
        [
            jnp.concatenate([a, rows[:, side:]], 1),
            jnp.concatenate([turned[side:], d], 1),
        ],
        0,
    )


def gram_kernel(rows_ref, keep_ref, give_ref, top_ref):
    share = top_ref.shape[0]
    rows = rows_ref[...]
    pack(product(rows, rows, TN), keep_ref, give_ref)
    start = pl.multiple_of(lax.axis_index("col") * share, share)
    top_ref[...] = rows_ref[pl.ds(start, share), :]


def inner_kernel(turned_ref, rows_ref, keep_ref, give_ref):
    terms = product(turned_ref[...], rows_ref[...])
    pack(0.5 * (terms + terms.T), keep_ref, give_ref)


def packed_parts(kernel, operands, extra, name):
    width = operands[-1].shape[1]
    vmem = pl.BlockSpec(memory_space=pltpu.VMEM)
    shapes = [(width // 4 + STEP, width)] * 2 + extra
    return pl.pallas_call(
        kernel,
        in_specs=[vmem] * len(operands),
        out_specs=[vmem] * len(shapes),
        out_shape=[jax.ShapeDtypeStruct(shape, jnp.float32) for shape in shapes],
        cost_estimate=pl.CostEstimate(
            flops=200_000_000, bytes_accessed=3_000_000, transcendentals=0
        ),
        compiler_params=pltpu.CompilerParams(vmem_limit_bytes=8 * MIB),
        name=name,
    )(*operands)


def eliminate(gram, upper_ref, inverse_ref, work, other, beside):
    width = upper_ref.shape[0]
    full = (STEP, width)
    lane = lax.broadcasted_iota(jnp.int32, full, 1)
    work[...] = gram
    other[...] = eye(width)
    for first in range(0, width, STEP):
        beside(first // STEP)
        a_rows = [jnp.broadcast_to(work[first + k : first + k + 1, :], full) for k in range(STEP)]
        x_rows = [jnp.broadcast_to(other[first + k : first + k + 1, :], full) for k in range(STEP)]
        entry, mult, inv = {}, {}, {}
        for i in range(STEP):
            for k in range(i + 1):
                column = a_rows[i][:, first + k : first + k + 1]
                entry[i, k] = jnp.broadcast_to(column, full)
        for k in range(STEP):
            inv[k] = 1.0 / entry[k, k]
            for i in range(k + 1, STEP):
                mult[i, k] = entry[i, k] * inv[k]
            for i in range(k + 1, STEP):
                for l in range(k + 1, i + 1):
                    entry[i, l] = entry[i, l] - mult[i, k] * entry[l, k]
        for i in range(STEP):
            for k in range(i):
                a_rows[i] = a_rows[i] - mult[i, k] * a_rows[k]
                x_rows[i] = x_rows[i] - mult[i, k] * x_rows[k]
        for k in range(STEP):
            root = lax.rsqrt(entry[k, k])
            root = root * (1.5 - 0.5 * entry[k, k] * root * root)
            row = slice(first + k, first + k + 1)
            upper_ref[row, :] = jnp.where(lane >= first + k, a_rows[k] * root, 0.0)[:1]
            inverse_ref[row, :] = (x_rows[k] * root)[:1]
        if first + STEP == width:
            break
        a_back = [a_rows[k] * inv[k] for k in range(STEP)]
        x_back = [x_rows[k] * inv[k] for k in range(STEP)]
        for k in range(STEP - 2, -1, -1):
            for l in range(k + 1, STEP):
                a_back[k] = a_back[k] - mult[l, k] * a_back[l]
                x_back[k] = x_back[k] - mult[l, k] * x_back[l]
        for g in range(first + STEP, width, STEP):
            block = work[g : g + STEP, :]
            a_new, x_new = block, other[g : g + STEP, :]
            for k in range(STEP):
                column = jnp.broadcast_to(block[:, first + k : first + k + 1], full)
                a_new = a_new - column * a_back[k]
                x_new = x_new - column * x_back[k]
            work[g : g + STEP, :] = a_new
            other[g : g + STEP, :] = x_new


def product_kernel(piece, share, parts_ref, mob_ref, upper_ref, inverse_ref, out_ref, *refs):
    work, other, rhs, held, found, sems = refs
    width = parts_ref.shape[2]
    count = sems.shape[0]
    tile = held.shape[0] // count
    loads = []
    for k in range(count):
        rows = pl.ds(k * tile, tile)
        loads.append(pltpu.make_async_copy(mob_ref.at[rows], held.at[rows], sems.at[k]))
        loads[k].start()
    rhs[...] = both_terms(pieces_of(parts_ref, piece))
    last = parts_ref.shape[1] - share
    out_ref[:, piece:, :] = jnp.broadcast_to(
        parts_ref[0, last:, :][None], (out_ref.shape[0], share, width)
    )

    def beside(index):
        k = index // 3 - 1
        if index % 3 or not 0 <= k < count:
            return
        loads[k].wait()
        rows = slice(k * tile, (k + 1) * tile)
        high, low = split(held[rows, :])
        wide = exact_dot(high, rhs[...], NN)
        low_part = exact_dot(low, rhs[:, :width], NN)
        found[rows, :] = wide[:, :width] + wide[:, width:] + low_part

    eliminate(unpack(parts_ref, piece), upper_ref, inverse_ref, work, other, beside)
    image = exact_dot(left_terms(found[...]), right_terms(inverse_ref[...]), NT)
    image = image + jnp.where(lax.axis_index("col") == 0, held[:, :width], 0.0)
    out_ref[:, :piece, :] = image.reshape(out_ref.shape[0], piece, width)


def factor_and_product(parts, mobility, piece, share):
    n_rows, n_cols = mobility.shape
    width = parts.shape[2]
    vmem = pl.BlockSpec(memory_space=pltpu.VMEM)
    square = jax.ShapeDtypeStruct((width, width), jnp.float32)
    mobility = pltpu.with_memory_space_constraint(mobility, pltpu.HBM)
    return pl.pallas_call(
        lambda *refs: product_kernel(piece, share, *refs),
        in_specs=[vmem, pl.BlockSpec(memory_space=pltpu.HBM)],
        out_specs=[vmem] * 3,
        out_shape=(
            square,
            square,
            jax.ShapeDtypeStruct((n_rows // piece, piece + share, width), jnp.float32),
        ),
        scratch_shapes=[
            pltpu.VMEM((width, width), jnp.float32),
            pltpu.VMEM((width, width), jnp.float32),
            pltpu.VMEM((n_cols, 2 * width), jnp.bfloat16),
            pltpu.VMEM(mobility.shape, jnp.float32),
            pltpu.VMEM((n_rows, width), jnp.float32),
            pltpu.SemaphoreType.DMA((4,)),
        ],
        cost_estimate=pl.CostEstimate(
            flops=6 * n_rows * n_cols * width, bytes_accessed=6_000_000, transcendentals=0
        ),
        compiler_params=pltpu.CompilerParams(vmem_limit_bytes=20 * MIB),
        name="factor_and_product",
    )(parts, mobility)


def copy_kernel(rows_ref, out_ref):
    out_ref[...] = jnp.broadcast_to(rows_ref[...][None], out_ref.shape)


def copies(rows, count):
    vmem = pl.BlockSpec(memory_space=pltpu.VMEM)
    return pl.pallas_call(
        copy_kernel,
        in_specs=[vmem],
        out_specs=vmem,
        out_shape=jax.ShapeDtypeStruct((count,) + rows.shape, rows.dtype),
        cost_estimate=pl.CostEstimate(flops=0, bytes_accessed=600_000, transcendentals=0),
        compiler_params=pltpu.CompilerParams(vmem_limit_bytes=4 * MIB),
        name="copies",
    )(rows)


def image_kernel(piece, got_ref, image_ref, copies_ref, top_ref):
    image = got_ref[0, :piece, :]
    for k in range(1, got_ref.shape[0]):
        image = image + got_ref[k, :piece, :]
    image_ref[...] = image
    copies_ref[...] = jnp.broadcast_to(image[None], copies_ref.shape)
    top_ref[...] = got_ref[:, piece:, :].reshape(top_ref.shape)


def image_piece(got, piece):
    count, _, width = got.shape
    vmem = pl.BlockSpec(memory_space=pltpu.VMEM)
    return pl.pallas_call(
        lambda *refs: image_kernel(piece, *refs),
        in_specs=[vmem],
        out_specs=[vmem] * 3,
        out_shape=(
            jax.ShapeDtypeStruct((piece, width), jnp.float32),
            jax.ShapeDtypeStruct((count, piece, width), jnp.float32),
            jax.ShapeDtypeStruct((width, width), jnp.float32),
        ),
        cost_estimate=pl.CostEstimate(
            flops=10_000_000, bytes_accessed=2_000_000, transcendentals=0
        ),
        compiler_params=pltpu.CompilerParams(vmem_limit_bytes=6 * MIB),
        name="image_piece",
    )(got)


def rows_kernel(rows_ref, inverse_ref, turned_ref):
    rows = exact_dot(left_terms(rows_ref[...]), right_terms(inverse_ref[...]), NT)
    turned_ref[...] = (rows + unit_rows(lax.axis_index("row"), rows.shape)).T


def kernel_kernel(piece, inverse_ref, top_ref, turned_ref, parts_ref, *outs):
    cols_out, rows_left, state_ref = outs
    width = inverse_ref.shape[0]
    identity = eye(width)
    ratio = -product(inverse_ref[...], top_ref[...], NT)
    state_ref[:width, :] = ratio
    state_ref[width:, :] = identity

    def go_on(state):
        return jnp.logical_and(state[0] < 40, state[1] > 1e-10)

    def double(state):
        power = state_ref[:width, :]
        both = product(state_ref[...], power)
        state_ref[:width, :] = both[:width]
        state_ref[width:, :] = state_ref[width:, :] + both[width:]
        return state[0] + 1, jnp.max(jnp.abs(both[:width]))

    lax.while_loop(go_on, double, (0, jnp.max(jnp.abs(ratio))))
    total = state_ref[width:, :]
    kernel = total + product(total, identity - product(identity - ratio, total))
    kernel_terms = right_terms(kernel)
    cols = exact_dot(
        left_terms(pieces_of(parts_ref, piece)), right_terms(inverse_ref[...]), NT
    )
    cols = cols + unit_rows(lax.axis_index("col"), cols.shape)
    cols_out[...] = both_terms(exact_dot(left_terms(cols), kernel_terms, NT))
    rows_left[...] = both_terms(exact_dot(left_terms(turned_ref[...].T), kernel_terms, NT))


def side_call(kernel, operands, shapes, scratch, name):
    vmem = pl.BlockSpec(memory_space=pltpu.VMEM)
    return pl.pallas_call(
        kernel,
        in_specs=[vmem] * len(operands),
        out_specs=[vmem] * len(shapes),
        out_shape=shapes,
        scratch_shapes=scratch,
        cost_estimate=pl.CostEstimate(
            flops=300_000_000, bytes_accessed=10_000_000, transcendentals=0
        ),
        compiler_params=pltpu.CompilerParams(vmem_limit_bytes=14 * MIB),
        name=name,
    )(*operands)


def update_kernel(piece, *refs):
    parts_ref, image_ref, cols_ref, rows_left, mob_ref = refs[:5]
    out_ref, lhs, rhs, held, sems_in, sems_out = refs[5:]
    count = sems_in.shape[0]
    tile = held.shape[0] // count
    loads, stores = [], []
    for k in range(count):
        rows = pl.ds(k * tile, tile)
        loads.append(pltpu.make_async_copy(mob_ref.at[rows], held.at[rows], sems_in.at[k]))
        stores.append(pltpu.make_async_copy(held.at[rows], out_ref.at[rows], sems_out.at[k]))
        loads[k].start()
    middle = lhs.shape[1] // 2
    lhs[:, :middle] = left_terms(image_ref[...])
    lhs[:, middle:] = to_left(rows_left[...])
    small = right_terms(unpack(parts_ref, piece))
    change = exact_dot(to_left(cols_ref[...]), small, NT)
    rhs[:, :middle] = to_right(cols_ref[...])
    rhs[:, middle:] = right_terms(pieces_of(parts_ref, piece) - change)
    for k in range(count):
        loads[k].wait()
        rows = slice(k * tile, (k + 1) * tile)
        held[rows, :] = held[rows, :] - exact_dot(lhs[rows, :], rhs[...], NT)
        stores[k].start()
    for k in range(count):
        stores[k].wait()


def update(operands, mobility, piece):
    n_rows, n_cols = mobility.shape
    terms = 3 * operands[-1].shape[1]
    vmem = pl.BlockSpec(memory_space=pltpu.VMEM)
    hbm = pl.BlockSpec(memory_space=pltpu.HBM)
    mobility = pltpu.with_memory_space_constraint(mobility, pltpu.HBM)
    return pl.pallas_call(
        lambda *refs: update_kernel(piece, *refs),
        in_specs=[vmem] * len(operands) + [hbm],
        out_specs=hbm,
        out_shape=pltpu.HBM(mobility.shape, jnp.float32),
        scratch_shapes=[
            pltpu.VMEM((n_rows, terms), jnp.bfloat16),
            pltpu.VMEM((n_cols, terms), jnp.bfloat16),
            pltpu.VMEM(mobility.shape, jnp.float32),
            pltpu.SemaphoreType.DMA((4,)),
            pltpu.SemaphoreType.DMA((4,)),
        ],
        cost_estimate=pl.CostEstimate(
            flops=2 * n_rows * n_cols * terms, bytes_accessed=9_000_000, transcendentals=0
        ),
        compiler_params=pltpu.CompilerParams(vmem_limit_bytes=20 * MIB),
        name="update",
    )(*operands, mobility)


def on_device(panel, mobility):
    piece, width = panel.shape
    n_row, n_col = lax.axis_size("row"), lax.axis_size("col")
    block_rows, block_cols = mobility.shape
    share = width // n_col
    transposing = [(i * n_col + j, j * n_col + i) for i in range(n_row) for j in range(n_col)]
    swap = [(i, i ^ 1) for i in range(n_row)]

    def gather_row(lone, keep, give, extra):
        summed = keep + lax.ppermute(give, "row", swap)
        sent = jnp.concatenate([lone, summed] + extra, 0)
        return lax.all_gather(sent, "row", axis=0)

    turned_panel = lax.ppermute(panel, BOTH, transposing)
    panel_rows = lax.all_to_all(copies(panel, n_col), "col", 0, 0).reshape(block_rows, width)
    panel_rows, turned_panel = lax.optimization_barrier((panel_rows, turned_panel))
    keep, give, top_part = packed_parts(
        gram_kernel, (panel_rows,), [(share, width)], "gram_parts"
    )
    panel_parts = gather_row(turned_panel, keep, give, [top_part])

    panel_factor, inverse, sent = factor_and_product(panel_parts, mobility, piece, share)
    got = lax.all_to_all(sent, "col", 0, 0)
    wide = jax.ShapeDtypeStruct((block_rows, 2 * width), jnp.bfloat16)
    tall = jax.ShapeDtypeStruct((width, block_rows), jnp.float32)
    (turned_rows,) = side_call(rows_kernel, (panel_rows, inverse), [tall], [], "basis_rows")
    got, turned_rows = lax.optimization_barrier((got, turned_rows))
    image, image_copies, top_rows = image_piece(got, piece)
    turned_image = lax.ppermute(image, BOTH, transposing)
    image_rows = lax.all_to_all(image_copies, "col", 0, 0).reshape(block_rows, width)
    cols_right, rows_left = side_call(
        lambda *refs: kernel_kernel(piece, *refs),
        (inverse, top_rows, turned_rows, panel_parts),
        [wide, wide],
        [pltpu.VMEM((2 * width, width), jnp.float32)],
        "kernel",
    )
    image_rows, turned_image, rows_left = lax.optimization_barrier(
        (image_rows, turned_image, rows_left)
    )
    keep, give = packed_parts(inner_kernel, (turned_rows, image_rows), [], "inner_parts")
    image_parts = gather_row(turned_image, keep, give, [])
    operands = (image_parts, image_rows, cols_right, rows_left)
    updated = update(operands, mobility, piece)
    return (updated, panel_factor)


def solution(mesh):
    in_specs = (P(("row", "col"), None), P("row", "col"))
    out_specs = (P("row", "col"), P())
    return jax.shard_map(
        on_device, mesh=mesh, in_specs=in_specs, out_specs=out_specs, check_vma=False
    )
```

```python
import jax
import jax.numpy as jnp
from jax import lax
from jax.experimental import pallas as pl
from jax.experimental.pallas import tpu as pltpu
from jax.sharding import PartitionSpec as P

BOTH = ("row", "col")
STEP = 8
MIB = 1 << 20
NN = (((1,), (0,)), ((), ()))
TN = (((0,), (0,)), ((), ()))
NT = (((1,), (1,)), ((), ()))


def product(first_op, second_op, dims=NN):
    return lax.dot_general(
        first_op,
        second_op,
        dims,
        precision=lax.Precision.HIGHEST,
        preferred_element_type=jnp.float32,
    )


def split(value):
    high = value.astype(jnp.bfloat16)
    return high, (value - high.astype(jnp.float32)).astype(jnp.bfloat16)


def both_terms(value):
    return jnp.concatenate(split(value), 1)


def left_terms(value):
    high, low = split(value)
    return jnp.concatenate([high, low, high], 1)


def right_terms(value):
    high, low = split(value)
    return jnp.concatenate([high, high, low], 1)


def to_left(pair):
    return jnp.concatenate([pair, pair[:, : pair.shape[1] // 2]], 1)


def to_right(pair):
    return jnp.concatenate([pair[:, : pair.shape[1] // 2], pair], 1)


def exact_dot(first_op, second_op, dims):
    return lax.dot_general(first_op, second_op, dims, preferred_element_type=jnp.float32)


def unit_rows(index, shape):
    rows = lax.broadcasted_iota(jnp.int32, shape, 0) + index * shape[0]
    return jnp.where(rows == lax.broadcasted_iota(jnp.int32, shape, 1), 1.0, 0.0)


def eye(width):
    return unit_rows(0, (width, width))


def pieces_of(parts_ref, piece):
    count, _, width = parts_ref.shape
    return parts_ref[:, :piece, :].reshape(count * piece, width)


def pack(value, keep_ref, give_ref):
    side = value.shape[0] // 2
    half = side // 2
    top = value[:side]
    low = pltpu.roll(value[side:], side, 1)
    row = lax.broadcasted_iota(jnp.int32, top.shape, 0)
    lane = lax.broadcasted_iota(jnp.int32, top.shape, 1)
    rows = jnp.where(jnp.logical_and(row < lane, lane < side), low, top)
    last = jnp.sum(jnp.where(row == lane, low, 0.0), axis=0, keepdims=True)
    even = lax.rem(lax.axis_index("row"), 2) == 0
    keep_ref[:half, :] = jnp.where(even, rows[:half], rows[half:])
    give_ref[:half, :] = jnp.where(even, rows[half:], rows[:half])
    keep_ref[half:, :] = jnp.broadcast_to(last, (STEP, last.shape[1]))
    give_ref[half:, :] = jnp.broadcast_to(last, (STEP, last.shape[1]))


def unpack(parts_ref, piece):
    width = parts_ref.shape[2]
    half = width // 4
    stop = piece + half + STEP
    sums = [parts_ref[h, piece:stop, :] for h in range(2)]
    for i in range(2, parts_ref.shape[0]):
        sums[i % 2] = sums[i % 2] + parts_ref[i, piece:stop, :]
    side = 2 * half
    rows = jnp.concatenate([sums[0][:half], sums[1][:half]], 0)
    turned = rows.T
    row = lax.broadcasted_iota(jnp.int32, (side, side), 0)
    lane = lax.broadcasted_iota(jnp.int32, (side, side), 1)
    left, across = rows[:, :side], turned[:side]
    last = sums[0][half : half + 1, :side]
    a = jnp.where(row >= lane, left, across)
    d = jnp.where(row == lane, last, jnp.where(row < lane, left, across))
    return jnp.concatenate(
        [
            jnp.concatenate([a, rows[:, side:]], 1),
            jnp.concatenate([turned[side:], d], 1),
        ],
        0,
    )


def gram_kernel(rows_ref, keep_ref, give_ref, top_ref):
    share = top_ref.shape[0]
    rows = rows_ref[...]
    pack(product(rows, rows, TN), keep_ref, give_ref)
    start = pl.multiple_of(lax.axis_index("col") * share, share)
    top_ref[...] = rows_ref[pl.ds(start, share), :]


def inner_kernel(turned_ref, rows_ref, keep_ref, give_ref):
    terms = product(turned_ref[...], rows_ref[...])
    pack(0.5 * (terms + terms.T), keep_ref, give_ref)


def packed_parts(kernel, operands, extra, name):
    width = operands[-1].shape[1]
    vmem = pl.BlockSpec(memory_space=pltpu.VMEM)
    shapes = [(width // 4 + STEP, width)] * 2 + extra
    return pl.pallas_call(
        kernel,
        in_specs=[vmem] * len(operands),
        out_specs=[vmem] * len(shapes),
        out_shape=[jax.ShapeDtypeStruct(shape, jnp.float32) for shape in shapes],
        cost_estimate=pl.CostEstimate(
            flops=200_000_000, bytes_accessed=3_000_000, transcendentals=0
        ),
        compiler_params=pltpu.CompilerParams(vmem_limit_bytes=8 * MIB),
        name=name,
    )(*operands)


def eliminate(gram, upper_ref, inverse_ref, work, other, beside):
    width = upper_ref.shape[0]
    full = (STEP, width)
    lane = lax.broadcasted_iota(jnp.int32, full, 1)
    work[...] = gram
    other[...] = eye(width)
    for first in range(0, width, STEP):
        beside(first // STEP)
        a_rows = [jnp.broadcast_to(work[first + k : first + k + 1, :], full) for k in range(STEP)]
        x_rows = [jnp.broadcast_to(other[first + k : first + k + 1, :], full) for k in range(STEP)]
        entry, mult, inv = {}, {}, {}
        for i in range(STEP):
            for k in range(i + 1):
                column = a_rows[i][:, first + k : first + k + 1]
                entry[i, k] = jnp.broadcast_to(column, full)
        for k in range(STEP):
            inv[k] = 1.0 / entry[k, k]
            for i in range(k + 1, STEP):
                mult[i, k] = entry[i, k] * inv[k]
            for i in range(k + 1, STEP):
                for l in range(k + 1, i + 1):
                    entry[i, l] = entry[i, l] - mult[i, k] * entry[l, k]
        for i in range(STEP):
            for k in range(i):
                a_rows[i] = a_rows[i] - mult[i, k] * a_rows[k]
                x_rows[i] = x_rows[i] - mult[i, k] * x_rows[k]
        for k in range(STEP):
            root = lax.rsqrt(entry[k, k])
            root = root * (1.5 - 0.5 * entry[k, k] * root * root)
            row = slice(first + k, first + k + 1)
            upper_ref[row, :] = jnp.where(lane >= first + k, a_rows[k] * root, 0.0)[:1]
            inverse_ref[row, :] = (x_rows[k] * root)[:1]
        if first + STEP == width:
            break
        a_back = [a_rows[k] * inv[k] for k in range(STEP)]
        x_back = [x_rows[k] * inv[k] for k in range(STEP)]
        for k in range(STEP - 2, -1, -1):
            for l in range(k + 1, STEP):
                a_back[k] = a_back[k] - mult[l, k] * a_back[l]
                x_back[k] = x_back[k] - mult[l, k] * x_back[l]
        for g in range(first + STEP, width, STEP):
            block = work[g : g + STEP, :]
            a_new, x_new = block, other[g : g + STEP, :]
            for k in range(STEP):
                column = jnp.broadcast_to(block[:, first + k : first + k + 1], full)
                a_new = a_new - column * a_back[k]
                x_new = x_new - column * x_back[k]
            work[g : g + STEP, :] = a_new
            other[g : g + STEP, :] = x_new


def product_kernel(piece, share, parts_ref, mob_ref, upper_ref, inverse_ref, out_ref, *refs):
    work, other, rhs, held, found, sems = refs
    width = parts_ref.shape[2]
    count = sems.shape[0]
    tile = held.shape[0] // count
    loads = []
    for k in range(count):
        rows = pl.ds(k * tile, tile)
        loads.append(pltpu.make_async_copy(mob_ref.at[rows], held.at[rows], sems.at[k]))
        loads[k].start()
    rhs[...] = both_terms(pieces_of(parts_ref, piece))
    last = parts_ref.shape[1] - share
    out_ref[:, piece:, :] = jnp.broadcast_to(
        parts_ref[0, last:, :][None], (out_ref.shape[0], share, width)
    )

    def beside(index):
        k = index // 3 - 1
        if index % 3 or not 0 <= k < count:
            return
        loads[k].wait()
        rows = slice(k * tile, (k + 1) * tile)
        high, low = split(held[rows, :])
        wide = exact_dot(high, rhs[...], NN)
        low_part = exact_dot(low, rhs[:, :width], NN)
        found[rows, :] = wide[:, :width] + wide[:, width:] + low_part

    eliminate(unpack(parts_ref, piece), upper_ref, inverse_ref, work, other, beside)
    image = exact_dot(left_terms(found[...]), right_terms(inverse_ref[...]), NT)
    image = image + jnp.where(lax.axis_index("col") == 0, held[:, :width], 0.0)
    out_ref[:, :piece, :] = image.reshape(out_ref.shape[0], piece, width)


def factor_and_product(parts, mobility, piece, share):
    n_rows, n_cols = mobility.shape
    width = parts.shape[2]
    vmem = pl.BlockSpec(memory_space=pltpu.VMEM)
    square = jax.ShapeDtypeStruct((width, width), jnp.float32)
    mobility = pltpu.with_memory_space_constraint(mobility, pltpu.HBM)
    return pl.pallas_call(
        lambda *refs: product_kernel(piece, share, *refs),
        in_specs=[vmem, pl.BlockSpec(memory_space=pltpu.HBM)],
        out_specs=[vmem] * 3,
        out_shape=(
            square,
            square,
            jax.ShapeDtypeStruct((n_rows // piece, piece + share, width), jnp.float32),
        ),
        scratch_shapes=[
            pltpu.VMEM((width, width), jnp.float32),
            pltpu.VMEM((width, width), jnp.float32),
            pltpu.VMEM((n_cols, 2 * width), jnp.bfloat16),
            pltpu.VMEM(mobility.shape, jnp.float32),
            pltpu.VMEM((n_rows, width), jnp.float32),
            pltpu.SemaphoreType.DMA((4,)),
        ],
        cost_estimate=pl.CostEstimate(
            flops=6 * n_rows * n_cols * width, bytes_accessed=6_000_000, transcendentals=0
        ),
        compiler_params=pltpu.CompilerParams(vmem_limit_bytes=20 * MIB),
        name="factor_and_product",
    )(parts, mobility)


def copy_kernel(rows_ref, out_ref, sems):
    sends = []
    for k in range(out_ref.shape[0]):
        sends.append(pltpu.make_async_copy(rows_ref, out_ref.at[k], sems.at[k]))
        sends[k].start()
    for send in sends:
        send.wait()


def copies(rows, count):
    hbm = pl.BlockSpec(memory_space=pltpu.HBM)
    shape = (count,) + rows.shape
    return pl.pallas_call(
        copy_kernel,
        in_specs=[hbm],
        out_specs=hbm,
        out_shape=pltpu.HBM(shape, rows.dtype),
        scratch_shapes=[pltpu.SemaphoreType.DMA((count,))],
        cost_estimate=pl.CostEstimate(flops=0, bytes_accessed=600_000, transcendentals=0),
        compiler_params=pltpu.CompilerParams(vmem_limit_bytes=4 * MIB),
        name="copies",
    )(pltpu.with_memory_space_constraint(rows, pltpu.HBM))


def join_kernel(lone_ref, keep_ref, came_ref, mob_ref, out_ref):
    piece = lone_ref.shape[0]
    out_ref[:piece, :] = lone_ref[...]
    out_ref[piece:, :] = keep_ref[...] + came_ref[...]


def join(lone, keep, came, mobility):
    vmem = pl.BlockSpec(memory_space=pltpu.VMEM)
    shape = (lone.shape[0] + keep.shape[0], lone.shape[1])
    return pl.pallas_call(
        join_kernel,
        in_specs=[vmem] * 3 + [pl.BlockSpec(memory_space=pltpu.HBM)],
        out_specs=vmem,
        out_shape=jax.ShapeDtypeStruct(shape, jnp.float32),
        cost_estimate=pl.CostEstimate(flops=0, bytes_accessed=100_000, transcendentals=0),
        compiler_params=pltpu.CompilerParams(vmem_limit_bytes=4 * MIB),
        name="join",
    )(lone, keep, came, pltpu.with_memory_space_constraint(mobility, pltpu.HBM))


def image_kernel(piece, got_ref, image_ref, copies_ref, top_ref):
    image = got_ref[0, :piece, :]
    for k in range(1, got_ref.shape[0]):
        image = image + got_ref[k, :piece, :]
    image_ref[...] = image
    copies_ref[...] = jnp.broadcast_to(image[None], copies_ref.shape)
    top_ref[...] = got_ref[:, piece:, :].reshape(top_ref.shape)


def image_piece(got, piece):
    count, _, width = got.shape
    vmem = pl.BlockSpec(memory_space=pltpu.VMEM)
    return pl.pallas_call(
        lambda *refs: image_kernel(piece, *refs),
        in_specs=[vmem],
        out_specs=[vmem] * 3,
        out_shape=(
            jax.ShapeDtypeStruct((piece, width), jnp.float32),
            jax.ShapeDtypeStruct((count, piece, width), jnp.float32),
            jax.ShapeDtypeStruct((width, width), jnp.float32),
        ),
        cost_estimate=pl.CostEstimate(
            flops=10_000_000, bytes_accessed=2_000_000, transcendentals=0
        ),
        compiler_params=pltpu.CompilerParams(vmem_limit_bytes=6 * MIB),
        name="image_piece",
    )(got)


def rows_kernel(rows_ref, inverse_ref, turned_ref):
    rows = exact_dot(left_terms(rows_ref[...]), right_terms(inverse_ref[...]), NT)
    turned_ref[...] = (rows + unit_rows(lax.axis_index("row"), rows.shape)).T


def kernel_kernel(piece, inverse_ref, top_ref, turned_ref, parts_ref, *outs):
    cols_out, rows_left, state_ref = outs
    width = inverse_ref.shape[0]
    identity = eye(width)
    ratio = -product(inverse_ref[...], top_ref[...], NT)
    state_ref[:width, :] = ratio
    state_ref[width:, :] = identity

    def go_on(state):
        return jnp.logical_and(state[0] < 40, state[1] > 1e-10)

    def double(state):
        power = state_ref[:width, :]
        both = product(state_ref[...], power)
        state_ref[:width, :] = both[:width]
        state_ref[width:, :] = state_ref[width:, :] + both[width:]
        return state[0] + 1, jnp.max(jnp.abs(both[:width]))

    lax.while_loop(go_on, double, (0, jnp.max(jnp.abs(ratio))))
    total = state_ref[width:, :]
    kernel = total + product(total, identity - product(identity - ratio, total))
    kernel_terms = right_terms(kernel)
    cols = exact_dot(
        left_terms(pieces_of(parts_ref, piece)), right_terms(inverse_ref[...]), NT
    )
    cols = cols + unit_rows(lax.axis_index("col"), cols.shape)
    cols_out[...] = both_terms(exact_dot(left_terms(cols), kernel_terms, NT))
    rows_left[...] = both_terms(exact_dot(left_terms(turned_ref[...].T), kernel_terms, NT))


def side_call(kernel, operands, shapes, scratch, name):
    vmem = pl.BlockSpec(memory_space=pltpu.VMEM)
    return pl.pallas_call(
        kernel,
        in_specs=[vmem] * len(operands),
        out_specs=[vmem] * len(shapes),
        out_shape=shapes,
        scratch_shapes=scratch,
        cost_estimate=pl.CostEstimate(
            flops=300_000_000, bytes_accessed=10_000_000, transcendentals=0
        ),
        compiler_params=pltpu.CompilerParams(vmem_limit_bytes=14 * MIB),
        name=name,
    )(*operands)


def update_kernel(piece, *refs):
    parts_ref, image_ref, cols_ref, rows_left, mob_ref = refs[:5]
    out_ref, lhs, rhs, held, sems = refs[5:]
    count = sems.shape[0]
    tile = held.shape[0] // count
    middle = lhs.shape[1] // 2
    lhs[:, :middle] = left_terms(image_ref[...])
    lhs[:, middle:] = to_left(rows_left[...])
    small = right_terms(unpack(parts_ref, piece))
    change = exact_dot(to_left(cols_ref[...]), small, NT)
    rhs[:middle, :] = to_right(cols_ref[...]).T
    rhs[middle:, :] = right_terms(pieces_of(parts_ref, piece) - change).T
    stores = []
    for k in range(count):
        rows = pl.ds(k * tile, tile)
        held[rows, :] = mob_ref[rows, :] - exact_dot(lhs[rows, :], rhs[...], NN)
        stores.append(pltpu.make_async_copy(held.at[rows], out_ref.at[rows], sems.at[k]))
        stores[k].start()
    for k in range(count):
        stores[k].wait()


def update(operands, mobility, piece):
    n_rows, n_cols = mobility.shape
    terms = 3 * operands[-1].shape[1]
    vmem = pl.BlockSpec(memory_space=pltpu.VMEM)
    hbm = pl.BlockSpec(memory_space=pltpu.HBM)
    return pl.pallas_call(
        lambda *refs: update_kernel(piece, *refs),
        in_specs=[vmem] * (len(operands) + 1),
        out_specs=hbm,
        out_shape=pltpu.HBM(mobility.shape, jnp.float32),
        scratch_shapes=[
            pltpu.VMEM((n_rows, terms), jnp.bfloat16),
            pltpu.VMEM((terms, n_cols), jnp.bfloat16),
            pltpu.VMEM(mobility.shape, jnp.float32),
            pltpu.SemaphoreType.DMA((4,)),
        ],
        cost_estimate=pl.CostEstimate(
            flops=2 * n_rows * n_cols * terms, bytes_accessed=9_000_000, transcendentals=0
        ),
        compiler_params=pltpu.CompilerParams(vmem_limit_bytes=20 * MIB),
        name="update",
    )(*operands, mobility)


def on_device(panel, mobility):
    piece, width = panel.shape
    n_row, n_col = lax.axis_size("row"), lax.axis_size("col")
    block_rows, block_cols = mobility.shape
    share = width // n_col
    transposing = [(i * n_col + j, j * n_col + i) for i in range(n_row) for j in range(n_col)]
    swap = [(i, i ^ 1) for i in range(n_row)]

    turned_panel = lax.ppermute(panel, BOTH, transposing)
    panel_rows = lax.all_to_all(copies(panel, n_col), "col", 0, 0).reshape(block_rows, width)
    panel_rows, turned_panel = lax.optimization_barrier((panel_rows, turned_panel))
    keep, give, top_part = packed_parts(
        gram_kernel, (panel_rows,), [(share, width)], "gram_parts"
    )
    packed = keep + lax.ppermute(give, "row", swap)
    panel_parts = lax.all_gather(jnp.concatenate([turned_panel, packed, top_part], 0), "row", axis=0)

    panel_factor, inverse, sent = factor_and_product(panel_parts, mobility, piece, share)
    got = lax.all_to_all(sent, "col", 0, 0)
    wide = jax.ShapeDtypeStruct((block_rows, 2 * width), jnp.bfloat16)
    tall = jax.ShapeDtypeStruct((width, block_rows), jnp.float32)
    (turned_rows,) = side_call(rows_kernel, (panel_rows, inverse), [tall], [], "basis_rows")
    got, turned_rows = lax.optimization_barrier((got, turned_rows))
    image, image_copies, top_rows = image_piece(got, piece)
    turned_image = lax.ppermute(image, BOTH, transposing)
    image_rows = lax.all_to_all(image_copies, "col", 0, 0).reshape(block_rows, width)
    cols_right, rows_left = side_call(
        lambda *refs: kernel_kernel(piece, *refs),
        (inverse, top_rows, turned_rows, panel_parts),
        [wide, wide],
        [pltpu.VMEM((2 * width, width), jnp.float32)],
        "kernel",
    )
    image_rows, turned_image, rows_left = lax.optimization_barrier(
        (image_rows, turned_image, rows_left)
    )
    keep, give = packed_parts(inner_kernel, (turned_rows, image_rows), [], "inner_parts")
    came = lax.ppermute(give, "row", swap)
    image_parts = lax.all_gather(join(turned_image, keep, came, mobility), "row", axis=0)
    operands = (image_parts, image_rows, cols_right, rows_left)
    updated = update(operands, mobility, piece)
    return (updated, panel_factor)


def solution(mesh):
    in_specs = (P(("row", "col"), None), P("row", "col"))
    out_specs = (P("row", "col"), P())
    return jax.shard_map(
        on_device, mesh=mesh, in_specs=in_specs, out_specs=out_specs, check_vma=False
    )
```

```python
import jax
import jax.numpy as jnp
from jax import lax
from jax.experimental import pallas as pl
from jax.experimental.pallas import tpu as pltpu
from jax.sharding import PartitionSpec as P

BOTH = ("row", "col")
STEP = 8
MIB = 1 << 20
NN = (((1,), (0,)), ((), ()))
TN = (((0,), (0,)), ((), ()))
NT = (((1,), (1,)), ((), ()))


def product(first_op, second_op, dims=NN):
    return lax.dot_general(
        first_op,
        second_op,
        dims,
        precision=lax.Precision.HIGHEST,
        preferred_element_type=jnp.float32,
    )


def split(value):
    high = value.astype(jnp.bfloat16)
    return high, (value - high.astype(jnp.float32)).astype(jnp.bfloat16)


def both_terms(value):
    return jnp.concatenate(split(value), 1)


def left_terms(value):
    high, low = split(value)
    return jnp.concatenate([high, low, high], 1)


def right_terms(value):
    high, low = split(value)
    return jnp.concatenate([high, high, low], 1)


def to_left(pair):
    return jnp.concatenate([pair, pair[:, : pair.shape[1] // 2]], 1)


def to_right(pair):
    return jnp.concatenate([pair[:, : pair.shape[1] // 2], pair], 1)


def exact_dot(first_op, second_op, dims):
    return lax.dot_general(first_op, second_op, dims, preferred_element_type=jnp.float32)


def unit_rows(index, shape):
    rows = lax.broadcasted_iota(jnp.int32, shape, 0) + index * shape[0]
    return jnp.where(rows == lax.broadcasted_iota(jnp.int32, shape, 1), 1.0, 0.0)


def eye(width):
    return unit_rows(0, (width, width))


def pieces_of(parts_ref, piece):
    count, _, width = parts_ref.shape
    return parts_ref[:, :piece, :].reshape(count * piece, width)


def pack(value, keep_ref, give_ref):
    side = value.shape[0] // 2
    half = side // 2
    top = value[:side]
    low = pltpu.roll(value[side:], side, 1)
    row = lax.broadcasted_iota(jnp.int32, top.shape, 0)
    lane = lax.broadcasted_iota(jnp.int32, top.shape, 1)
    rows = jnp.where(jnp.logical_and(row < lane, lane < side), low, top)
    last = jnp.sum(jnp.where(row == lane, low, 0.0), axis=0, keepdims=True)
    even = lax.rem(lax.axis_index("row"), 2) == 0
    keep_ref[:half, :] = jnp.where(even, rows[:half], rows[half:])
    give_ref[:half, :] = jnp.where(even, rows[half:], rows[:half])
    keep_ref[half:, :] = jnp.broadcast_to(last, (STEP, last.shape[1]))
    give_ref[half:, :] = jnp.broadcast_to(last, (STEP, last.shape[1]))


def unpack(parts_ref, piece):
    half = parts_ref.shape[2] // 4
    stop = piece + half
    sums = [parts_ref[0, piece:stop, :], parts_ref[1, piece : stop + STEP, :]]
    for i in range(2, parts_ref.shape[0], 2):
        sums[0] = sums[0] + parts_ref[i, piece:stop, :]
        sums[1] = sums[1] + parts_ref[i + 1, piece : stop + STEP, :]
    side = 2 * half
    rows = jnp.concatenate([sums[0], sums[1][:half]], 0)
    turned = rows.T
    row = lax.broadcasted_iota(jnp.int32, (side, side), 0)
    lane = lax.broadcasted_iota(jnp.int32, (side, side), 1)
    left, across = rows[:, :side], turned[:side]
    last = sums[1][half : half + 1, :side]
    a = jnp.where(row >= lane, left, across)
    d = jnp.where(row == lane, last, jnp.where(row < lane, left, across))
    return jnp.concatenate(
        [
            jnp.concatenate([a, rows[:, side:]], 1),
            jnp.concatenate([turned[side:], d], 1),
        ],
        0,
    )


def gram_kernel(rows_ref, keep_ref, give_ref, top_ref):
    share = top_ref.shape[0]
    rows = rows_ref[...]
    pack(product(rows, rows, TN), keep_ref, give_ref)
    start = pl.multiple_of(lax.axis_index("col") * share, share)
    top_ref[...] = rows_ref[pl.ds(start, share), :]


def inner_kernel(turned_ref, rows_ref, keep_ref, give_ref):
    terms = product(turned_ref[...], rows_ref[...])
    pack(0.5 * (terms + terms.T), keep_ref, give_ref)


def packed_parts(kernel, operands, extra, name):
    width = operands[-1].shape[1]
    vmem = pl.BlockSpec(memory_space=pltpu.VMEM)
    shapes = [(width // 4 + STEP, width)] * 2 + extra
    return pl.pallas_call(
        kernel,
        in_specs=[vmem] * len(operands),
        out_specs=[vmem] * len(shapes),
        out_shape=[jax.ShapeDtypeStruct(shape, jnp.float32) for shape in shapes],
        cost_estimate=pl.CostEstimate(
            flops=200_000_000, bytes_accessed=3_000_000, transcendentals=0
        ),
        compiler_params=pltpu.CompilerParams(vmem_limit_bytes=8 * MIB),
        name=name,
    )(*operands)


def eliminate(gram, upper_ref, inverse_ref, work, other, beside):
    width = upper_ref.shape[0]
    full = (STEP, width)
    lane = lax.broadcasted_iota(jnp.int32, full, 1)
    work[...] = gram
    other[...] = eye(width)
    for first in range(0, width, STEP):
        beside(first // STEP)
        a_rows = [jnp.broadcast_to(work[first + k : first + k + 1, :], full) for k in range(STEP)]
        x_rows = [jnp.broadcast_to(other[first + k : first + k + 1, :], full) for k in range(STEP)]
        entry, mult, inv = {}, {}, {}
        for i in range(STEP):
            for k in range(i + 1):
                column = a_rows[i][:, first + k : first + k + 1]
                entry[i, k] = jnp.broadcast_to(column, full)
        for k in range(STEP):
            inv[k] = 1.0 / entry[k, k]
            for i in range(k + 1, STEP):
                mult[i, k] = entry[i, k] * inv[k]
            for i in range(k + 1, STEP):
                for l in range(k + 1, i + 1):
                    entry[i, l] = entry[i, l] - mult[i, k] * entry[l, k]
        for i in range(STEP):
            for k in range(i):
                a_rows[i] = a_rows[i] - mult[i, k] * a_rows[k]
                x_rows[i] = x_rows[i] - mult[i, k] * x_rows[k]
        for k in range(STEP):
            root = lax.rsqrt(entry[k, k])
            root = root * (1.5 - 0.5 * entry[k, k] * root * root)
            row = slice(first + k, first + k + 1)
            upper_ref[row, :] = jnp.where(lane >= first + k, a_rows[k] * root, 0.0)[:1]
            inverse_ref[row, :] = (x_rows[k] * root)[:1]
        if first + STEP == width:
            break
        a_back = [a_rows[k] * inv[k] for k in range(STEP)]
        x_back = [x_rows[k] * inv[k] for k in range(STEP)]
        for k in range(STEP - 2, -1, -1):
            for l in range(k + 1, STEP):
                a_back[k] = a_back[k] - mult[l, k] * a_back[l]
                x_back[k] = x_back[k] - mult[l, k] * x_back[l]
        for g in range(first + STEP, width, STEP):
            block = work[g : g + STEP, :]
            a_new, x_new = block, other[g : g + STEP, :]
            for k in range(STEP):
                column = jnp.broadcast_to(block[:, first + k : first + k + 1], full)
                a_new = a_new - column * a_back[k]
                x_new = x_new - column * x_back[k]
            work[g : g + STEP, :] = a_new
            other[g : g + STEP, :] = x_new


def product_kernel(piece, share, parts_ref, mob_ref, upper_ref, inverse_ref, out_ref, *refs):
    work, other, rhs, held, found, sems = refs
    width = parts_ref.shape[2]
    count = sems.shape[0]
    tile = held.shape[0] // count
    loads = []
    for k in range(count):
        rows = pl.ds(k * tile, tile)
        loads.append(pltpu.make_async_copy(mob_ref.at[rows], held.at[rows], sems.at[k]))
        loads[k].start()
    rhs[...] = both_terms(pieces_of(parts_ref, piece))
    last = parts_ref.shape[1] - share
    out_ref[:, piece:, :] = jnp.broadcast_to(
        parts_ref[0, last:, :][None], (out_ref.shape[0], share, width)
    )

    def beside(index):
        k = index // 3 - 1
        if index % 3 or not 0 <= k < count:
            return
        loads[k].wait()
        rows = slice(k * tile, (k + 1) * tile)
        high, low = split(held[rows, :])
        wide = exact_dot(high, rhs[...], NN)
        low_part = exact_dot(low, rhs[:, :width], NN)
        found[rows, :] = wide[:, :width] + wide[:, width:] + low_part

    eliminate(unpack(parts_ref, piece), upper_ref, inverse_ref, work, other, beside)
    image = exact_dot(left_terms(found[...]), right_terms(inverse_ref[...]), NT)
    image = image + jnp.where(lax.axis_index("col") == 0, held[:, :width], 0.0)
    out_ref[:, :piece, :] = image.reshape(out_ref.shape[0], piece, width)


def factor_and_product(parts, mobility, piece, share):
    n_rows, n_cols = mobility.shape
    width = parts.shape[2]
    vmem = pl.BlockSpec(memory_space=pltpu.VMEM)
    square = jax.ShapeDtypeStruct((width, width), jnp.float32)
    mobility = pltpu.with_memory_space_constraint(mobility, pltpu.HBM)
    return pl.pallas_call(
        lambda *refs: product_kernel(piece, share, *refs),
        in_specs=[vmem, pl.BlockSpec(memory_space=pltpu.HBM)],
        out_specs=[vmem] * 3,
        out_shape=(
            square,
            square,
            jax.ShapeDtypeStruct((n_rows // piece, piece + share, width), jnp.float32),
        ),
        scratch_shapes=[
            pltpu.VMEM((width, width), jnp.float32),
            pltpu.VMEM((width, width), jnp.float32),
            pltpu.VMEM((n_cols, 2 * width), jnp.bfloat16),
            pltpu.VMEM(mobility.shape, jnp.float32),
            pltpu.VMEM((n_rows, width), jnp.float32),
            pltpu.SemaphoreType.DMA((4,)),
        ],
        cost_estimate=pl.CostEstimate(
            flops=6 * n_rows * n_cols * width, bytes_accessed=6_000_000, transcendentals=0
        ),
        compiler_params=pltpu.CompilerParams(vmem_limit_bytes=20 * MIB),
        name="factor_and_product",
    )(parts, mobility)


def copy_kernel(rows_ref, out_ref, held, sem):
    load = pltpu.make_async_copy(rows_ref, held, sem)
    load.start()
    load.wait()
    out_ref[...] = jnp.broadcast_to(held[...][None], out_ref.shape)


def copies(rows, count):
    hbm = pl.BlockSpec(memory_space=pltpu.HBM)
    return pl.pallas_call(
        copy_kernel,
        in_specs=[hbm],
        out_specs=pl.BlockSpec(memory_space=pltpu.VMEM),
        out_shape=jax.ShapeDtypeStruct((count,) + rows.shape, rows.dtype),
        scratch_shapes=[pltpu.VMEM(rows.shape, rows.dtype), pltpu.SemaphoreType.DMA],
        cost_estimate=pl.CostEstimate(flops=0, bytes_accessed=600_000, transcendentals=0),
        compiler_params=pltpu.CompilerParams(vmem_limit_bytes=4 * MIB),
        name="copies",
    )(pltpu.with_memory_space_constraint(rows, pltpu.HBM))


def join_kernel(lone_ref, keep_ref, came_ref, mob_ref, out_ref):
    piece = lone_ref.shape[0]
    out_ref[:piece, :] = lone_ref[...]
    out_ref[piece:, :] = keep_ref[...] + came_ref[...]


def join(lone, keep, came, mobility):
    vmem = pl.BlockSpec(memory_space=pltpu.VMEM)
    shape = (lone.shape[0] + keep.shape[0], lone.shape[1])
    return pl.pallas_call(
        join_kernel,
        in_specs=[vmem] * 3 + [pl.BlockSpec(memory_space=pltpu.HBM)],
        out_specs=vmem,
        out_shape=jax.ShapeDtypeStruct(shape, jnp.float32),
        cost_estimate=pl.CostEstimate(flops=0, bytes_accessed=100_000, transcendentals=0),
        compiler_params=pltpu.CompilerParams(vmem_limit_bytes=4 * MIB),
        name="join",
    )(lone, keep, came, pltpu.with_memory_space_constraint(mobility, pltpu.HBM))


def image_kernel(piece, got_ref, image_ref, copies_ref, top_ref):
    image = got_ref[0, :piece, :]
    for k in range(1, got_ref.shape[0]):
        image = image + got_ref[k, :piece, :]
    image_ref[...] = image
    copies_ref[...] = jnp.broadcast_to(image[None], copies_ref.shape)
    top_ref[...] = got_ref[:, piece:, :].reshape(top_ref.shape)


def image_piece(got, piece):
    count, _, width = got.shape
    vmem = pl.BlockSpec(memory_space=pltpu.VMEM)
    return pl.pallas_call(
        lambda *refs: image_kernel(piece, *refs),
        in_specs=[vmem],
        out_specs=[vmem] * 3,
        out_shape=(
            jax.ShapeDtypeStruct((piece, width), jnp.float32),
            jax.ShapeDtypeStruct((count, piece, width), jnp.float32),
            jax.ShapeDtypeStruct((width, width), jnp.float32),
        ),
        cost_estimate=pl.CostEstimate(
            flops=10_000_000, bytes_accessed=2_000_000, transcendentals=0
        ),
        compiler_params=pltpu.CompilerParams(vmem_limit_bytes=6 * MIB),
        name="image_piece",
    )(got)


def rows_kernel(rows_ref, inverse_ref, turned_ref):
    rows = exact_dot(left_terms(rows_ref[...]), right_terms(inverse_ref[...]), NT)
    turned_ref[...] = (rows + unit_rows(lax.axis_index("row"), rows.shape)).T


def kernel_kernel(piece, inverse_ref, top_ref, turned_ref, parts_ref, *outs):
    cols_out, rows_left, state_ref = outs
    width = inverse_ref.shape[0]
    identity = eye(width)
    ratio = -product(inverse_ref[...], top_ref[...], NT)
    state_ref[:width, :] = ratio
    state_ref[width:, :] = identity

    def go_on(state):
        return jnp.logical_and(state[0] < 40, state[1] > 1e-10)

    def double(state):
        power = state_ref[:width, :]
        both = product(state_ref[...], power)
        state_ref[:width, :] = both[:width]
        state_ref[width:, :] = state_ref[width:, :] + both[width:]
        return state[0] + 1, jnp.max(jnp.abs(both[:width]))

    lax.while_loop(go_on, double, (0, jnp.max(jnp.abs(ratio))))
    total = state_ref[width:, :]
    kernel = total + product(total, identity - product(identity - ratio, total))
    kernel_terms = right_terms(kernel)
    cols = exact_dot(
        left_terms(pieces_of(parts_ref, piece)), right_terms(inverse_ref[...]), NT
    )
    cols = cols + unit_rows(lax.axis_index("col"), cols.shape)
    cols_out[...] = both_terms(exact_dot(left_terms(cols), kernel_terms, NT))
    rows_left[...] = both_terms(exact_dot(left_terms(turned_ref[...].T), kernel_terms, NT))


def side_call(kernel, operands, shapes, scratch, name):
    vmem = pl.BlockSpec(memory_space=pltpu.VMEM)
    return pl.pallas_call(
        kernel,
        in_specs=[vmem] * len(operands),
        out_specs=[vmem] * len(shapes),
        out_shape=shapes,
        scratch_shapes=scratch,
        cost_estimate=pl.CostEstimate(
            flops=300_000_000, bytes_accessed=10_000_000, transcendentals=0
        ),
        compiler_params=pltpu.CompilerParams(vmem_limit_bytes=14 * MIB),
        name=name,
    )(*operands)


def update_kernel(piece, *refs):
    parts_ref, image_ref, cols_ref, rows_left, mob_ref = refs[:5]
    out_ref, lhs, rhs, held, sems = refs[5:]
    count = sems.shape[0]
    tile = held.shape[0] // count
    middle = lhs.shape[1] // 2
    lhs[:, :middle] = left_terms(image_ref[...])
    lhs[:, middle:] = to_left(rows_left[...])
    small = right_terms(unpack(parts_ref, piece))
    change = exact_dot(to_left(cols_ref[...]), small, NT)
    rhs[:middle, :] = to_right(cols_ref[...]).T
    rhs[middle:, :] = right_terms(pieces_of(parts_ref, piece) - change).T
    stores = []
    for k in range(count):
        rows = pl.ds(k * tile, tile)
        held[rows, :] = mob_ref[rows, :] - exact_dot(lhs[rows, :], rhs[...], NN)
        stores.append(pltpu.make_async_copy(held.at[rows], out_ref.at[rows], sems.at[k]))
        stores[k].start()
    for k in range(count):
        stores[k].wait()


def update(operands, mobility, piece):
    n_rows, n_cols = mobility.shape
    terms = 3 * operands[-1].shape[1]
    vmem = pl.BlockSpec(memory_space=pltpu.VMEM)
    hbm = pl.BlockSpec(memory_space=pltpu.HBM)
    return pl.pallas_call(
        lambda *refs: update_kernel(piece, *refs),
        in_specs=[vmem] * (len(operands) + 1),
        out_specs=hbm,
        out_shape=pltpu.HBM(mobility.shape, jnp.float32),
        scratch_shapes=[
            pltpu.VMEM((n_rows, terms), jnp.bfloat16),
            pltpu.VMEM((terms, n_cols), jnp.bfloat16),
            pltpu.VMEM(mobility.shape, jnp.float32),
            pltpu.SemaphoreType.DMA((4,)),
        ],
        cost_estimate=pl.CostEstimate(
            flops=2 * n_rows * n_cols * terms, bytes_accessed=9_000_000, transcendentals=0
        ),
        compiler_params=pltpu.CompilerParams(vmem_limit_bytes=20 * MIB),
        name="update",
    )(*operands, mobility)


def on_device(panel, mobility):
    piece, width = panel.shape
    n_row, n_col = lax.axis_size("row"), lax.axis_size("col")
    block_rows, block_cols = mobility.shape
    share = width // n_col
    transposing = [(i * n_col + j, j * n_col + i) for i in range(n_row) for j in range(n_col)]
    swap = [(i, i ^ 1) for i in range(n_row)]

    turned_panel = lax.ppermute(panel, BOTH, transposing)
    panel_rows = lax.all_to_all(copies(panel, n_col), "col", 0, 0).reshape(block_rows, width)
    panel_rows, turned_panel = lax.optimization_barrier((panel_rows, turned_panel))
    keep, give, top_part = packed_parts(
        gram_kernel, (panel_rows,), [(share, width)], "gram_parts"
    )
    packed = keep + lax.ppermute(give, "row", swap)
    even = lax.axis_index("row") % 2 == 0
    tail = jnp.where(even, top_part, packed[-STEP:])
    sent = jnp.concatenate([turned_panel, packed[:-STEP], tail], 0)
    panel_parts = lax.all_gather(sent, "row", axis=0)

    panel_factor, inverse, sent = factor_and_product(panel_parts, mobility, piece, share)
    got = lax.all_to_all(sent, "col", 0, 0)
    wide = jax.ShapeDtypeStruct((block_rows, 2 * width), jnp.bfloat16)
    tall = jax.ShapeDtypeStruct((width, block_rows), jnp.float32)
    (turned_rows,) = side_call(rows_kernel, (panel_rows, inverse), [tall], [], "basis_rows")
    got, turned_rows = lax.optimization_barrier((got, turned_rows))
    image, image_copies, top_rows = image_piece(got, piece)
    turned_image = lax.ppermute(image, BOTH, transposing)
    image_rows = lax.all_to_all(image_copies, "col", 0, 0).reshape(block_rows, width)
    cols_right, rows_left = side_call(
        lambda *refs: kernel_kernel(piece, *refs),
        (inverse, top_rows, turned_rows, panel_parts),
        [wide, wide],
        [pltpu.VMEM((2 * width, width), jnp.float32)],
        "kernel",
    )
    image_rows, turned_image, rows_left = lax.optimization_barrier(
        (image_rows, turned_image, rows_left)
    )
    keep, give = packed_parts(inner_kernel, (turned_rows, image_rows), [], "inner_parts")
    came = lax.ppermute(give, "row", swap)
    image_parts = lax.all_gather(join(turned_image, keep, came, mobility), "row", axis=0)
    operands = (image_parts, image_rows, cols_right, rows_left)
    updated = update(operands, mobility, piece)
    return (updated, panel_factor)


def solution(mesh):
    in_specs = (P(("row", "col"), None), P("row", "col"))
    out_specs = (P("row", "col"), P())
    return jax.shard_map(
        on_device, mesh=mesh, in_specs=in_specs, out_specs=out_specs, check_vma=False
    )
```

```python
import jax
import jax.numpy as jnp
from jax import lax
from jax.experimental import pallas as pl
from jax.experimental.pallas import tpu as pltpu
from jax.sharding import PartitionSpec as P

BOTH = ("row", "col")
STEP = 8
MIB = 1 << 20
NN = (((1,), (0,)), ((), ()))
TN = (((0,), (0,)), ((), ()))
NT = (((1,), (1,)), ((), ()))


def product(first_op, second_op, dims=NN):
    return lax.dot_general(
        first_op,
        second_op,
        dims,
        precision=lax.Precision.HIGHEST,
        preferred_element_type=jnp.float32,
    )


def split(value):
    high = value.astype(jnp.bfloat16)
    return high, (value - high.astype(jnp.float32)).astype(jnp.bfloat16)


def both_terms(value):
    return jnp.concatenate(split(value), 1)


def left_terms(value):
    high, low = split(value)
    return jnp.concatenate([high, low, high], 1)


def right_terms(value):
    high, low = split(value)
    return jnp.concatenate([high, high, low], 1)


def to_left(pair):
    return jnp.concatenate([pair, pair[:, : pair.shape[1] // 2]], 1)


def to_right(pair):
    return jnp.concatenate([pair[:, : pair.shape[1] // 2], pair], 1)


def exact_dot(first_op, second_op, dims):
    return lax.dot_general(first_op, second_op, dims, preferred_element_type=jnp.float32)


def unit_rows(index, shape):
    rows = lax.broadcasted_iota(jnp.int32, shape, 0) + index * shape[0]
    return jnp.where(rows == lax.broadcasted_iota(jnp.int32, shape, 1), 1.0, 0.0)


def eye(width):
    return unit_rows(0, (width, width))


def pieces_of(parts_ref, piece):
    count, _, width = parts_ref.shape
    return parts_ref[:, :piece, :].reshape(count * piece, width)


def pack(value, keep_ref, give_ref):
    side = value.shape[0] // 2
    half = side // 2
    top = value[:side]
    low = pltpu.roll(value[side:], side, 1)
    row = lax.broadcasted_iota(jnp.int32, top.shape, 0)
    lane = lax.broadcasted_iota(jnp.int32, top.shape, 1)
    rows = jnp.where(jnp.logical_and(row < lane, lane < side), low, top)
    last = jnp.sum(jnp.where(row == lane, low, 0.0), axis=0, keepdims=True)
    even = lax.rem(lax.axis_index("row"), 2) == 0
    keep_ref[:half, :] = jnp.where(even, rows[:half], rows[half:])
    give_ref[:half, :] = jnp.where(even, rows[half:], rows[:half])
    keep_ref[half:, :] = jnp.broadcast_to(last, (STEP, last.shape[1]))
    give_ref[half:, :] = jnp.broadcast_to(last, (STEP, last.shape[1]))


def unpack(parts_ref, piece):
    half = parts_ref.shape[2] // 4
    stop = piece + half
    sums = [parts_ref[0, piece:stop, :], parts_ref[1, piece : stop + STEP, :]]
    for i in range(2, parts_ref.shape[0], 2):
        sums[0] = sums[0] + parts_ref[i, piece:stop, :]
        sums[1] = sums[1] + parts_ref[i + 1, piece : stop + STEP, :]
    side = 2 * half
    rows = jnp.concatenate([sums[0], sums[1][:half]], 0)
    turned = rows.T
    row = lax.broadcasted_iota(jnp.int32, (side, side), 0)
    lane = lax.broadcasted_iota(jnp.int32, (side, side), 1)
    left, across = rows[:, :side], turned[:side]
    last = sums[1][half : half + 1, :side]
    a = jnp.where(row >= lane, left, across)
    d = jnp.where(row == lane, last, jnp.where(row < lane, left, across))
    return jnp.concatenate(
        [
            jnp.concatenate([a, rows[:, side:]], 1),
            jnp.concatenate([turned[side:], d], 1),
        ],
        0,
    )


def gram_kernel(rows_ref, keep_ref, give_ref, top_ref):
    share = top_ref.shape[0]
    rows = rows_ref[...]
    pack(product(rows, rows, TN), keep_ref, give_ref)
    start = pl.multiple_of(lax.axis_index("col") * share, share)
    top_ref[...] = rows_ref[pl.ds(start, share), :]


def inner_kernel(turned_ref, rows_ref, keep_ref, give_ref):
    terms = product(turned_ref[...], rows_ref[...])
    pack(0.5 * (terms + terms.T), keep_ref, give_ref)


def packed_parts(kernel, operands, extra, name):
    width = operands[-1].shape[1]
    vmem = pl.BlockSpec(memory_space=pltpu.VMEM)
    shapes = [(width // 4 + STEP, width)] * 2 + extra
    return pl.pallas_call(
        kernel,
        in_specs=[vmem] * len(operands),
        out_specs=[vmem] * len(shapes),
        out_shape=[jax.ShapeDtypeStruct(shape, jnp.float32) for shape in shapes],
        cost_estimate=pl.CostEstimate(
            flops=1_000, bytes_accessed=1_000, transcendentals=0
        ),
        compiler_params=pltpu.CompilerParams(vmem_limit_bytes=8 * MIB),
        name=name,
    )(*operands)


def eliminate(gram, upper_ref, inverse_ref, work, other, beside):
    width = upper_ref.shape[0]
    full = (STEP, width)
    lane = lax.broadcasted_iota(jnp.int32, full, 1)
    work[...] = gram
    other[...] = eye(width)
    for first in range(0, width, STEP):
        beside(first // STEP)
        a_rows = [jnp.broadcast_to(work[first + k : first + k + 1, :], full) for k in range(STEP)]
        x_rows = [jnp.broadcast_to(other[first + k : first + k + 1, :], full) for k in range(STEP)]
        entry, mult, inv = {}, {}, {}
        for i in range(STEP):
            for k in range(i + 1):
                column = a_rows[i][:, first + k : first + k + 1]
                entry[i, k] = jnp.broadcast_to(column, full)
        for k in range(STEP):
            inv[k] = 1.0 / entry[k, k]
            for i in range(k + 1, STEP):
                mult[i, k] = entry[i, k] * inv[k]
            for i in range(k + 1, STEP):
                for l in range(k + 1, i + 1):
                    entry[i, l] = entry[i, l] - mult[i, k] * entry[l, k]
        for i in range(STEP):
            for k in range(i):
                a_rows[i] = a_rows[i] - mult[i, k] * a_rows[k]
                x_rows[i] = x_rows[i] - mult[i, k] * x_rows[k]
        for k in range(STEP):
            root = lax.rsqrt(entry[k, k])
            root = root * (1.5 - 0.5 * entry[k, k] * root * root)
            row = slice(first + k, first + k + 1)
            upper_ref[row, :] = jnp.where(lane >= first + k, a_rows[k] * root, 0.0)[:1]
            inverse_ref[row, :] = (x_rows[k] * root)[:1]
        if first + STEP == width:
            break
        a_back = [a_rows[k] * inv[k] for k in range(STEP)]
        x_back = [x_rows[k] * inv[k] for k in range(STEP)]
        for k in range(STEP - 2, -1, -1):
            for l in range(k + 1, STEP):
                a_back[k] = a_back[k] - mult[l, k] * a_back[l]
                x_back[k] = x_back[k] - mult[l, k] * x_back[l]
        for g in range(first + STEP, width, STEP):
            block = work[g : g + STEP, :]
            a_new, x_new = block, other[g : g + STEP, :]
            for k in range(STEP):
                column = jnp.broadcast_to(block[:, first + k : first + k + 1], full)
                a_new = a_new - column * a_back[k]
                x_new = x_new - column * x_back[k]
            work[g : g + STEP, :] = a_new
            other[g : g + STEP, :] = x_new


def product_kernel(piece, share, parts_ref, mob_ref, upper_ref, inverse_ref, out_ref, *refs):
    work, other, rhs, held, found, sems = refs
    width = parts_ref.shape[2]
    count = sems.shape[0]
    tile = held.shape[0] // count
    loads = []
    for k in range(count):
        rows = pl.ds(k * tile, tile)
        loads.append(pltpu.make_async_copy(mob_ref.at[rows], held.at[rows], sems.at[k]))
        loads[k].start()
    rhs[...] = both_terms(pieces_of(parts_ref, piece))
    last = parts_ref.shape[1] - share
    out_ref[:, piece:, :] = jnp.broadcast_to(
        parts_ref[0, last:, :][None], (out_ref.shape[0], share, width)
    )

    def beside(index):
        k = index // 3 - 1
        if index % 3 or not 0 <= k < count:
            return
        loads[k].wait()
        rows = slice(k * tile, (k + 1) * tile)
        high, low = split(held[rows, :])
        wide = exact_dot(high, rhs[...], NN)
        low_part = exact_dot(low, rhs[:, :width], NN)
        found[rows, :] = wide[:, :width] + wide[:, width:] + low_part

    eliminate(unpack(parts_ref, piece), upper_ref, inverse_ref, work, other, beside)
    image = exact_dot(left_terms(found[...]), right_terms(inverse_ref[...]), NT)
    image = image + jnp.where(lax.axis_index("col") == 0, held[:, :width], 0.0)
    out_ref[:, :piece, :] = image.reshape(out_ref.shape[0], piece, width)


def factor_and_product(parts, mobility, piece, share):
    n_rows, n_cols = mobility.shape
    width = parts.shape[2]
    vmem = pl.BlockSpec(memory_space=pltpu.VMEM)
    square = jax.ShapeDtypeStruct((width, width), jnp.float32)
    mobility = pltpu.with_memory_space_constraint(mobility, pltpu.HBM)
    return pl.pallas_call(
        lambda *refs: product_kernel(piece, share, *refs),
        in_specs=[vmem, pl.BlockSpec(memory_space=pltpu.HBM)],
        out_specs=[vmem] * 3,
        out_shape=(
            square,
            square,
            jax.ShapeDtypeStruct((n_rows // piece, piece + share, width), jnp.float32),
        ),
        scratch_shapes=[
            pltpu.VMEM((width, width), jnp.float32),
            pltpu.VMEM((width, width), jnp.float32),
            pltpu.VMEM((n_cols, 2 * width), jnp.bfloat16),
            pltpu.VMEM(mobility.shape, jnp.float32),
            pltpu.VMEM((n_rows, width), jnp.float32),
            pltpu.SemaphoreType.DMA((4,)),
        ],
        cost_estimate=pl.CostEstimate(
            flops=6 * n_rows * n_cols * width, bytes_accessed=6_000_000, transcendentals=0
        ),
        compiler_params=pltpu.CompilerParams(vmem_limit_bytes=20 * MIB),
        name="factor_and_product",
    )(parts, mobility)


def copy_kernel(rows_ref, out_ref, held, sem):
    load = pltpu.make_async_copy(rows_ref, held, sem)
    load.start()
    load.wait()
    out_ref[...] = jnp.broadcast_to(held[...][None], out_ref.shape)


def copies(rows, count):
    hbm = pl.BlockSpec(memory_space=pltpu.HBM)
    return pl.pallas_call(
        copy_kernel,
        in_specs=[hbm],
        out_specs=pl.BlockSpec(memory_space=pltpu.VMEM),
        out_shape=jax.ShapeDtypeStruct((count,) + rows.shape, rows.dtype),
        scratch_shapes=[pltpu.VMEM(rows.shape, rows.dtype), pltpu.SemaphoreType.DMA],
        cost_estimate=pl.CostEstimate(flops=0, bytes_accessed=600_000, transcendentals=0),
        compiler_params=pltpu.CompilerParams(vmem_limit_bytes=4 * MIB),
        name="copies",
    )(pltpu.with_memory_space_constraint(rows, pltpu.HBM))


def join_kernel(lone_ref, keep_ref, came_ref, mob_ref, out_ref):
    piece = lone_ref.shape[0]
    out_ref[:piece, :] = lone_ref[...]
    out_ref[piece:, :] = keep_ref[...] + came_ref[...]


def join(lone, keep, came, mobility):
    vmem = pl.BlockSpec(memory_space=pltpu.VMEM)
    shape = (lone.shape[0] + keep.shape[0], lone.shape[1])
    return pl.pallas_call(
        join_kernel,
        in_specs=[vmem] * 3 + [pl.BlockSpec(memory_space=pltpu.HBM)],
        out_specs=vmem,
        out_shape=jax.ShapeDtypeStruct(shape, jnp.float32),
        cost_estimate=pl.CostEstimate(flops=0, bytes_accessed=100_000, transcendentals=0),
        compiler_params=pltpu.CompilerParams(vmem_limit_bytes=4 * MIB),
        name="join",
    )(lone, keep, came, pltpu.with_memory_space_constraint(mobility, pltpu.HBM))


def image_kernel(piece, got_ref, image_ref, copies_ref, top_ref):
    image = got_ref[0, :piece, :]
    for k in range(1, got_ref.shape[0]):
        image = image + got_ref[k, :piece, :]
    image_ref[...] = image
    copies_ref[...] = jnp.broadcast_to(image[None], copies_ref.shape)
    top_ref[...] = got_ref[:, piece:, :].reshape(top_ref.shape)


def image_piece(got, piece):
    count, _, width = got.shape
    vmem = pl.BlockSpec(memory_space=pltpu.VMEM)
    return pl.pallas_call(
        lambda *refs: image_kernel(piece, *refs),
        in_specs=[vmem],
        out_specs=[vmem] * 3,
        out_shape=(
            jax.ShapeDtypeStruct((piece, width), jnp.float32),
            jax.ShapeDtypeStruct((count, piece, width), jnp.float32),
            jax.ShapeDtypeStruct((width, width), jnp.float32),
        ),
        cost_estimate=pl.CostEstimate(
            flops=10_000_000, bytes_accessed=2_000_000, transcendentals=0
        ),
        compiler_params=pltpu.CompilerParams(vmem_limit_bytes=6 * MIB),
        name="image_piece",
    )(got)


def rows_kernel(rows_ref, inverse_ref, turned_ref):
    rows = exact_dot(left_terms(rows_ref[...]), right_terms(inverse_ref[...]), NT)
    turned_ref[...] = (rows + unit_rows(lax.axis_index("row"), rows.shape)).T


def kernel_kernel(piece, inverse_ref, top_ref, turned_ref, parts_ref, *outs):
    cols_out, rows_left, state_ref = outs
    width = inverse_ref.shape[0]
    identity = eye(width)
    ratio = -product(inverse_ref[...], top_ref[...], NT)
    state_ref[:width, :] = ratio
    state_ref[width:, :] = identity

    def go_on(state):
        return jnp.logical_and(state[0] < 40, state[1] > 1e-10)

    def double(state):
        power = state_ref[:width, :]
        both = product(state_ref[...], power)
        state_ref[:width, :] = both[:width]
        state_ref[width:, :] = state_ref[width:, :] + both[width:]
        return state[0] + 1, jnp.max(jnp.abs(both[:width]))

    lax.while_loop(go_on, double, (0, jnp.max(jnp.abs(ratio))))
    total = state_ref[width:, :]
    kernel = total + product(total, identity - product(identity - ratio, total))
    kernel_terms = right_terms(kernel)
    cols = exact_dot(
        left_terms(pieces_of(parts_ref, piece)), right_terms(inverse_ref[...]), NT
    )
    cols = cols + unit_rows(lax.axis_index("col"), cols.shape)
    cols_out[...] = both_terms(exact_dot(left_terms(cols), kernel_terms, NT))
    rows_left[...] = both_terms(exact_dot(left_terms(turned_ref[...].T), kernel_terms, NT))


def side_call(kernel, operands, shapes, scratch, name):
    vmem = pl.BlockSpec(memory_space=pltpu.VMEM)
    return pl.pallas_call(
        kernel,
        in_specs=[vmem] * len(operands),
        out_specs=[vmem] * len(shapes),
        out_shape=shapes,
        scratch_shapes=scratch,
        cost_estimate=pl.CostEstimate(
            flops=300_000_000, bytes_accessed=10_000_000, transcendentals=0
        ),
        compiler_params=pltpu.CompilerParams(vmem_limit_bytes=14 * MIB),
        name=name,
    )(*operands)


def update_kernel(piece, *refs):
    parts_ref, image_ref, cols_ref, rows_left, mob_ref = refs[:5]
    out_ref, lhs, rhs, held, sems = refs[5:]
    count = sems.shape[0]
    tile = held.shape[0] // count
    middle = lhs.shape[1] // 2
    lhs[:, :middle] = left_terms(image_ref[...])
    lhs[:, middle:] = to_left(rows_left[...])
    small = right_terms(unpack(parts_ref, piece))
    change = exact_dot(to_left(cols_ref[...]), small, NT)
    rhs[:middle, :] = to_right(cols_ref[...]).T
    rhs[middle:, :] = right_terms(pieces_of(parts_ref, piece) - change).T
    stores = []
    for k in range(count):
        rows = pl.ds(k * tile, tile)
        held[rows, :] = mob_ref[rows, :] - exact_dot(lhs[rows, :], rhs[...], NN)
        stores.append(pltpu.make_async_copy(held.at[rows], out_ref.at[rows], sems.at[k]))
        stores[k].start()
    for k in range(count):
        stores[k].wait()


def update(operands, mobility, piece):
    n_rows, n_cols = mobility.shape
    terms = 3 * operands[-1].shape[1]
    vmem = pl.BlockSpec(memory_space=pltpu.VMEM)
    hbm = pl.BlockSpec(memory_space=pltpu.HBM)
    return pl.pallas_call(
        lambda *refs: update_kernel(piece, *refs),
        in_specs=[vmem] * (len(operands) + 1),
        out_specs=hbm,
        out_shape=pltpu.HBM(mobility.shape, jnp.float32),
        scratch_shapes=[
            pltpu.VMEM((n_rows, terms), jnp.bfloat16),
            pltpu.VMEM((terms, n_cols), jnp.bfloat16),
            pltpu.VMEM(mobility.shape, jnp.float32),
            pltpu.SemaphoreType.DMA((4,)),
        ],
        cost_estimate=pl.CostEstimate(
            flops=2 * n_rows * n_cols * terms, bytes_accessed=9_000_000, transcendentals=0
        ),
        compiler_params=pltpu.CompilerParams(vmem_limit_bytes=20 * MIB),
        name="update",
    )(*operands, mobility)


def on_device(panel, mobility):
    piece, width = panel.shape
    n_row, n_col = lax.axis_size("row"), lax.axis_size("col")
    block_rows, block_cols = mobility.shape
    share = width // n_col
    transposing = [(i * n_col + j, j * n_col + i) for i in range(n_row) for j in range(n_col)]
    swap = [(i, i ^ 1) for i in range(n_row)]

    turned_panel = lax.ppermute(panel, BOTH, transposing)
    panel_rows = lax.all_to_all(copies(panel, n_col), "col", 0, 0).reshape(block_rows, width)
    keep, give, top_part = packed_parts(
        gram_kernel, (panel_rows,), [(share, width)], "gram_parts"
    )
    give, turned_panel = lax.optimization_barrier((give, turned_panel))
    packed = keep + lax.ppermute(give, "row", swap)
    even = lax.axis_index("row") % 2 == 0
    tail = jnp.where(even, top_part, packed[-STEP:])
    sent = jnp.concatenate([turned_panel, packed[:-STEP], tail], 0)
    panel_parts = lax.all_gather(sent, "row", axis=0)

    panel_factor, inverse, sent = factor_and_product(panel_parts, mobility, piece, share)
    got = lax.all_to_all(sent, "col", 0, 0)
    wide = jax.ShapeDtypeStruct((block_rows, 2 * width), jnp.bfloat16)
    tall = jax.ShapeDtypeStruct((width, block_rows), jnp.float32)
    (turned_rows,) = side_call(rows_kernel, (panel_rows, inverse), [tall], [], "basis_rows")
    got, turned_rows = lax.optimization_barrier((got, turned_rows))
    image, image_copies, top_rows = image_piece(got, piece)
    turned_image = lax.ppermute(image, BOTH, transposing)
    image_rows = lax.all_to_all(image_copies, "col", 0, 0).reshape(block_rows, width)
    cols_right, rows_left = side_call(
        lambda *refs: kernel_kernel(piece, *refs),
        (inverse, top_rows, turned_rows, panel_parts),
        [wide, wide],
        [pltpu.VMEM((2 * width, width), jnp.float32)],
        "kernel",
    )
    image_rows, rows_left = lax.optimization_barrier((image_rows, rows_left))
    keep, give = packed_parts(inner_kernel, (turned_rows, image_rows), [], "inner_parts")
    came = lax.ppermute(give, "row", swap)
    image_parts = lax.all_gather(join(turned_image, keep, came, mobility), "row", axis=0)
    operands = (image_parts, image_rows, cols_right, rows_left)
    updated = update(operands, mobility, piece)
    return (updated, panel_factor)


def solution(mesh):
    in_specs = (P(("row", "col"), None), P("row", "col"))
    out_specs = (P("row", "col"), P())
    return jax.shard_map(
        on_device, mesh=mesh, in_specs=in_specs, out_specs=out_specs, check_vma=False
    )
```

```python
import jax
import jax.numpy as jnp
from jax import lax
from jax.experimental import pallas as pl
from jax.experimental.pallas import tpu as pltpu
from jax.sharding import PartitionSpec as P

BOTH = ("row", "col")
STEP = 8
MIB = 1 << 20
NN = (((1,), (0,)), ((), ()))
TN = (((0,), (0,)), ((), ()))
NT = (((1,), (1,)), ((), ()))


def product(first_op, second_op, dims=NN):
    return lax.dot_general(
        first_op,
        second_op,
        dims,
        precision=lax.Precision.HIGHEST,
        preferred_element_type=jnp.float32,
    )


def split(value):
    high = value.astype(jnp.bfloat16)
    return high, (value - high.astype(jnp.float32)).astype(jnp.bfloat16)


def both_terms(value):
    return jnp.concatenate(split(value), 1)


def left_terms(value):
    high, low = split(value)
    return jnp.concatenate([high, low, high], 1)


def right_terms(value):
    high, low = split(value)
    return jnp.concatenate([high, high, low], 1)


def to_left(pair):
    return jnp.concatenate([pair, pair[:, : pair.shape[1] // 2]], 1)


def to_right(pair):
    return jnp.concatenate([pair[:, : pair.shape[1] // 2], pair], 1)


def exact_dot(first_op, second_op, dims):
    return lax.dot_general(first_op, second_op, dims, preferred_element_type=jnp.float32)


def unit_rows(index, shape):
    rows = lax.broadcasted_iota(jnp.int32, shape, 0) + index * shape[0]
    return jnp.where(rows == lax.broadcasted_iota(jnp.int32, shape, 1), 1.0, 0.0)


def eye(width):
    return unit_rows(0, (width, width))


def pieces_of(parts_ref, piece):
    count, _, width = parts_ref.shape
    return parts_ref[:, :piece, :].reshape(count * piece, width)


def pack(value, keep_ref, give_ref):
    side = value.shape[0] // 2
    half = side // 2
    top = value[:side]
    low = pltpu.roll(value[side:], side, 1)
    row = lax.broadcasted_iota(jnp.int32, top.shape, 0)
    lane = lax.broadcasted_iota(jnp.int32, top.shape, 1)
    rows = jnp.where(jnp.logical_and(row < lane, lane < side), low, top)
    last = jnp.sum(jnp.where(row == lane, low, 0.0), axis=0, keepdims=True)
    even = lax.rem(lax.axis_index("row"), 2) == 0
    keep_ref[:half, :] = jnp.where(even, rows[:half], rows[half:])
    give_ref[:half, :] = jnp.where(even, rows[half:], rows[:half])
    keep_ref[half:, :] = jnp.broadcast_to(last, (STEP, last.shape[1]))
    give_ref[half:, :] = jnp.broadcast_to(last, (STEP, last.shape[1]))


def unpack(parts_ref, piece):
    half = parts_ref.shape[2] // 4
    stop = piece + half
    sums = [parts_ref[0, piece:stop, :], parts_ref[1, piece : stop + STEP, :]]
    for i in range(2, parts_ref.shape[0], 2):
        sums[0] = sums[0] + parts_ref[i, piece:stop, :]
        sums[1] = sums[1] + parts_ref[i + 1, piece : stop + STEP, :]
    side = 2 * half
    rows = jnp.concatenate([sums[0], sums[1][:half]], 0)
    turned = rows.T
    row = lax.broadcasted_iota(jnp.int32, (side, side), 0)
    lane = lax.broadcasted_iota(jnp.int32, (side, side), 1)
    left, across = rows[:, :side], turned[:side]
    last = sums[1][half : half + 1, :side]
    a = jnp.where(row >= lane, left, across)
    d = jnp.where(row == lane, last, jnp.where(row < lane, left, across))
    return jnp.concatenate(
        [
            jnp.concatenate([a, rows[:, side:]], 1),
            jnp.concatenate([turned[side:], d], 1),
        ],
        0,
    )


def gram_kernel(rows_ref, keep_ref, give_ref, top_ref):
    share = top_ref.shape[0]
    rows = rows_ref[...]
    pack(product(rows, rows, TN), keep_ref, give_ref)
    start = pl.multiple_of(lax.axis_index("col") * share, share)
    top_ref[...] = rows_ref[pl.ds(start, share), :]


def inner_kernel(turned_ref, rows_ref, keep_ref, give_ref):
    terms = product(turned_ref[...], rows_ref[...])
    pack(0.5 * (terms + terms.T), keep_ref, give_ref)


def packed_parts(kernel, operands, extra, name):
    width = operands[-1].shape[1]
    vmem = pl.BlockSpec(memory_space=pltpu.VMEM)
    shapes = [(width // 4 + STEP, width)] * 2 + extra
    return pl.pallas_call(
        kernel,
        in_specs=[vmem] * len(operands),
        out_specs=[vmem] * len(shapes),
        out_shape=[jax.ShapeDtypeStruct(shape, jnp.float32) for shape in shapes],
        cost_estimate=pl.CostEstimate(
            flops=1_000, bytes_accessed=1_000, transcendentals=0
        ),
        compiler_params=pltpu.CompilerParams(vmem_limit_bytes=8 * MIB),
        name=name,
    )(*operands)


def eliminate(gram, upper_ref, inverse_ref, work, other, stash, beside):
    width = upper_ref.shape[0]
    full = (STEP, width)
    lane = lax.broadcasted_iota(jnp.int32, full, 1)
    work[...] = gram
    other[...] = eye(width)
    for first in range(0, width, STEP):
        beside(first // STEP)
        a_rows = [jnp.broadcast_to(work[first + k : first + k + 1, :], full) for k in range(STEP)]
        x_rows = [jnp.broadcast_to(other[first + k : first + k + 1, :], full) for k in range(STEP)]
        entry, mult, inv = {}, {}, {}
        pivot = work[first : first + STEP, :]
        for k in range(STEP):
            stash[k] = jnp.broadcast_to(pivot[:, first + k : first + k + 1], full)
        for i in range(STEP):
            for k in range(i + 1):
                entry[i, k] = jnp.broadcast_to(stash[k, i : i + 1, :], full)
        for k in range(STEP):
            inv[k] = 1.0 / entry[k, k]
            for i in range(k + 1, STEP):
                mult[i, k] = entry[i, k] * inv[k]
            for i in range(k + 1, STEP):
                for l in range(k + 1, i + 1):
                    entry[i, l] = entry[i, l] - mult[i, k] * entry[l, k]
        for i in range(STEP):
            for k in range(i):
                a_rows[i] = a_rows[i] - mult[i, k] * a_rows[k]
                x_rows[i] = x_rows[i] - mult[i, k] * x_rows[k]
        for k in range(STEP):
            root = lax.rsqrt(entry[k, k])
            root = root * (1.5 - 0.5 * entry[k, k] * root * root)
            row = slice(first + k, first + k + 1)
            upper_ref[row, :] = jnp.where(lane >= first + k, a_rows[k] * root, 0.0)[:1]
            inverse_ref[row, :] = (x_rows[k] * root)[:1]
        if first + STEP == width:
            break
        a_back = [a_rows[k] * inv[k] for k in range(STEP)]
        x_back = [x_rows[k] * inv[k] for k in range(STEP)]
        for k in range(STEP - 2, -1, -1):
            for l in range(k + 1, STEP):
                a_back[k] = a_back[k] - mult[l, k] * a_back[l]
                x_back[k] = x_back[k] - mult[l, k] * x_back[l]
        for g in range(first + STEP, width, STEP):
            block = work[g : g + STEP, :]
            a_new, x_new = block, other[g : g + STEP, :]
            for k in range(STEP):
                column = jnp.broadcast_to(block[:, first + k : first + k + 1], full)
                a_new = a_new - column * a_back[k]
                x_new = x_new - column * x_back[k]
            work[g : g + STEP, :] = a_new
            other[g : g + STEP, :] = x_new


def product_kernel(piece, share, parts_ref, mob_ref, upper_ref, inverse_ref, out_ref, *refs):
    work, other, stash, rhs, held, found, sems = refs
    width = parts_ref.shape[2]
    count = sems.shape[0]
    tile = held.shape[0] // count
    loads = []
    for k in range(count):
        rows = pl.ds(k * tile, tile)
        loads.append(pltpu.make_async_copy(mob_ref.at[rows], held.at[rows], sems.at[k]))
        loads[k].start()
    rhs[...] = both_terms(pieces_of(parts_ref, piece))
    last = parts_ref.shape[1] - share
    out_ref[:, piece:, :] = jnp.broadcast_to(
        parts_ref[0, last:, :][None], (out_ref.shape[0], share, width)
    )

    def beside(index):
        k = index // 3 - 1
        if index % 3 or not 0 <= k < count:
            return
        loads[k].wait()
        rows = slice(k * tile, (k + 1) * tile)
        high, low = split(held[rows, :])
        wide = exact_dot(high, rhs[...], NN)
        low_part = exact_dot(low, rhs[:, :width], NN)
        found[rows, :] = wide[:, :width] + wide[:, width:] + low_part

    eliminate(unpack(parts_ref, piece), upper_ref, inverse_ref, work, other, stash, beside)
    image = exact_dot(left_terms(found[...]), right_terms(inverse_ref[...]), NT)
    image = image + jnp.where(lax.axis_index("col") == 0, held[:, :width], 0.0)
    out_ref[:, :piece, :] = image.reshape(out_ref.shape[0], piece, width)


def factor_and_product(parts, mobility, piece, share):
    n_rows, n_cols = mobility.shape
    width = parts.shape[2]
    vmem = pl.BlockSpec(memory_space=pltpu.VMEM)
    square = jax.ShapeDtypeStruct((width, width), jnp.float32)
    mobility = pltpu.with_memory_space_constraint(mobility, pltpu.HBM)
    return pl.pallas_call(
        lambda *refs: product_kernel(piece, share, *refs),
        in_specs=[vmem, pl.BlockSpec(memory_space=pltpu.HBM)],
        out_specs=[vmem] * 3,
        out_shape=(
            square,
            square,
            jax.ShapeDtypeStruct((n_rows // piece, piece + share, width), jnp.float32),
        ),
        scratch_shapes=[
            pltpu.VMEM((width, width), jnp.float32),
            pltpu.VMEM((width, width), jnp.float32),
            pltpu.VMEM((STEP, STEP, width), jnp.float32),
            pltpu.VMEM((n_cols, 2 * width), jnp.bfloat16),
            pltpu.VMEM(mobility.shape, jnp.float32),
            pltpu.VMEM((n_rows, width), jnp.float32),
            pltpu.SemaphoreType.DMA((4,)),
        ],
        cost_estimate=pl.CostEstimate(
            flops=6 * n_rows * n_cols * width, bytes_accessed=6_000_000, transcendentals=0
        ),
        compiler_params=pltpu.CompilerParams(vmem_limit_bytes=20 * MIB),
        name="factor_and_product",
    )(parts, mobility)


def copy_kernel(rows_ref, out_ref, held, sem):
    load = pltpu.make_async_copy(rows_ref, held, sem)
    load.start()
    load.wait()
    out_ref[...] = jnp.broadcast_to(held[...][None], out_ref.shape)


def copies(rows, count):
    hbm = pl.BlockSpec(memory_space=pltpu.HBM)
    return pl.pallas_call(
        copy_kernel,
        in_specs=[hbm],
        out_specs=pl.BlockSpec(memory_space=pltpu.VMEM),
        out_shape=jax.ShapeDtypeStruct((count,) + rows.shape, rows.dtype),
        scratch_shapes=[pltpu.VMEM(rows.shape, rows.dtype), pltpu.SemaphoreType.DMA],
        cost_estimate=pl.CostEstimate(flops=0, bytes_accessed=600_000, transcendentals=0),
        compiler_params=pltpu.CompilerParams(vmem_limit_bytes=4 * MIB),
        name="copies",
    )(pltpu.with_memory_space_constraint(rows, pltpu.HBM))


def join_kernel(lone_ref, keep_ref, came_ref, mob_ref, out_ref):
    piece = lone_ref.shape[0]
    out_ref[:piece, :] = lone_ref[...]
    out_ref[piece:, :] = keep_ref[...] + came_ref[...]


def join(lone, keep, came, mobility):
    vmem = pl.BlockSpec(memory_space=pltpu.VMEM)
    shape = (lone.shape[0] + keep.shape[0], lone.shape[1])
    return pl.pallas_call(
        join_kernel,
        in_specs=[vmem] * 3 + [pl.BlockSpec(memory_space=pltpu.HBM)],
        out_specs=vmem,
        out_shape=jax.ShapeDtypeStruct(shape, jnp.float32),
        cost_estimate=pl.CostEstimate(flops=0, bytes_accessed=100_000, transcendentals=0),
        compiler_params=pltpu.CompilerParams(vmem_limit_bytes=4 * MIB),
        name="join",
    )(lone, keep, came, pltpu.with_memory_space_constraint(mobility, pltpu.HBM))


def image_kernel(piece, got_ref, image_ref, copies_ref, top_ref):
    image = got_ref[0, :piece, :]
    for k in range(1, got_ref.shape[0]):
        image = image + got_ref[k, :piece, :]
    image_ref[...] = image
    copies_ref[...] = jnp.broadcast_to(image[None], copies_ref.shape)
    top_ref[...] = got_ref[:, piece:, :].reshape(top_ref.shape)


def image_piece(got, piece):
    count, _, width = got.shape
    vmem = pl.BlockSpec(memory_space=pltpu.VMEM)
    return pl.pallas_call(
        lambda *refs: image_kernel(piece, *refs),
        in_specs=[vmem],
        out_specs=[vmem] * 3,
        out_shape=(
            jax.ShapeDtypeStruct((piece, width), jnp.float32),
            jax.ShapeDtypeStruct((count, piece, width), jnp.float32),
            jax.ShapeDtypeStruct((width, width), jnp.float32),
        ),
        cost_estimate=pl.CostEstimate(
            flops=10_000_000, bytes_accessed=2_000_000, transcendentals=0
        ),
        compiler_params=pltpu.CompilerParams(vmem_limit_bytes=6 * MIB),
        name="image_piece",
    )(got)


def rows_kernel(rows_ref, inverse_ref, turned_ref):
    rows = exact_dot(left_terms(rows_ref[...]), right_terms(inverse_ref[...]), NT)
    turned_ref[...] = (rows + unit_rows(lax.axis_index("row"), rows.shape)).T


def kernel_kernel(piece, inverse_ref, top_ref, turned_ref, parts_ref, *outs):
    cols_out, rows_left, state_ref = outs
    width = inverse_ref.shape[0]
    identity = eye(width)
    ratio = -product(inverse_ref[...], top_ref[...], NT)
    state_ref[:width, :] = ratio
    state_ref[width:, :] = identity

    def go_on(state):
        return jnp.logical_and(state[0] < 40, state[1] > 1e-10)

    def double(state):
        power = state_ref[:width, :]
        both = product(state_ref[...], power)
        state_ref[:width, :] = both[:width]
        state_ref[width:, :] = state_ref[width:, :] + both[width:]
        return state[0] + 1, jnp.max(jnp.abs(both[:width]))

    lax.while_loop(go_on, double, (0, jnp.max(jnp.abs(ratio))))
    total = state_ref[width:, :]
    kernel = total + product(total, identity - product(identity - ratio, total))
    kernel_terms = right_terms(kernel)
    cols = exact_dot(
        left_terms(pieces_of(parts_ref, piece)), right_terms(inverse_ref[...]), NT
    )
    cols = cols + unit_rows(lax.axis_index("col"), cols.shape)
    cols_out[...] = both_terms(exact_dot(left_terms(cols), kernel_terms, NT))
    rows_left[...] = both_terms(exact_dot(left_terms(turned_ref[...].T), kernel_terms, NT))


def side_call(kernel, operands, shapes, scratch, name):
    vmem = pl.BlockSpec(memory_space=pltpu.VMEM)
    return pl.pallas_call(
        kernel,
        in_specs=[vmem] * len(operands),
        out_specs=[vmem] * len(shapes),
        out_shape=shapes,
        scratch_shapes=scratch,
        cost_estimate=pl.CostEstimate(
            flops=300_000_000, bytes_accessed=10_000_000, transcendentals=0
        ),
        compiler_params=pltpu.CompilerParams(vmem_limit_bytes=14 * MIB),
        name=name,
    )(*operands)


def update_kernel(piece, *refs):
    parts_ref, image_ref, cols_ref, rows_left, mob_ref = refs[:5]
    out_ref, lhs, rhs, held, sems = refs[5:]
    count = sems.shape[0]
    tile = held.shape[0] // count
    middle = lhs.shape[1] // 2
    lhs[:, :middle] = left_terms(image_ref[...])
    lhs[:, middle:] = to_left(rows_left[...])
    small = right_terms(unpack(parts_ref, piece))
    change = exact_dot(to_left(cols_ref[...]), small, NT)
    rhs[:middle, :] = to_right(cols_ref[...]).T
    rhs[middle:, :] = right_terms(pieces_of(parts_ref, piece) - change).T
    stores = []
    for k in range(count):
        rows = pl.ds(k * tile, tile)
        held[rows, :] = mob_ref[rows, :] - exact_dot(lhs[rows, :], rhs[...], NN)
        stores.append(pltpu.make_async_copy(held.at[rows], out_ref.at[rows], sems.at[k]))
        stores[k].start()
    for k in range(count):
        stores[k].wait()


def update(operands, mobility, piece):
    n_rows, n_cols = mobility.shape
    terms = 3 * operands[-1].shape[1]
    vmem = pl.BlockSpec(memory_space=pltpu.VMEM)
    hbm = pl.BlockSpec(memory_space=pltpu.HBM)
    return pl.pallas_call(
        lambda *refs: update_kernel(piece, *refs),
        in_specs=[vmem] * (len(operands) + 1),
        out_specs=hbm,
        out_shape=pltpu.HBM(mobility.shape, jnp.float32),
        scratch_shapes=[
            pltpu.VMEM((n_rows, terms), jnp.bfloat16),
            pltpu.VMEM((terms, n_cols), jnp.bfloat16),
            pltpu.VMEM(mobility.shape, jnp.float32),
            pltpu.SemaphoreType.DMA((4,)),
        ],
        cost_estimate=pl.CostEstimate(
            flops=2 * n_rows * n_cols * terms, bytes_accessed=9_000_000, transcendentals=0
        ),
        compiler_params=pltpu.CompilerParams(vmem_limit_bytes=20 * MIB),
        name="update",
    )(*operands, mobility)


def on_device(panel, mobility):
    piece, width = panel.shape
    n_row, n_col = lax.axis_size("row"), lax.axis_size("col")
    block_rows, block_cols = mobility.shape
    share = width // n_col
    transposing = [(i * n_col + j, j * n_col + i) for i in range(n_row) for j in range(n_col)]
    swap = [(i, i ^ 1) for i in range(n_row)]

    turned_panel = lax.ppermute(panel, BOTH, transposing)
    panel_rows = lax.all_to_all(copies(panel, n_col), "col", 0, 0).reshape(block_rows, width)
    keep, give, top_part = packed_parts(
        gram_kernel, (panel_rows,), [(share, width)], "gram_parts"
    )
    give, turned_panel = lax.optimization_barrier((give, turned_panel))
    packed = keep + lax.ppermute(give, "row", swap)
    even = lax.axis_index("row") % 2 == 0
    tail = jnp.where(even, top_part, packed[-STEP:])
    sent = jnp.concatenate([turned_panel, packed[:-STEP], tail], 0)
    panel_parts = lax.all_gather(sent, "row", axis=0)

    panel_factor, inverse, sent = factor_and_product(panel_parts, mobility, piece, share)
    got = lax.all_to_all(sent, "col", 0, 0)
    wide = jax.ShapeDtypeStruct((block_rows, 2 * width), jnp.bfloat16)
    tall = jax.ShapeDtypeStruct((width, block_rows), jnp.float32)
    (turned_rows,) = side_call(rows_kernel, (panel_rows, inverse), [tall], [], "basis_rows")
    got, turned_rows = lax.optimization_barrier((got, turned_rows))
    image, image_copies, top_rows = image_piece(got, piece)
    turned_image = lax.ppermute(image, BOTH, transposing)
    image_rows = lax.all_to_all(image_copies, "col", 0, 0).reshape(block_rows, width)
    cols_right, rows_left = side_call(
        lambda *refs: kernel_kernel(piece, *refs),
        (inverse, top_rows, turned_rows, panel_parts),
        [wide, wide],
        [pltpu.VMEM((2 * width, width), jnp.float32)],
        "kernel",
    )
    image_rows, rows_left = lax.optimization_barrier((image_rows, rows_left))
    keep, give = packed_parts(inner_kernel, (turned_rows, image_rows), [], "inner_parts")
    came = lax.ppermute(give, "row", swap)
    image_parts = lax.all_gather(join(turned_image, keep, came, mobility), "row", axis=0)
    operands = (image_parts, image_rows, cols_right, rows_left)
    updated = update(operands, mobility, piece)
    return (updated, panel_factor)


def solution(mesh):
    in_specs = (P(("row", "col"), None), P("row", "col"))
    out_specs = (P("row", "col"), P())
    return jax.shard_map(
        on_device, mesh=mesh, in_specs=in_specs, out_specs=out_specs, check_vma=False
    )
```

```python
import jax
import jax.numpy as jnp
from jax import lax
from jax.experimental import pallas as pl
from jax.experimental.pallas import tpu as pltpu
from jax.sharding import PartitionSpec as P

BOTH = ("row", "col")
STEP = 8
MIB = 1 << 20
NN = (((1,), (0,)), ((), ()))
TN = (((0,), (0,)), ((), ()))
NT = (((1,), (1,)), ((), ()))


def product(first_op, second_op, dims=NN):
    return lax.dot_general(
        first_op,
        second_op,
        dims,
        precision=lax.Precision.HIGHEST,
        preferred_element_type=jnp.float32,
    )


def split(value):
    high = value.astype(jnp.bfloat16)
    return high, (value - high.astype(jnp.float32)).astype(jnp.bfloat16)


def both_terms(value):
    return jnp.concatenate(split(value), 1)


def left_terms(value):
    high, low = split(value)
    return jnp.concatenate([high, low, high], 1)


def right_terms(value):
    high, low = split(value)
    return jnp.concatenate([high, high, low], 1)


def to_left(pair):
    return jnp.concatenate([pair, pair[:, : pair.shape[1] // 2]], 1)


def to_right(pair):
    return jnp.concatenate([pair[:, : pair.shape[1] // 2], pair], 1)


def exact_dot(first_op, second_op, dims):
    return lax.dot_general(first_op, second_op, dims, preferred_element_type=jnp.float32)


def unit_rows(index, shape):
    rows = lax.broadcasted_iota(jnp.int32, shape, 0) + index * shape[0]
    return jnp.where(rows == lax.broadcasted_iota(jnp.int32, shape, 1), 1.0, 0.0)


def eye(width):
    return unit_rows(0, (width, width))


def pieces_of(parts_ref, piece):
    count, _, width = parts_ref.shape
    return parts_ref[:, :piece, :].reshape(count * piece, width)


def pack(value, keep_ref, give_ref):
    side = value.shape[0] // 2
    half = side // 2
    top = value[:side]
    low = pltpu.roll(value[side:], side, 1)
    row = lax.broadcasted_iota(jnp.int32, top.shape, 0)
    lane = lax.broadcasted_iota(jnp.int32, top.shape, 1)
    rows = jnp.where(jnp.logical_and(row < lane, lane < side), low, top)
    last = jnp.sum(jnp.where(row == lane, low, 0.0), axis=0, keepdims=True)
    even = lax.rem(lax.axis_index("row"), 2) == 0
    keep_ref[:half, :] = jnp.where(even, rows[:half], rows[half:])
    give_ref[:half, :] = jnp.where(even, rows[half:], rows[:half])
    keep_ref[half:, :] = jnp.broadcast_to(last, (STEP, last.shape[1]))
    give_ref[half:, :] = jnp.broadcast_to(last, (STEP, last.shape[1]))


def unpack(parts_ref, piece):
    half = parts_ref.shape[2] // 4
    stop = piece + half
    sums = [parts_ref[0, piece:stop, :], parts_ref[1, piece : stop + STEP, :]]
    for i in range(2, parts_ref.shape[0], 2):
        sums[0] = sums[0] + parts_ref[i, piece:stop, :]
        sums[1] = sums[1] + parts_ref[i + 1, piece : stop + STEP, :]
    side = 2 * half
    rows = jnp.concatenate([sums[0], sums[1][:half]], 0)
    turned = rows.T
    row = lax.broadcasted_iota(jnp.int32, (side, side), 0)
    lane = lax.broadcasted_iota(jnp.int32, (side, side), 1)
    left, across = rows[:, :side], turned[:side]
    last = sums[1][half : half + 1, :side]
    a = jnp.where(row >= lane, left, across)
    d = jnp.where(row == lane, last, jnp.where(row < lane, left, across))
    return jnp.concatenate(
        [
            jnp.concatenate([a, rows[:, side:]], 1),
            jnp.concatenate([turned[side:], d], 1),
        ],
        0,
    )


def gram_kernel(rows_ref, keep_ref, give_ref, top_ref):
    share = top_ref.shape[0]
    rows = rows_ref[...]
    pack(product(rows, rows, TN), keep_ref, give_ref)
    start = pl.multiple_of(lax.axis_index("col") * share, share)
    top_ref[...] = rows_ref[pl.ds(start, share), :]


def inner_kernel(turned_ref, rows_ref, keep_ref, give_ref):
    terms = product(turned_ref[...], rows_ref[...])
    pack(0.5 * (terms + terms.T), keep_ref, give_ref)


def packed_parts(kernel, operands, extra, name):
    width = operands[-1].shape[1]
    vmem = pl.BlockSpec(memory_space=pltpu.VMEM)
    shapes = [(width // 4 + STEP, width)] * 2 + extra
    return pl.pallas_call(
        kernel,
        in_specs=[vmem] * len(operands),
        out_specs=[vmem] * len(shapes),
        out_shape=[jax.ShapeDtypeStruct(shape, jnp.float32) for shape in shapes],
        cost_estimate=pl.CostEstimate(
            flops=1_000, bytes_accessed=1_000, transcendentals=0
        ),
        compiler_params=pltpu.CompilerParams(vmem_limit_bytes=8 * MIB),
        name=name,
    )(*operands)


def eliminate(gram, upper_ref, inverse_ref, work, other, stash, beside):
    width = upper_ref.shape[0]
    full = (STEP, width)
    lane = lax.broadcasted_iota(jnp.int32, full, 1)
    work[...] = gram
    other[...] = eye(width)
    for first in range(0, width, STEP):
        beside(first // STEP)
        a_rows = [jnp.broadcast_to(work[first + k : first + k + 1, :], full) for k in range(STEP)]
        x_rows = [jnp.broadcast_to(other[first + k : first + k + 1, :], full) for k in range(STEP)]
        entry, mult, inv = {}, {}, {}
        pivot = work[first : first + STEP, :]
        for k in range(STEP):
            stash[k] = jnp.broadcast_to(pivot[:, first + k : first + k + 1], full)
        for i in range(STEP):
            for k in range(i + 1):
                entry[i, k] = jnp.broadcast_to(stash[k, i : i + 1, :], full)
        for k in range(STEP):
            inv[k] = 1.0 / entry[k, k]
            for i in range(k + 1, STEP):
                mult[i, k] = entry[i, k] * inv[k]
            for i in range(k + 1, STEP):
                for l in range(k + 1, i + 1):
                    entry[i, l] = entry[i, l] - mult[i, k] * entry[l, k]
        for i in range(STEP):
            for k in range(i):
                a_rows[i] = a_rows[i] - mult[i, k] * a_rows[k]
                x_rows[i] = x_rows[i] - mult[i, k] * x_rows[k]
        for k in range(STEP):
            root = lax.rsqrt(entry[k, k])
            root = root * (1.5 - 0.5 * entry[k, k] * root * root)
            row = slice(first + k, first + k + 1)
            upper_ref[row, :] = jnp.where(lane >= first + k, a_rows[k] * root, 0.0)[:1]
            inverse_ref[row, :] = (x_rows[k] * root)[:1]
        if first + STEP == width:
            break
        a_back = [a_rows[k] * inv[k] for k in range(STEP)]
        x_back = [x_rows[k] * inv[k] for k in range(STEP)]
        for k in range(STEP - 2, -1, -1):
            for l in range(k + 1, STEP):
                a_back[k] = a_back[k] - mult[l, k] * a_back[l]
                x_back[k] = x_back[k] - mult[l, k] * x_back[l]
        for g in range(first + STEP, width, STEP):
            block = work[g : g + STEP, :]
            a_new, x_new = block, other[g : g + STEP, :]
            for k in range(STEP):
                column = jnp.broadcast_to(block[:, first + k : first + k + 1], full)
                a_new = a_new - column * a_back[k]
                x_new = x_new - column * x_back[k]
            work[g : g + STEP, :] = a_new
            other[g : g + STEP, :] = x_new


def product_kernel(piece, share, parts_ref, mob_ref, upper_ref, inverse_ref, out_ref, *refs):
    work, other, stash, rhs, held, found, sems = refs
    width = parts_ref.shape[2]
    count = sems.shape[0]
    tile = held.shape[0] // count
    loads = []
    for k in range(count):
        rows = pl.ds(k * tile, tile)
        loads.append(pltpu.make_async_copy(mob_ref.at[rows], held.at[rows], sems.at[k]))
        loads[k].start()
    rhs[...] = both_terms(pieces_of(parts_ref, piece))
    last = parts_ref.shape[1] - share
    out_ref[:, piece:, :] = jnp.broadcast_to(
        parts_ref[0, last:, :][None], (out_ref.shape[0], share, width)
    )

    def beside(index):
        k = index // 3 - 1
        if index % 3 or not 0 <= k < count:
            return
        loads[k].wait()
        rows = slice(k * tile, (k + 1) * tile)
        high, low = split(held[rows, :])
        wide = exact_dot(high, rhs[...], NN)
        low_part = exact_dot(low, rhs[:, :width], NN)
        found[rows, :] = wide[:, :width] + wide[:, width:] + low_part

    eliminate(unpack(parts_ref, piece), upper_ref, inverse_ref, work, other, stash, beside)
    image = exact_dot(left_terms(found[...]), right_terms(inverse_ref[...]), NT)
    image = image + jnp.where(lax.axis_index("col") == 0, held[:, :width], 0.0)
    out_ref[:, :piece, :] = image.reshape(out_ref.shape[0], piece, width)


def factor_and_product(parts, mobility, piece, share):
    n_rows, n_cols = mobility.shape
    width = parts.shape[2]
    vmem = pl.BlockSpec(memory_space=pltpu.VMEM)
    square = jax.ShapeDtypeStruct((width, width), jnp.float32)
    mobility = pltpu.with_memory_space_constraint(mobility, pltpu.HBM)
    return pl.pallas_call(
        lambda *refs: product_kernel(piece, share, *refs),
        in_specs=[vmem, pl.BlockSpec(memory_space=pltpu.HBM)],
        out_specs=[vmem] * 3,
        out_shape=(
            square,
            square,
            jax.ShapeDtypeStruct((n_rows // piece, piece + share, width), jnp.float32),
        ),
        scratch_shapes=[
            pltpu.VMEM((width, width), jnp.float32),
            pltpu.VMEM((width, width), jnp.float32),
            pltpu.VMEM((STEP, STEP, width), jnp.float32),
            pltpu.VMEM((n_cols, 2 * width), jnp.bfloat16),
            pltpu.VMEM(mobility.shape, jnp.float32),
            pltpu.VMEM((n_rows, width), jnp.float32),
            pltpu.SemaphoreType.DMA((4,)),
        ],
        cost_estimate=pl.CostEstimate(
            flops=6 * n_rows * n_cols * width, bytes_accessed=6_000_000, transcendentals=0
        ),
        compiler_params=pltpu.CompilerParams(vmem_limit_bytes=20 * MIB),
        name="factor_and_product",
    )(parts, mobility)


def copy_kernel(rows_ref, out_ref, held, sem):
    load = pltpu.make_async_copy(rows_ref, held, sem)
    load.start()
    load.wait()
    out_ref[...] = jnp.broadcast_to(held[...][None], out_ref.shape)


def copies(rows, count):
    hbm = pl.BlockSpec(memory_space=pltpu.HBM)
    return pl.pallas_call(
        copy_kernel,
        in_specs=[hbm],
        out_specs=pl.BlockSpec(memory_space=pltpu.VMEM),
        out_shape=jax.ShapeDtypeStruct((count,) + rows.shape, rows.dtype),
        scratch_shapes=[pltpu.VMEM(rows.shape, rows.dtype), pltpu.SemaphoreType.DMA],
        cost_estimate=pl.CostEstimate(flops=0, bytes_accessed=600_000, transcendentals=0),
        compiler_params=pltpu.CompilerParams(vmem_limit_bytes=4 * MIB),
        name="copies",
    )(pltpu.with_memory_space_constraint(rows, pltpu.HBM))


def join_kernel(lone_ref, keep_ref, came_ref, mob_ref, out_ref):
    piece = lone_ref.shape[0]
    out_ref[:piece, :] = lone_ref[...]
    out_ref[piece:, :] = keep_ref[...] + came_ref[...]


def join(lone, keep, came, mobility):
    vmem = pl.BlockSpec(memory_space=pltpu.VMEM)
    shape = (lone.shape[0] + keep.shape[0], lone.shape[1])
    return pl.pallas_call(
        join_kernel,
        in_specs=[vmem] * 3 + [pl.BlockSpec(memory_space=pltpu.HBM)],
        out_specs=vmem,
        out_shape=jax.ShapeDtypeStruct(shape, jnp.float32),
        cost_estimate=pl.CostEstimate(flops=0, bytes_accessed=100_000, transcendentals=0),
        compiler_params=pltpu.CompilerParams(vmem_limit_bytes=4 * MIB),
        name="join",
    )(lone, keep, came, pltpu.with_memory_space_constraint(mobility, pltpu.HBM))


def image_kernel(piece, got_ref, image_ref, copies_ref, top_ref):
    image = got_ref[0, :piece, :]
    for k in range(1, got_ref.shape[0]):
        image = image + got_ref[k, :piece, :]
    image_ref[...] = image
    copies_ref[...] = jnp.broadcast_to(image[None], copies_ref.shape)
    top_ref[...] = got_ref[:, piece:, :].reshape(top_ref.shape)


def image_piece(got, piece):
    count, _, width = got.shape
    vmem = pl.BlockSpec(memory_space=pltpu.VMEM)
    return pl.pallas_call(
        lambda *refs: image_kernel(piece, *refs),
        in_specs=[vmem],
        out_specs=[vmem] * 3,
        out_shape=(
            jax.ShapeDtypeStruct((piece, width), jnp.float32),
            jax.ShapeDtypeStruct((count, piece, width), jnp.float32),
            jax.ShapeDtypeStruct((width, width), jnp.float32),
        ),
        cost_estimate=pl.CostEstimate(
            flops=10_000_000, bytes_accessed=2_000_000, transcendentals=0
        ),
        compiler_params=pltpu.CompilerParams(vmem_limit_bytes=6 * MIB),
        name="image_piece",
    )(got)


def rows_kernel(rows_ref, inverse_ref, turned_ref):
    rows = exact_dot(left_terms(rows_ref[...]), right_terms(inverse_ref[...]), NT)
    turned_ref[...] = (rows + unit_rows(lax.axis_index("row"), rows.shape)).T


def kernel_kernel(piece, inverse_ref, top_ref, turned_ref, parts_ref, *outs):
    cols_out, rows_left, state_ref = outs
    width = inverse_ref.shape[0]
    identity = eye(width)
    ratio = -product(inverse_ref[...], top_ref[...], NT)
    state_ref[:width, :] = ratio
    state_ref[width:, :] = identity

    def go_on(state):
        return jnp.logical_and(state[0] < 40, state[1] > 1e-10)

    def double(state):
        power = state_ref[:width, :]
        both = product(state_ref[...], power)
        state_ref[:width, :] = both[:width]
        state_ref[width:, :] = state_ref[width:, :] + both[width:]
        return state[0] + 1, jnp.max(jnp.abs(both[:width]))

    lax.while_loop(go_on, double, (0, jnp.max(jnp.abs(ratio))))
    total = state_ref[width:, :]
    kernel = total + product(total, identity - product(identity - ratio, total))
    kernel_terms = right_terms(kernel)
    cols = exact_dot(
        left_terms(pieces_of(parts_ref, piece)), right_terms(inverse_ref[...]), NT
    )
    cols = cols + unit_rows(lax.axis_index("col"), cols.shape)
    cols_out[...] = both_terms(exact_dot(left_terms(cols), kernel_terms, NT))
    rows_left[...] = both_terms(exact_dot(left_terms(turned_ref[...].T), kernel_terms, NT))


def side_call(kernel, operands, shapes, scratch, name):
    vmem = pl.BlockSpec(memory_space=pltpu.VMEM)
    return pl.pallas_call(
        kernel,
        in_specs=[vmem] * len(operands),
        out_specs=[vmem] * len(shapes),
        out_shape=shapes,
        scratch_shapes=scratch,
        cost_estimate=pl.CostEstimate(
            flops=300_000_000, bytes_accessed=10_000_000, transcendentals=0
        ),
        compiler_params=pltpu.CompilerParams(vmem_limit_bytes=14 * MIB),
        name=name,
    )(*operands)


def update_kernel(piece, *refs):
    parts_ref, image_ref, cols_ref, rows_left, mob_ref = refs[:5]
    out_ref, lhs, rhs, held, sems = refs[5:]
    count = sems.shape[0]
    tile = held.shape[0] // count
    middle = lhs.shape[1] // 2
    lhs[:, :middle] = left_terms(image_ref[...])
    lhs[:, middle:] = to_left(rows_left[...])
    small = right_terms(unpack(parts_ref, piece))
    change = exact_dot(to_left(cols_ref[...]), small, NT)
    rhs[:middle, :] = to_right(cols_ref[...]).T
    rhs[middle:, :] = right_terms(pieces_of(parts_ref, piece) - change).T
    stores = []
    for k in range(count):
        rows = pl.ds(k * tile, tile)
        held[rows, :] = mob_ref[rows, :] - exact_dot(lhs[rows, :], rhs[...], NN)
        stores.append(pltpu.make_async_copy(held.at[rows], out_ref.at[rows], sems.at[k]))
        stores[k].start()
    for k in range(count):
        stores[k].wait()


def update(operands, mobility, piece):
    n_rows, n_cols = mobility.shape
    terms = 3 * operands[-1].shape[1]
    vmem = pl.BlockSpec(memory_space=pltpu.VMEM)
    hbm = pl.BlockSpec(memory_space=pltpu.HBM)
    return pl.pallas_call(
        lambda *refs: update_kernel(piece, *refs),
        in_specs=[vmem] * (len(operands) + 1),
        out_specs=hbm,
        out_shape=pltpu.HBM(mobility.shape, jnp.float32),
        scratch_shapes=[
            pltpu.VMEM((n_rows, terms), jnp.bfloat16),
            pltpu.VMEM((terms, n_cols), jnp.bfloat16),
            pltpu.VMEM(mobility.shape, jnp.float32),
            pltpu.SemaphoreType.DMA((4,)),
        ],
        cost_estimate=pl.CostEstimate(
            flops=2 * n_rows * n_cols * terms, bytes_accessed=9_000_000, transcendentals=0
        ),
        compiler_params=pltpu.CompilerParams(vmem_limit_bytes=20 * MIB),
        name="update",
    )(*operands, mobility)


def on_device(panel, mobility):
    piece, width = panel.shape
    n_row, n_col = lax.axis_size("row"), lax.axis_size("col")
    block_rows, block_cols = mobility.shape
    share = width // n_col
    transposing = [(i * n_col + j, j * n_col + i) for i in range(n_row) for j in range(n_col)]
    swap = [(i, i ^ 1) for i in range(n_row)]

    turned_panel = lax.ppermute(panel, BOTH, transposing)
    panel_rows = lax.all_to_all(copies(panel, n_col), "col", 0, 0).reshape(block_rows, width)
    keep, give, top_part = packed_parts(
        gram_kernel, (panel_rows,), [(share, width)], "gram_parts"
    )
    keep, turned_panel = lax.optimization_barrier((keep, turned_panel))
    packed = keep + lax.ppermute(give, "row", swap)
    even = lax.axis_index("row") % 2 == 0
    tail = jnp.where(even, top_part, packed[-STEP:])
    sent = jnp.concatenate([turned_panel, packed[:-STEP], tail], 0)
    panel_parts = lax.all_gather(sent, "row", axis=0)

    panel_factor, inverse, sent = factor_and_product(panel_parts, mobility, piece, share)
    got = lax.all_to_all(sent, "col", 0, 0)
    wide = jax.ShapeDtypeStruct((block_rows, 2 * width), jnp.bfloat16)
    tall = jax.ShapeDtypeStruct((width, block_rows), jnp.float32)
    (turned_rows,) = side_call(rows_kernel, (panel_rows, inverse), [tall], [], "basis_rows")
    got, turned_rows = lax.optimization_barrier((got, turned_rows))
    image, image_copies, top_rows = image_piece(got, piece)
    turned_image = lax.ppermute(image, BOTH, transposing)
    image_rows = lax.all_to_all(image_copies, "col", 0, 0).reshape(block_rows, width)
    cols_right, rows_left = side_call(
        lambda *refs: kernel_kernel(piece, *refs),
        (inverse, top_rows, turned_rows, panel_parts),
        [wide, wide],
        [pltpu.VMEM((2 * width, width), jnp.float32)],
        "kernel",
    )
    image_rows, rows_left = lax.optimization_barrier((image_rows, rows_left))
    keep, give = packed_parts(inner_kernel, (turned_rows, image_rows), [], "inner_parts")
    came = lax.ppermute(give, "row", swap)
    image_parts = lax.all_gather(join(turned_image, keep, came, mobility), "row", axis=0)
    operands = (image_parts, image_rows, cols_right, rows_left)
    updated = update(operands, mobility, piece)
    return (updated, panel_factor)


def solution(mesh):
    in_specs = (P(("row", "col"), None), P("row", "col"))
    out_specs = (P("row", "col"), P())
    return jax.shard_map(
        on_device, mesh=mesh, in_specs=in_specs, out_specs=out_specs, check_vma=False
    )
```

```python
import jax
import jax.numpy as jnp
from jax import lax
from jax.experimental import pallas as pl
from jax.experimental.pallas import tpu as pltpu
from jax.sharding import PartitionSpec as P

BOTH = ("row", "col")
STEP = 8
MIB = 1 << 20
NN = (((1,), (0,)), ((), ()))
TN = (((0,), (0,)), ((), ()))
NT = (((1,), (1,)), ((), ()))


def product(first_op, second_op, dims=NN):
    return lax.dot_general(
        first_op,
        second_op,
        dims,
        precision=lax.Precision.HIGHEST,
        preferred_element_type=jnp.float32,
    )


def split(value):
    high = value.astype(jnp.bfloat16)
    return high, (value - high.astype(jnp.float32)).astype(jnp.bfloat16)


def both_terms(value):
    return jnp.concatenate(split(value), 1)


def left_terms(value):
    high, low = split(value)
    return jnp.concatenate([high, low, high], 1)


def right_terms(value):
    high, low = split(value)
    return jnp.concatenate([high, high, low], 1)


def to_left(pair):
    return jnp.concatenate([pair, pair[:, : pair.shape[1] // 2]], 1)


def to_right(pair):
    return jnp.concatenate([pair[:, : pair.shape[1] // 2], pair], 1)


def exact_dot(first_op, second_op, dims):
    return lax.dot_general(first_op, second_op, dims, preferred_element_type=jnp.float32)


def unit_rows(index, shape):
    rows = lax.broadcasted_iota(jnp.int32, shape, 0) + index * shape[0]
    return jnp.where(rows == lax.broadcasted_iota(jnp.int32, shape, 1), 1.0, 0.0)


def eye(width):
    return unit_rows(0, (width, width))


def pieces_of(parts_ref, piece):
    count, _, width = parts_ref.shape
    return parts_ref[:, :piece, :].reshape(count * piece, width)


def pack(value, keep_ref, give_ref):
    side = value.shape[0] // 2
    half = side // 2
    top = value[:side]
    low = pltpu.roll(value[side:], side, 1)
    row = lax.broadcasted_iota(jnp.int32, top.shape, 0)
    lane = lax.broadcasted_iota(jnp.int32, top.shape, 1)
    rows = jnp.where(jnp.logical_and(row < lane, lane < side), low, top)
    last = jnp.sum(jnp.where(row == lane, low, 0.0), axis=0, keepdims=True)
    even = lax.rem(lax.axis_index("row"), 2) == 0
    keep_ref[:half, :] = jnp.where(even, rows[:half], rows[half:])
    give_ref[:half, :] = jnp.where(even, rows[half:], rows[:half])
    keep_ref[half:, :] = jnp.broadcast_to(last, (STEP, last.shape[1]))
    give_ref[half:, :] = jnp.broadcast_to(last, (STEP, last.shape[1]))


def unpack(parts_ref, piece):
    half = parts_ref.shape[2] // 4
    stop = piece + half
    sums = [parts_ref[0, piece:stop, :], parts_ref[1, piece : stop + STEP, :]]
    for i in range(2, parts_ref.shape[0], 2):
        sums[0] = sums[0] + parts_ref[i, piece:stop, :]
        sums[1] = sums[1] + parts_ref[i + 1, piece : stop + STEP, :]
    side = 2 * half
    rows = jnp.concatenate([sums[0], sums[1][:half]], 0)
    turned = rows.T
    row = lax.broadcasted_iota(jnp.int32, (side, side), 0)
    lane = lax.broadcasted_iota(jnp.int32, (side, side), 1)
    left, across = rows[:, :side], turned[:side]
    last = sums[1][half : half + 1, :side]
    a = jnp.where(row >= lane, left, across)
    d = jnp.where(row == lane, last, jnp.where(row < lane, left, across))
    return jnp.concatenate(
        [
            jnp.concatenate([a, rows[:, side:]], 1),
            jnp.concatenate([turned[side:], d], 1),
        ],
        0,
    )


def gram_kernel(rows_ref, keep_ref, give_ref, top_ref):
    share = top_ref.shape[0]
    rows = rows_ref[...]
    pack(product(rows, rows, TN), keep_ref, give_ref)
    start = pl.multiple_of(lax.axis_index("col") * share, share)
    top_ref[...] = rows_ref[pl.ds(start, share), :]


def inner_kernel(turned_ref, rows_ref, keep_ref, give_ref):
    terms = product(turned_ref[...], rows_ref[...])
    pack(0.5 * (terms + terms.T), keep_ref, give_ref)


def packed_parts(kernel, operands, extra, name):
    width = operands[-1].shape[1]
    vmem = pl.BlockSpec(memory_space=pltpu.VMEM)
    shapes = [(width // 4 + STEP, width)] * 2 + extra
    return pl.pallas_call(
        kernel,
        in_specs=[vmem] * len(operands),
        out_specs=[vmem] * len(shapes),
        out_shape=[jax.ShapeDtypeStruct(shape, jnp.float32) for shape in shapes],
        cost_estimate=pl.CostEstimate(
            flops=1_000, bytes_accessed=1_000, transcendentals=0
        ),
        compiler_params=pltpu.CompilerParams(vmem_limit_bytes=8 * MIB),
        name=name,
    )(*operands)


def eliminate(gram, upper_ref, inverse_ref, work, other, stash, beside):
    width = upper_ref.shape[0]
    full = (STEP, width)
    lane = lax.broadcasted_iota(jnp.int32, full, 1)
    work[...] = gram
    other[...] = eye(width)
    for first in range(0, width, STEP):
        beside(first // STEP)
        a_rows = [jnp.broadcast_to(work[first + k : first + k + 1, :], full) for k in range(STEP)]
        x_rows = [jnp.broadcast_to(other[first + k : first + k + 1, :], full) for k in range(STEP)]
        entry, mult, inv = {}, {}, {}
        pivot = work[first : first + STEP, :]
        for k in range(STEP):
            stash[k] = jnp.broadcast_to(pivot[:, first + k : first + k + 1], full)
        for i in range(STEP):
            for k in range(i + 1):
                entry[i, k] = jnp.broadcast_to(stash[k, i : i + 1, :], full)
        for k in range(STEP):
            inv[k] = 1.0 / entry[k, k]
            for i in range(k + 1, STEP):
                mult[i, k] = entry[i, k] * inv[k]
            for i in range(k + 1, STEP):
                for l in range(k + 1, i + 1):
                    entry[i, l] = entry[i, l] - mult[i, k] * entry[l, k]
        for i in range(STEP):
            for k in range(i):
                a_rows[i] = a_rows[i] - mult[i, k] * a_rows[k]
                x_rows[i] = x_rows[i] - mult[i, k] * x_rows[k]
        for k in range(STEP):
            root = lax.rsqrt(entry[k, k])
            root = root * (1.5 - 0.5 * entry[k, k] * root * root)
            row = slice(first + k, first + k + 1)
            upper_ref[row, :] = jnp.where(lane >= first + k, a_rows[k] * root, 0.0)[:1]
            inverse_ref[row, :] = (x_rows[k] * root)[:1]
        if first + STEP == width:
            break
        a_back = [a_rows[k] * inv[k] for k in range(STEP)]
        x_back = [x_rows[k] * inv[k] for k in range(STEP)]
        for k in range(STEP - 2, -1, -1):
            for l in range(k + 1, STEP):
                a_back[k] = a_back[k] - mult[l, k] * a_back[l]
                x_back[k] = x_back[k] - mult[l, k] * x_back[l]
        for g in range(first + STEP, width, STEP):
            block = work[g : g + STEP, :]
            a_new, x_new = block, other[g : g + STEP, :]
            for k in range(STEP):
                column = jnp.broadcast_to(block[:, first + k : first + k + 1], full)
                a_new = a_new - column * a_back[k]
                x_new = x_new - column * x_back[k]
            work[g : g + STEP, :] = a_new
            other[g : g + STEP, :] = x_new


def product_kernel(piece, share, parts_ref, mob_ref, upper_ref, inverse_ref, out_ref, *refs):
    work, other, stash, rhs, held, found, sems = refs
    width = parts_ref.shape[2]
    count = sems.shape[0]
    tile = held.shape[0] // count
    loads = []
    for k in range(count):
        rows = pl.ds(k * tile, tile)
        loads.append(pltpu.make_async_copy(mob_ref.at[rows], held.at[rows], sems.at[k]))
        loads[k].start()
    rhs[...] = both_terms(pieces_of(parts_ref, piece))
    last = parts_ref.shape[1] - share
    out_ref[:, piece:, :] = jnp.broadcast_to(
        parts_ref[0, last:, :][None], (out_ref.shape[0], share, width)
    )

    def beside(index):
        k = index // 2 - 4
        if index % 2 or not 0 <= k < count:
            return
        loads[k].wait()
        rows = slice(k * tile, (k + 1) * tile)
        high, low = split(held[rows, :])
        wide = exact_dot(high, rhs[...], NN)
        low_part = exact_dot(low, rhs[:, :width], NN)
        found[rows, :] = wide[:, :width] + wide[:, width:] + low_part

    eliminate(unpack(parts_ref, piece), upper_ref, inverse_ref, work, other, stash, beside)
    image = exact_dot(left_terms(found[...]), right_terms(inverse_ref[...]), NT)
    image = image + jnp.where(lax.axis_index("col") == 0, held[:, :width], 0.0)
    out_ref[:, :piece, :] = image.reshape(out_ref.shape[0], piece, width)


def factor_and_product(parts, mobility, piece, share):
    n_rows, n_cols = mobility.shape
    width = parts.shape[2]
    vmem = pl.BlockSpec(memory_space=pltpu.VMEM)
    square = jax.ShapeDtypeStruct((width, width), jnp.float32)
    mobility = pltpu.with_memory_space_constraint(mobility, pltpu.HBM)
    return pl.pallas_call(
        lambda *refs: product_kernel(piece, share, *refs),
        in_specs=[vmem, pl.BlockSpec(memory_space=pltpu.HBM)],
        out_specs=[vmem] * 3,
        out_shape=(
            square,
            square,
            jax.ShapeDtypeStruct((n_rows // piece, piece + share, width), jnp.float32),
        ),
        scratch_shapes=[
            pltpu.VMEM((width, width), jnp.float32),
            pltpu.VMEM((width, width), jnp.float32),
            pltpu.VMEM((STEP, STEP, width), jnp.float32),
            pltpu.VMEM((n_cols, 2 * width), jnp.bfloat16),
            pltpu.VMEM(mobility.shape, jnp.float32),
            pltpu.VMEM((n_rows, width), jnp.float32),
            pltpu.SemaphoreType.DMA((4,)),
        ],
        cost_estimate=pl.CostEstimate(
            flops=6 * n_rows * n_cols * width, bytes_accessed=6_000_000, transcendentals=0
        ),
        compiler_params=pltpu.CompilerParams(vmem_limit_bytes=20 * MIB),
        name="factor_and_product",
    )(parts, mobility)


def copy_kernel(rows_ref, out_ref, held, sem):
    load = pltpu.make_async_copy(rows_ref, held, sem)
    load.start()
    load.wait()
    out_ref[...] = jnp.broadcast_to(held[...][None], out_ref.shape)


def copies(rows, count):
    hbm = pl.BlockSpec(memory_space=pltpu.HBM)
    return pl.pallas_call(
        copy_kernel,
        in_specs=[hbm],
        out_specs=pl.BlockSpec(memory_space=pltpu.VMEM),
        out_shape=jax.ShapeDtypeStruct((count,) + rows.shape, rows.dtype),
        scratch_shapes=[pltpu.VMEM(rows.shape, rows.dtype), pltpu.SemaphoreType.DMA],
        cost_estimate=pl.CostEstimate(flops=0, bytes_accessed=600_000, transcendentals=0),
        compiler_params=pltpu.CompilerParams(vmem_limit_bytes=4 * MIB),
        name="copies",
    )(pltpu.with_memory_space_constraint(rows, pltpu.HBM))


def join_kernel(lone_ref, keep_ref, came_ref, mob_ref, out_ref):
    piece = lone_ref.shape[0]
    out_ref[:piece, :] = lone_ref[...]
    out_ref[piece:, :] = keep_ref[...] + came_ref[...]


def join(lone, keep, came, mobility):
    vmem = pl.BlockSpec(memory_space=pltpu.VMEM)
    shape = (lone.shape[0] + keep.shape[0], lone.shape[1])
    return pl.pallas_call(
        join_kernel,
        in_specs=[vmem] * 3 + [pl.BlockSpec(memory_space=pltpu.HBM)],
        out_specs=vmem,
        out_shape=jax.ShapeDtypeStruct(shape, jnp.float32),
        cost_estimate=pl.CostEstimate(flops=0, bytes_accessed=100_000, transcendentals=0),
        compiler_params=pltpu.CompilerParams(vmem_limit_bytes=4 * MIB),
        name="join",
    )(lone, keep, came, pltpu.with_memory_space_constraint(mobility, pltpu.HBM))


def image_kernel(piece, got_ref, image_ref, copies_ref, top_ref):
    image = got_ref[0, :piece, :]
    for k in range(1, got_ref.shape[0]):
        image = image + got_ref[k, :piece, :]
    image_ref[...] = image
    copies_ref[...] = jnp.broadcast_to(image[None], copies_ref.shape)
    top_ref[...] = got_ref[:, piece:, :].reshape(top_ref.shape)


def image_piece(got, piece):
    count, _, width = got.shape
    vmem = pl.BlockSpec(memory_space=pltpu.VMEM)
    return pl.pallas_call(
        lambda *refs: image_kernel(piece, *refs),
        in_specs=[vmem],
        out_specs=[vmem] * 3,
        out_shape=(
            jax.ShapeDtypeStruct((piece, width), jnp.float32),
            jax.ShapeDtypeStruct((count, piece, width), jnp.float32),
            jax.ShapeDtypeStruct((width, width), jnp.float32),
        ),
        cost_estimate=pl.CostEstimate(
            flops=10_000_000, bytes_accessed=2_000_000, transcendentals=0
        ),
        compiler_params=pltpu.CompilerParams(vmem_limit_bytes=6 * MIB),
        name="image_piece",
    )(got)


def rows_kernel(rows_ref, inverse_ref, turned_ref):
    rows = exact_dot(left_terms(rows_ref[...]), right_terms(inverse_ref[...]), NT)
    turned_ref[...] = (rows + unit_rows(lax.axis_index("row"), rows.shape)).T


def kernel_kernel(piece, inverse_ref, top_ref, turned_ref, parts_ref, *outs):
    cols_out, rows_left, state_ref = outs
    width = inverse_ref.shape[0]
    identity = eye(width)
    ratio = -product(inverse_ref[...], top_ref[...], NT)
    state_ref[:width, :] = ratio
    state_ref[width:, :] = identity

    def go_on(state):
        return jnp.logical_and(state[0] < 40, state[1] > 1e-10)

    def double(state):
        power = state_ref[:width, :]
        both = product(state_ref[...], power)
        state_ref[:width, :] = both[:width]
        state_ref[width:, :] = state_ref[width:, :] + both[width:]
        return state[0] + 1, jnp.max(jnp.abs(both[:width]))

    lax.while_loop(go_on, double, (0, jnp.max(jnp.abs(ratio))))
    total = state_ref[width:, :]
    kernel = total + product(total, identity - product(identity - ratio, total))
    kernel_terms = right_terms(kernel)
    cols = exact_dot(
        left_terms(pieces_of(parts_ref, piece)), right_terms(inverse_ref[...]), NT
    )
    cols = cols + unit_rows(lax.axis_index("col"), cols.shape)
    cols_out[...] = both_terms(exact_dot(left_terms(cols), kernel_terms, NT))
    rows_left[...] = both_terms(exact_dot(left_terms(turned_ref[...].T), kernel_terms, NT))


def side_call(kernel, operands, shapes, scratch, name):
    vmem = pl.BlockSpec(memory_space=pltpu.VMEM)
    return pl.pallas_call(
        kernel,
        in_specs=[vmem] * len(operands),
        out_specs=[vmem] * len(shapes),
        out_shape=shapes,
        scratch_shapes=scratch,
        cost_estimate=pl.CostEstimate(
            flops=300_000_000, bytes_accessed=10_000_000, transcendentals=0
        ),
        compiler_params=pltpu.CompilerParams(vmem_limit_bytes=14 * MIB),
        name=name,
    )(*operands)


def update_kernel(piece, *refs):
    parts_ref, image_ref, cols_ref, rows_left, mob_ref = refs[:5]
    out_ref, lhs, rhs, held, sems = refs[5:]
    count = sems.shape[0]
    tile = held.shape[0] // count
    middle = lhs.shape[1] // 2
    lhs[:, :middle] = left_terms(image_ref[...])
    lhs[:, middle:] = to_left(rows_left[...])
    small = right_terms(unpack(parts_ref, piece))
    change = exact_dot(to_left(cols_ref[...]), small, NT)
    rhs[:middle, :] = to_right(cols_ref[...]).T
    rhs[middle:, :] = right_terms(pieces_of(parts_ref, piece) - change).T
    stores = []
    for k in range(count):
        rows = pl.ds(k * tile, tile)
        held[rows, :] = mob_ref[rows, :] - exact_dot(lhs[rows, :], rhs[...], NN)
        stores.append(pltpu.make_async_copy(held.at[rows], out_ref.at[rows], sems.at[k]))
        stores[k].start()
    for k in range(count):
        stores[k].wait()


def update(operands, mobility, piece):
    n_rows, n_cols = mobility.shape
    terms = 3 * operands[-1].shape[1]
    vmem = pl.BlockSpec(memory_space=pltpu.VMEM)
    hbm = pl.BlockSpec(memory_space=pltpu.HBM)
    return pl.pallas_call(
        lambda *refs: update_kernel(piece, *refs),
        in_specs=[vmem] * (len(operands) + 1),
        out_specs=hbm,
        out_shape=pltpu.HBM(mobility.shape, jnp.float32),
        scratch_shapes=[
            pltpu.VMEM((n_rows, terms), jnp.bfloat16),
            pltpu.VMEM((terms, n_cols), jnp.bfloat16),
            pltpu.VMEM(mobility.shape, jnp.float32),
            pltpu.SemaphoreType.DMA((4,)),
        ],
        cost_estimate=pl.CostEstimate(
            flops=2 * n_rows * n_cols * terms, bytes_accessed=9_000_000, transcendentals=0
        ),
        compiler_params=pltpu.CompilerParams(vmem_limit_bytes=20 * MIB),
        name="update",
    )(*operands, mobility)


def on_device(panel, mobility):
    piece, width = panel.shape
    n_row, n_col = lax.axis_size("row"), lax.axis_size("col")
    block_rows, block_cols = mobility.shape
    share = width // n_col
    transposing = [(i * n_col + j, j * n_col + i) for i in range(n_row) for j in range(n_col)]
    swap = [(i, i ^ 1) for i in range(n_row)]

    turned_panel = lax.ppermute(panel, BOTH, transposing)
    panel_rows = lax.all_to_all(copies(panel, n_col), "col", 0, 0).reshape(block_rows, width)
    keep, give, top_part = packed_parts(
        gram_kernel, (panel_rows,), [(share, width)], "gram_parts"
    )
    keep, turned_panel = lax.optimization_barrier((keep, turned_panel))
    packed = keep + lax.ppermute(give, "row", swap)
    even = lax.axis_index("row") % 2 == 0
    tail = jnp.where(even, top_part, packed[-STEP:])
    sent = jnp.concatenate([turned_panel, packed[:-STEP], tail], 0)
    panel_parts = lax.all_gather(sent, "row", axis=0)

    panel_factor, inverse, sent = factor_and_product(panel_parts, mobility, piece, share)
    got = lax.all_to_all(sent, "col", 0, 0)
    wide = jax.ShapeDtypeStruct((block_rows, 2 * width), jnp.bfloat16)
    tall = jax.ShapeDtypeStruct((width, block_rows), jnp.float32)
    (turned_rows,) = side_call(rows_kernel, (panel_rows, inverse), [tall], [], "basis_rows")
    got, turned_rows = lax.optimization_barrier((got, turned_rows))
    image, image_copies, top_rows = image_piece(got, piece)
    turned_image = lax.ppermute(image, BOTH, transposing)
    image_rows = lax.all_to_all(image_copies, "col", 0, 0).reshape(block_rows, width)
    cols_right, rows_left = side_call(
        lambda *refs: kernel_kernel(piece, *refs),
        (inverse, top_rows, turned_rows, panel_parts),
        [wide, wide],
        [pltpu.VMEM((2 * width, width), jnp.float32)],
        "kernel",
    )
    image_rows, rows_left = lax.optimization_barrier((image_rows, rows_left))
    keep, give = packed_parts(inner_kernel, (turned_rows, image_rows), [], "inner_parts")
    came = lax.ppermute(give, "row", swap)
    image_parts = lax.all_gather(join(turned_image, keep, came, mobility), "row", axis=0)
    operands = (image_parts, image_rows, cols_right, rows_left)
    updated = update(operands, mobility, piece)
    return (updated, panel_factor)


def solution(mesh):
    in_specs = (P(("row", "col"), None), P("row", "col"))
    out_specs = (P("row", "col"), P())
    return jax.shard_map(
        on_device, mesh=mesh, in_specs=in_specs, out_specs=out_specs, check_vma=False
    )
```
